256 devices in a mesh: comp: 8 (over z_lo, core), geo: 32 (over y, z_hi, x).
Axes of the slice: x: 4, y: 4, z: 8 (z_hi: 2, z_lo: 4; z = z_hi * 4 + z_lo), core: 2. Of those that a mesh axis runs over, the one named last changes fastest.
Arguments:
- spectrum: float32 [432, 1024, 256], P(None, ('comp', 'geo')), may hold values from 0.05 to 2
- wind_speed: float32 [1024, 256], P(('comp', 'geo')), may hold values from 0.2 to 2
- growth: float32 [432], replicated, may hold values from 0 to 0.4
- dissip: float32 [432], replicated, may hold values from 0.1 to 1
- ice_rate: float32 [432], replicated, may hold values from 0.2 to 2
- coupling: float32 [432, 432], replicated, may hold values from -0.3125 to 0.3125
- cfl_lon: float32 [432], replicated, may hold values from -0.45 to 0.45
- cfl_lat: float32 [432], replicated, may hold values from -0.45 to 0.45
- sea_mask: int32 [1024, 256], P(('comp', 'geo')), may hold values 0 or 1
- ice_mask: int32 [1024, 256], P(('comp', 'geo')), may hold values 0 or 1
- fold_partner: int32 [1024], replicated, may hold values from 0 to 1023, as said below
Outputs:
- updated: float32 [432, 1024, 256], P(None, ('comp', 'geo'))
The draws below stay inside these ranges and needn't reach their ends.
Inputs may be any that keep to these rules, and one draw needn't show every extreme that they name: fold_partner[i] = (s - i) modulo 1024 for one s of each draw, so a partner's partner is the column itself.
All inputs are finite; a program needn't handle non-finite values. No bound on the sum of `sea_mask` or of `ice_mask` on one device may be relied on, other than what follows from the above.
Results may differ from the reference program's by a relative error of at most 0.000057.
Values sent between devices are 32-bit elements; how exact they have to be, the bound alone decides.
No kernel may reach another device: no remote copies, remote signals or barrier semaphores. Data moves between devices by JAX's collectives and lax.ppermute only.
A program may use at most 64 MiB of HBM per device.

```python
import math
import jax
import jax.numpy as jnp
from jax import lax

COMP = 432
LAT = 256
NLON = 1024


def draw_fold_partner(key, part):
    offset = jax.random.randint(key, (), 0, NLON).astype(jnp.int32)
    return ((offset - jnp.arange(NLON, dtype=jnp.int32)) % NLON).astype(jnp.int32)


def set_ends(array, key, low, largest):
    extent = array.shape
    index_at = [jax.random.randint(jax.random.fold_in(key, axis), (), 0, extent[axis]) for axis in range(len(extent))]
    array = array.at[tuple(index_at)].set(low)
    longest = extent.index(max(extent))
    index_at[longest] = (index_at[longest] + 1) % extent[longest]
    return array.at[tuple(index_at)].set(largest)


def levels(own_key, dims, pieces, least, top_value):
    level, own = 1.0, jax.random.fold_in(own_key, 6)
    for axis_at, parts in pieces:
        steps = jnp.exp(jax.random.uniform(jax.random.fold_in(own, axis_at), (parts,), jnp.float32, least / len(pieces), top_value / len(pieces)))
        level = level * jnp.repeat(steps, dims[axis_at] // parts).reshape([-1 if axis == axis_at else 1 for axis in range(len(dims))])
    return level


def scatter_about(rng, extent, deviation, bound, held_as=jnp.bfloat16):
    return jnp.clip(deviation * jax.random.normal(rng, extent, jnp.float32), -bound, bound).astype(held_as)


def setup_inputs(seed: int = 0) -> dict:
    streams_of = jax.random.split(jax.random.key(seed), 12)
    spectrum = jnp.clip(jnp.exp(math.log(2.0) - 3.6888794 * jax.random.uniform(streams_of[0], (COMP, NLON, LAT), jnp.float32) ** levels(streams_of[0], (COMP, NLON, LAT), ((1, 256),), -0.2, 0.2)), 0.05, 2.0)
    wind_speed = jnp.clip(jnp.exp(math.log(2.0) - 2.3025851 * jax.random.uniform(streams_of[1], (NLON, LAT), jnp.float32) ** levels(streams_of[1], (NLON, LAT), ((0, 256),), -0.2, 0.2)), 0.2, 2.0)
    growth = jnp.clip(jax.random.uniform(streams_of[2], (COMP,), jnp.float32, 0.0, 0.4), 0.0, 0.4)
    dissip = jnp.clip(jnp.exp(jax.random.uniform(streams_of[3], (COMP,), jnp.float32, math.log(0.1), math.log(1.0))), 0.1, 1.0)
    ice_rate = jnp.clip(jnp.exp(jax.random.uniform(streams_of[4], (COMP,), jnp.float32, math.log(0.2), math.log(2.0))), 0.2, 2.0)
    coupling = scatter_about(streams_of[5], (COMP, COMP), COMP ** -0.5, 0.3125, jnp.float32)
    cfl_lon = jnp.clip(jax.random.uniform(streams_of[6], (COMP,), jnp.float32, -0.45, 0.45), -0.45, 0.45)
    cfl_lat = jnp.clip(jax.random.uniform(streams_of[7], (COMP,), jnp.float32, -0.45, 0.45), -0.45, 0.45)
    sea_mask = set_ends((jax.random.randint(streams_of[8], (NLON, LAT), 0, 5) < 4).astype(jnp.int32), jax.random.fold_in(streams_of[8], 1), 0, 1)
    ice_mask = set_ends((jax.random.randint(streams_of[9], (NLON, LAT), 0, 4) < 1).astype(jnp.int32), jax.random.fold_in(streams_of[9], 1), 0, 1)
    fold_partner = draw_fold_partner(jax.random.fold_in(streams_of[11], 71), 0)
    return {"spectrum": spectrum, "wind_speed": wind_speed, "growth": growth, "dissip": dissip, "ice_rate": ice_rate, "coupling": coupling, "cfl_lon": cfl_lon, "cfl_lat": cfl_lat, "sea_mask": sea_mask, "ice_mask": ice_mask, "fold_partner": fold_partner}


def reference(spectrum, wind_speed, growth, dissip, ice_rate, coupling, cfl_lon, cfl_lat, sea_mask, ice_mask, fold_partner):
    sea_field = sea_mask.astype(jnp.float32)
    ice_field = ice_mask.astype(jnp.float32)
    mean_energy = jnp.sum(spectrum, axis=0) / COMP
    net_rate = growth[:, None, None] * wind_speed[None] - dissip[:, None, None] * (mean_energy / (1.0 + mean_energy))[None] - ice_rate[:, None, None] * ice_field[None]
    coupled = jnp.dot(coupling, spectrum.reshape(COMP, -1), precision=lax.Precision.HIGHEST).reshape(spectrum.shape)
    source = sea_field[None] * (spectrum * jnp.exp(net_rate) + 0.5 * coupled)
    east_vals = jnp.roll(source, -1, axis=1)
    sea_east = jnp.roll(sea_field, -1, axis=0)
    lon_speed = cfl_lon[:, None, None]
    lon_flux = (sea_field * sea_east)[None] * (jnp.maximum(lon_speed, 0.0) * source + jnp.minimum(lon_speed, 0.0) * east_vals)
    lon_change = lon_flux - jnp.roll(lon_flux, 1, axis=1)
    north_vals = source[:, fold_partner, -1]
    north_sea = sea_field[fold_partner, -1]
    upper_vals = jnp.concatenate([source[:, :, 1:], north_vals[:, :, None]], axis=2)
    upper_sea = jnp.concatenate([sea_field[:, 1:], north_sea[:, None]], axis=1)
    lat_speed = cfl_lat[:, None, None]
    lat_flux = (sea_field * upper_sea)[None] * (jnp.maximum(lat_speed, 0.0) * source + jnp.minimum(lat_speed, 0.0) * upper_vals)
    south_flux = jnp.concatenate([jnp.zeros_like(lat_flux[:, :, :1]), lat_flux[:, :, :-1]], axis=2)
    return source - lon_change - (lat_flux - south_flux)
```

```python
import functools

import jax
import jax.numpy as jnp
from jax import lax
from jax.experimental import pallas as pl
from jax.experimental.pallas import tpu as pltpu
from jax.sharding import PartitionSpec as P

AXES = ("comp", "geo")
CAP = 256
VMEM = pl.BlockSpec(memory_space=pltpu.VMEM)
SMEM = pl.BlockSpec(memory_space=pltpu.SMEM)
ANY = pl.BlockSpec(memory_space=pl.ANY)
LIMIT = 56 * 1024 * 1024


def columns_of(rows_refs, stage, width):
    stage[...] = jnp.zeros(stage.shape, jnp.float32)
    for row, ref in enumerate(rows_refs):
        stage[row : row + 1, :width] = ref[...]
    return stage[...].T


def source_kernel(
    cap, par_ref, cfl_smem, x_hbm, wind, growth, dissip, ice_rate, coupling, sea_ref, ice_ref,
    src, odd_msg, even_msg, top, xs, stage, cols, top_stage, sems,
):
    comps, lon_dev, lats = x_hbm.shape
    order = (0, lon_dev - 1, *range(1, lon_dev - 1))
    copies = [pltpu.make_async_copy(x_hbm.at[:, j, :], xs.at[j], sems.at[j]) for j in range(lon_dev)]
    for j in order:
        copies[j].start()
    cols[...] = columns_of((growth, dissip, ice_rate), stage, comps)
    grow_c, diss_c, rate_c = (cols[:comps, i : i + 1] for i in range(3))
    coup = coupling[...]
    coup_hi = coup.astype(jnp.bfloat16)
    coup_lo = (coup - coup_hi.astype(jnp.float32)).astype(jnp.bfloat16)
    dot = functools.partial(jnp.dot, preferred_element_type=jnp.float32)
    top_stage[comps:, :] = jnp.zeros((top_stage.shape[0] - comps, 128), jnp.float32)
    lane = lax.broadcasted_iota(jnp.int32, (comps, 128), 1)
    lane8 = lax.broadcasted_iota(jnp.int32, (8, 128), 1)
    tops = jnp.zeros((comps, 128), jnp.float32)
    sea_tops = jnp.zeros((8, 128), jnp.float32)
    for j in order:
        copies[j].wait()
        x = xs[j]
        mean = jnp.sum(x, axis=0, keepdims=True) / comps
        sat = mean / (1.0 + mean)
        sea = sea_ref[j : j + 1, :].astype(jnp.float32)
        ice = ice_ref[j : j + 1, :].astype(jnp.float32)
        x_hi = x.astype(jnp.bfloat16)
        x_lo = (x - x_hi.astype(jnp.float32)).astype(jnp.bfloat16)
        coupled = dot(coup_hi, x_hi) + dot(coup_hi, x_lo) + dot(coup_lo, x_hi)
        net = grow_c * wind[j : j + 1, :] - diss_c * sat - rate_c * ice
        value = sea * (x * jnp.exp(net) + 0.5 * coupled)
        src[j] = value
        last = value[:, lats - 128 :]
        tops = jnp.where(lane == j, pltpu.roll(last, j + 1, 1), tops)
        sea_last = jnp.broadcast_to(sea[:, lats - 128 :], (8, 128))
        sea_tops = jnp.where(lane8 == j, pltpu.roll(sea_last, j + 1, 1), sea_tops)
    top_stage[:comps, :] = tops
    top_stage[comps : comps + 8, :] = sea_tops
    turned = top_stage[...].T[:lon_dev]
    for slot in range(top.shape[0]):
        top[slot] = turned
    odd = par_ref[0]
    west, east = 0, lon_dev - 1
    odd_col = jnp.where(odd == 1, east, west)
    even_col = jnp.where(odd == 1, west, east)
    odd_sign = jnp.where(odd == 1, 1.0, -1.0)

    def pack(k, at):
        at_odd, at_even = at
        speed = cfl_smem[k] * odd_sign
        odd_msg[pl.ds(at_odd, 1), :] = src[odd_col, pl.ds(k, 1), :]
        even_msg[pl.ds(at_even, 1), :] = src[even_col, pl.ds(k, 1), :]
        return at_odd + (speed > 0.0).astype(jnp.int32), at_even + (speed < 0.0).astype(jnp.int32)

    lax.fori_loop(0, comps, pack, (jnp.int32(0), jnp.int32(0)), unroll=8)
    odd_msg[cap : cap + 8, :] = jnp.broadcast_to(
        jnp.where(odd == 1, sea_ref[east : east + 1, :], sea_ref[west : west + 1, :]), (8, lats)
    ).astype(jnp.float32)
    even_msg[cap : cap + 8, :] = jnp.broadcast_to(
        jnp.where(odd == 1, sea_ref[west : west + 1, :], sea_ref[east : east + 1, :]), (8, lats)
    ).astype(jnp.float32)


def reroute_kernel(n_comp, n_geo, where, fold, got, out, sems):
    me_comp, me_geo = where[1], where[2]
    lon_dev = got.shape[1]
    copies = []
    for i in range(2):
        q = lax.rem(fold[0] // lon_dev - i + n_comp * n_geo, n_comp * n_geo)
        q_comp, q_geo = q // n_geo, lax.rem(q, n_geo)
        to_geo = lax.rem(q_geo - me_geo + n_geo, n_geo)
        borrow = (to_geo > q_geo).astype(jnp.int32)
        of_comp = lax.rem(q_comp - me_comp - borrow + 2 * n_comp, n_comp)
        copies.append(pltpu.make_async_copy(got.at[of_comp], out.at[to_geo], sems.at[i]))
    for copy in copies:
        copy.start()
    for copy in copies:
        copy.wait()


def transport_kernel(
    cap, n_comp, n_geo, where, fold, cfl_smem, src, odd_msg, even_msg, seam, cfl_lon, cfl_lat, sea_ref,
    out, outs, halo, stage, cols, seam_cols, sems,
):
    lon_dev, comps, lats = src.shape
    odd, me_geo = where[0], where[2]
    size = cap + 8

    def unpack(k, at):
        at_west, at_east = at
        speed = cfl_smem[k]
        row_odd = jnp.where(odd == 1, at_east, at_west)
        row_even = jnp.where(odd == 1, at_west, at_east)
        from_odd = (speed > 0.0) != (odd == 1)

        @pl.when(from_odd)
        def _():
            halo[pl.ds(k, 1), :] = odd_msg[pl.ds(row_odd, 1), :]

        @pl.when(jnp.logical_not(from_odd))
        def _():
            halo[pl.ds(k, 1), :] = even_msg[pl.ds(row_even, 1), :]

        return at_west + (speed > 0.0).astype(jnp.int32), at_east + (speed < 0.0).astype(jnp.int32)

    lax.fori_loop(0, comps, unpack, (jnp.int32(0), jnp.int32(0)), unroll=8)
    sea_odd, sea_even = odd_msg[cap : cap + 1, :], even_msg[cap : cap + 1, :]
    sea_west = jnp.where(odd == 1, sea_even, sea_odd)
    sea_east = jnp.where(odd == 1, sea_odd, sea_even)
    cols[...] = columns_of((cfl_lon, cfl_lat), stage, comps)
    q = fold[0] // lon_dev
    shift = lax.rem(fold[0], lon_dev)
    slot_0 = lax.rem(lax.rem(q, n_geo) - me_geo + n_geo, n_geo)
    slot_1 = lax.rem(slot_0 - 1 + n_geo, n_geo)
    stage[...] = jnp.zeros(stage.shape, jnp.float32)
    for j in range(lon_dev):
        place = shift - j
        slot = jnp.where(place >= 0, slot_0, slot_1)
        row = jnp.where(place >= 0, place, place + lon_dev)
        stage[j : j + 1, :] = seam[slot, pl.ds(row, 1), :]
    seam_cols[...] = stage[...].T
    sea = [sea_ref[j : j + 1, :].astype(jnp.float32) for j in range(lon_dev)]
    open_lon = [
        (sea_west if j == 0 else sea[j - 1]) * (sea_east if j == lon_dev else sea[j]) for j in range(lon_dev + 1)
    ]
    lane_row = lax.broadcasted_iota(jnp.int32, (1, lats), 1)
    open_lat = []
    for j in range(lon_dev):
        north = stage[j : j + 1, comps : comps + 1]
        upper = jnp.where(lane_row == lats - 1, north, pltpu.roll(jnp.broadcast_to(sea[j], (8, lats)), lats - 1, 1)[:1])
        open_lat.append(sea[j] * upper)
    step = 8
    lane = lax.broadcasted_iota(jnp.int32, (step, lats), 1)
    wide = [jnp.broadcast_to(v, (step, lats)) for v in open_lon]
    tall = [jnp.broadcast_to(v, (step, lats)) for v in open_lat]

    def rows(i, carry):
        at = pl.ds(pl.multiple_of(i * step, step), step)
        params = cols[at, :]
        lon_pos = jnp.maximum(params[:, 0:1], 0.0)
        lon_neg = jnp.minimum(params[:, 0:1], 0.0)
        lat_pos = jnp.maximum(params[:, 1:2], 0.0)
        lat_neg = jnp.minimum(params[:, 1:2], 0.0)
        norths = seam_cols[at, :]
        edge = halo[at, :]
        vals = [src[j, at, :] for j in range(lon_dev)]
        flux = []
        for j in range(lon_dev + 1):
            lower = jnp.where(lon_pos > 0.0, lon_pos * edge, 0.0) if j == 0 else lon_pos * vals[j - 1]
            upper = jnp.where(lon_neg < 0.0, lon_neg * edge, 0.0) if j == lon_dev else lon_neg * vals[j]
            flux.append(wide[j] * (lower + upper))
        for j in range(lon_dev):
            up = jnp.where(lane == lats - 1, norths[:, j : j + 1], pltpu.roll(vals[j], lats - 1, 1))
            lat = tall[j] * (lat_pos * vals[j] + lat_neg * up)
            south = jnp.where(lane == 0, 0.0, pltpu.roll(lat, 1, 1))
            outs[j, at, :] = vals[j] - (flux[j + 1] - flux[j]) - (lat - south)
        return carry

    lax.fori_loop(0, comps // step, rows, 0, unroll=2)
    copies = [pltpu.make_async_copy(outs.at[j], out.at[:, j, :], sems.at[j]) for j in range(lon_dev)]
    for copy in copies:
        copy.start()
    for copy in copies:
        copy.wait()


def exchange(cap, n_comp, n_geo, args):
    (spectrum, wind_speed, growth, dissip, ice_rate, coupling, cfl_lon, cfl_lat, sea_mask, ice_mask, fold_partner) = args
    comps, lon_dev, lats = spectrum.shape
    count = n_comp * n_geo
    wide = -(-(comps + 8) // 128) * 128
    me_comp, me_geo = lax.axis_index("comp"), lax.axis_index("geo")
    where = jnp.stack([lax.rem(me_geo, 2), me_comp, me_geo]).astype(jnp.int32)
    row = lambda v: v.reshape(1, comps)
    f32 = jnp.float32
    size = cap + 8
    params = pltpu.CompilerParams(vmem_limit_bytes=LIMIT)
    src, odd_msg, even_msg, top = pl.pallas_call(
        functools.partial(source_kernel, cap),
        out_shape=(
            jax.ShapeDtypeStruct((lon_dev, comps, lats), f32),
            jax.ShapeDtypeStruct((size, lats), f32),
            jax.ShapeDtypeStruct((size, lats), f32),
            jax.ShapeDtypeStruct((n_comp, lon_dev, wide), f32),
        ),
        in_specs=[SMEM, SMEM, ANY] + [VMEM] * 7,
        out_specs=(VMEM,) * 4,
        scratch_shapes=[
            pltpu.VMEM((lon_dev, comps, lats), f32),
            pltpu.VMEM((128, wide), f32),
            pltpu.VMEM((wide, 128), f32),
            pltpu.VMEM((wide, 128), f32),
            pltpu.SemaphoreType.DMA((lon_dev,)),
        ],
        compiler_params=params,
        name="source",
    )(where, cfl_lon, spectrum, wind_speed, row(growth), row(dissip), row(ice_rate), coupling, sea_mask, ice_mask)
    odd_pairs = [(d, (d + 1) % count if d % 2 else (d - 1) % count) for d in range(count)]
    even_pairs = [(d, d - 1 if d % 2 else d + 1) for d in range(count)]
    odd_got = lax.ppermute(odd_msg, AXES, odd_pairs)
    even_got = lax.ppermute(even_msg, AXES, even_pairs)
    by_comp = lax.all_to_all(top, "comp", 0, 0, tiled=True)
    slots = pl.pallas_call(
        functools.partial(reroute_kernel, n_comp, n_geo),
        out_shape=jax.ShapeDtypeStruct((n_geo, lon_dev, wide), f32),
        in_specs=[SMEM, SMEM, ANY],
        out_specs=ANY,
        scratch_shapes=[pltpu.SemaphoreType.DMA((2,))],
        name="reroute",
    )(where, fold_partner, by_comp)
    seam = lax.all_to_all(slots, "geo", 0, 0, tiled=True)
    return pl.pallas_call(
        functools.partial(transport_kernel, cap, n_comp, n_geo),
        out_shape=jax.ShapeDtypeStruct((comps, lon_dev, lats), f32),
        in_specs=[SMEM, SMEM, SMEM] + [VMEM] * 7,
        out_specs=ANY,
        scratch_shapes=[
            pltpu.VMEM((lon_dev, comps, lats), f32),
            pltpu.VMEM((comps, lats), f32),
            pltpu.VMEM((128, wide), f32),
            pltpu.VMEM((wide, 128), f32),
            pltpu.VMEM((wide, 128), f32),
            pltpu.SemaphoreType.DMA((lon_dev,)),
        ],
        compiler_params=params,
        name="transport",
    )(where, fold_partner, cfl_lon, src, odd_got, even_got, seam, row(cfl_lon), row(cfl_lat), sea_mask)


def solution(mesh):
    n_comp, n_geo = mesh.shape["comp"], mesh.shape["geo"]
    lon = P(AXES, None)
    placed = (P(None, AXES, None), lon, P(), P(), P(), P(), P(), P(), lon, lon, P())

    def on_device(*args):
        cfl_lon = args[6]
        most = jnp.maximum(jnp.sum((cfl_lon > 0.0).astype(jnp.int32)), jnp.sum((cfl_lon < 0.0).astype(jnp.int32)))
        comps = args[0].shape[0]
        return lax.cond(
            most > CAP,
            lambda *a: exchange(comps, n_comp, n_geo, a),
            lambda *a: exchange(CAP, n_comp, n_geo, a),
            *args,
        )

    return jax.shard_map(
        on_device, mesh=mesh, in_specs=placed, out_specs=P(None, AXES, None), check_vma=False
    )
```

```python
import functools

import jax
import jax.numpy as jnp
from jax import lax
from jax.experimental import pallas as pl
from jax.experimental.pallas import tpu as pltpu
from jax.sharding import PartitionSpec as P

AXES = ("comp", "geo")
CAP = 256
VMEM = pl.BlockSpec(memory_space=pltpu.VMEM)
SMEM = pl.BlockSpec(memory_space=pltpu.SMEM)
ANY = pl.BlockSpec(memory_space=pl.ANY)
LIMIT = 56 * 1024 * 1024


CHUNKS = 3


def columns_of(rows, stage):
    stage[...] = jnp.zeros(stage.shape, jnp.float32)
    for i, value in enumerate(rows):
        stage[i : i + 1, : value.shape[1]] = value
    return stage[...].T


def halves(value):
    high = value.astype(jnp.bfloat16)
    return high, (value - high.astype(jnp.float32)).astype(jnp.bfloat16)


def dot(a, b, contract=(1, 0)):
    return lax.dot_general(a, b, (((contract[0],), (contract[1],)), ((), ())), preferred_element_type=jnp.float32)


def source_kernel(
    cap, where, x_hbm, wind, growth, dissip, ice_rate, cfl_lon, cfl_lat, coupling, sea_ref, ice_ref,
    src, odd_msg, even_msg, top, places, xs, ss, stage, cols, top_stage, in_sems, out_sems,
):
    comps, lon_dev, lats = x_hbm.shape
    west, east = 0, lon_dev - 1
    order = (west, east, *range(1, lon_dev - 1))
    copies = [pltpu.make_async_copy(x_hbm.at[:, j, :], xs.at[j], in_sems.at[j]) for j in range(lon_dev)]
    for j in order:
        copies[j].start()
    odd = where[0]
    cols[...] = columns_of((growth[...], dissip[...], ice_rate[...]), stage)
    grow_c, diss_c, rate_c = (cols[:comps, i : i + 1] for i in range(3))
    coup_hi, coup_lo = halves(coupling[...])
    speed = cfl_lon[...] * jnp.where(odd == 1, 1.0, -1.0)
    pick = lax.broadcasted_iota(jnp.int32, (16, comps), 0)
    flags = jnp.where(pick == 0, speed, jnp.where(pick == 1, -speed, -cfl_lat[...])) > 0.0
    upto = lax.broadcasted_iota(jnp.int32, (comps, comps), 0) <= lax.broadcasted_iota(jnp.int32, (comps, comps), 1)
    ones = jnp.where(upto, 1.0, 0.0).astype(jnp.bfloat16)
    rank = dot(jnp.where(flags, 1.0, 0.0).astype(jnp.bfloat16), ones)
    place = jnp.where(flags, rank - 1.0, -1.0)
    places[...] = place[:8]

    def packing(i, rows):
        at = lax.broadcasted_iota(jnp.int32, (rows, comps), 0).astype(jnp.float32)
        return jnp.where(at == place[i : i + 1, :], 1.0, 0.0).astype(jnp.bfloat16)

    top_stage[comps:, :] = jnp.zeros((top_stage.shape[0] - comps, 128), jnp.float32)
    lane = lax.broadcasted_iota(jnp.int32, (comps, 128), 1)
    tops = jnp.zeros((comps, 128), jnp.float32)
    done = []
    for j in order:
        copies[j].wait()
        x = xs[j]
        mean = jnp.sum(x, axis=0, keepdims=True) / comps
        sat = mean / (1.0 + mean)
        sea = sea_ref[j : j + 1, :].astype(jnp.float32)
        ice = ice_ref[j : j + 1, :].astype(jnp.float32)
        x_hi, x_lo = halves(x)
        coupled = dot(coup_hi, x_hi) + dot(coup_hi, x_lo) + dot(coup_lo, x_hi)
        net = grow_c * wind[j : j + 1, :] - diss_c * sat - rate_c * ice
        value = sea * (x * jnp.exp(net) + 0.5 * coupled)
        ss[j] = value
        out = pltpu.make_async_copy(ss.at[j], src.at[j], out_sems.at[j])
        out.start()
        done.append(out)
        tops = jnp.where(lane == j, pltpu.roll(value[:, lats - 128 :], j + 1, 1), tops)
    top_stage[:comps, :] = tops
    lat_w = top.shape[2]
    top_hi, top_lo = halves(top_stage[...].T[:, :comps])
    top_pack = packing(2, lat_w)
    packed = (dot(top_hi, top_pack, (1, 1)) + dot(top_lo, top_pack, (1, 1)))[:lon_dev]
    sea_top = sea_ref[:, lats - 1 : lats].astype(jnp.float32)
    packed = jnp.where(lax.broadcasted_iota(jnp.int32, (lon_dev, lat_w), 1) == lat_w - 1, sea_top, packed)
    for slot in range(top.shape[0]):
        top[slot] = packed
    sea_w = sea_ref[west : west + 1, :].astype(jnp.float32)
    sea_e = sea_ref[east : east + 1, :].astype(jnp.float32)
    for i, (msg, col, sea) in enumerate((
        (odd_msg, jnp.where(odd == 1, east, west), jnp.where(odd == 1, sea_e, sea_w)),
        (even_msg, jnp.where(odd == 1, west, east), jnp.where(odd == 1, sea_w, sea_e)),
    )):
        hi, lo = halves(ss[col])
        pack = packing(i, cap)
        msg[:cap, :] = dot(pack, hi) + dot(pack, lo)
        msg[cap : cap + 8, :] = jnp.broadcast_to(sea, (8, lats))
    for out in done:
        out.wait()


def reroute_kernel(n_comp, n_geo, where, fold, got, out, sems):
    me_comp, me_geo = where[1], where[2]
    lon_dev = got.shape[1]
    copies = []
    for i in range(2):
        q = lax.rem(fold[0] // lon_dev - i + n_comp * n_geo, n_comp * n_geo)
        q_comp, q_geo = q // n_geo, lax.rem(q, n_geo)
        to_geo = lax.rem(q_geo - me_geo + n_geo, n_geo)
        borrow = (to_geo > q_geo).astype(jnp.int32)
        of_comp = lax.rem(q_comp - me_comp - borrow + 2 * n_comp, n_comp)
        copies.append(pltpu.make_async_copy(got.at[of_comp], out.at[to_geo], sems.at[i]))
    for copy in copies:
        copy.start()
    for copy in copies:
        copy.wait()


def transport_kernel(
    cap, n_geo, where, fold, src_hbm, odd_hbm, even_hbm, seam_hbm, places, cfl_lon, cfl_lat, sea_ref,
    out, src, outs, msgs, seam, halo, norths, stage, cols, top_rows, in_sems, out_sems,
):
    lon_dev, comps, lats = src.shape
    odd, me_geo = where[0], where[2]
    q = fold[0] // lon_dev
    shift = lax.rem(fold[0], lon_dev)
    slot_0 = lax.rem(lax.rem(q, n_geo) - me_geo + n_geo, n_geo)
    slot_1 = lax.rem(slot_0 - 1 + n_geo, n_geo)
    copies = [
        pltpu.make_async_copy(seam_hbm.at[slot_0], seam.at[0], in_sems.at[0]),
        pltpu.make_async_copy(seam_hbm.at[slot_1], seam.at[1], in_sems.at[1]),
        pltpu.make_async_copy(odd_hbm, msgs.at[0], in_sems.at[2]),
        pltpu.make_async_copy(even_hbm, msgs.at[1], in_sems.at[3]),
        pltpu.make_async_copy(src_hbm, src, in_sems.at[4]),
    ]
    for copy in copies:
        copy.start()
    cols[...] = columns_of((cfl_lon[...], cfl_lat[...], places[1:2, :], places[0:1, :], places[2:3, :]), stage)
    copies[0].wait()
    copies[1].wait()
    lat_w = seam.shape[2]
    top_rows[...] = jnp.zeros(top_rows.shape, jnp.float32)
    for j in range(lon_dev):
        place = shift - j
        block = jnp.where(place >= 0, 0, 1)
        row = jnp.where(place >= 0, place, place + lon_dev)
        top_rows[j : j + 1, :] = seam[block, pl.ds(row, 1), :]

    def spread(i, width):
        at = lax.broadcasted_iota(jnp.int32, (comps, width), 1).astype(jnp.float32)
        return jnp.where(at == cols[:comps, 2 + i : 3 + i], 1.0, 0.0).astype(jnp.bfloat16)

    top_hi, top_lo = halves(top_rows[...])
    top_spread = spread(2, lat_w)
    norths[...] = dot(top_spread, top_hi, (1, 1)) + dot(top_spread, top_lo, (1, 1))
    copies[2].wait()
    copies[3].wait()
    total = None
    for i in range(2):
        hi, lo = halves(msgs[i, :cap, :])
        part = spread(i, cap)
        part = dot(part, hi) + dot(part, lo)
        total = part if total is None else total + part
    halo[...] = total
    sea_odd, sea_even = msgs[0, cap : cap + 1, :], msgs[1, cap : cap + 1, :]
    sea_west = jnp.where(odd == 1, sea_even, sea_odd)
    sea_east = jnp.where(odd == 1, sea_odd, sea_even)
    sea = [sea_ref[j : j + 1, :].astype(jnp.float32) for j in range(lon_dev)]
    open_lon = [
        (sea_west if j == 0 else sea[j - 1]) * (sea_east if j == lon_dev else sea[j]) for j in range(lon_dev + 1)
    ]
    step = 8
    lane = lax.broadcasted_iota(jnp.int32, (step, lats), 1)
    first, last = lane == 0, lane == lats - 1
    tall = []
    for j in range(lon_dev):
        own = jnp.broadcast_to(sea[j], (step, lats))
        north = jnp.broadcast_to(top_rows[j : j + 1, lat_w - 1 : lat_w], (step, lats))
        tall.append(own * jnp.where(last, north, pltpu.roll(own, lats - 1, 1)))
    wide = [jnp.broadcast_to(v, (step, lats)) for v in open_lon]
    copies[4].wait()

    def rows(i, carry):
        at = pl.ds(pl.multiple_of(i * step, step), step)
        params = cols[at, :]
        lon_pos = jnp.maximum(params[:, 0:1], 0.0)
        lon_neg = jnp.minimum(params[:, 0:1], 0.0)
        lat_pos = jnp.maximum(params[:, 1:2], 0.0)
        lat_neg = jnp.minimum(params[:, 1:2], 0.0)
        tops = norths[at, :]
        edge = halo[at, :]
        vals = [src[j, at, :] for j in range(lon_dev)]
        ends = [edge, *vals, edge]
        flux = [wide[j] * (lon_pos * ends[j] + lon_neg * ends[j + 1]) for j in range(lon_dev + 1)]
        for j in range(lon_dev):
            up = jnp.where(last, tops[:, j : j + 1], pltpu.roll(vals[j], lats - 1, 1))
            lat = tall[j] * (lat_pos * vals[j] + lat_neg * up)
            south = jnp.where(first, 0.0, pltpu.roll(lat, 1, 1))
            outs[j, at, :] = vals[j] - (flux[j + 1] - flux[j]) - (lat - south)
        return carry

    piece = comps // CHUNKS
    done = []
    for c in range(CHUNKS):
        lax.fori_loop(c * piece // step, (c + 1) * piece // step, rows, 0, unroll=2)
        at = pl.ds(c * piece, piece)
        for j in range(lon_dev):
            copy = pltpu.make_async_copy(outs.at[j, at, :], out.at[at, j, :], out_sems.at[c, j])
            copy.start()
            done.append(copy)
    for copy in done:
        copy.wait()


def exchange(cap, lat_cap, n_comp, n_geo, args):
    (spectrum, wind_speed, growth, dissip, ice_rate, coupling, cfl_lon, cfl_lat, sea_mask, ice_mask, fold_partner) = args
    comps, lon_dev, lats = spectrum.shape
    count = n_comp * n_geo
    wide = -(-comps // 128) * 128
    lat_w = -(-(lat_cap + 1) // 128) * 128
    size = cap + 8
    me_comp, me_geo = lax.axis_index("comp"), lax.axis_index("geo")
    where = jnp.stack([lax.rem(me_geo, 2), me_comp, me_geo]).astype(jnp.int32)
    row = lambda v: v.reshape(1, comps)
    f32 = jnp.float32
    params = pltpu.CompilerParams(vmem_limit_bytes=LIMIT)
    src, odd_msg, even_msg, top, places = pl.pallas_call(
        functools.partial(source_kernel, cap),
        out_shape=(
            jax.ShapeDtypeStruct((lon_dev, comps, lats), f32),
            jax.ShapeDtypeStruct((size, lats), f32),
            jax.ShapeDtypeStruct((size, lats), f32),
            jax.ShapeDtypeStruct((n_comp, lon_dev, lat_w), f32),
            jax.ShapeDtypeStruct((8, comps), f32),
        ),
        in_specs=[SMEM, ANY] + [VMEM] * 9,
        out_specs=(ANY, VMEM, VMEM, VMEM, VMEM),
        scratch_shapes=[
            pltpu.VMEM((lon_dev, comps, lats), f32),
            pltpu.VMEM((lon_dev, comps, lats), f32),
            pltpu.VMEM((128, wide), f32),
            pltpu.VMEM((wide, 128), f32),
            pltpu.VMEM((wide, 128), f32),
            pltpu.SemaphoreType.DMA((lon_dev,)),
            pltpu.SemaphoreType.DMA((lon_dev,)),
        ],
        compiler_params=params,
        name="source",
    )(
        where, spectrum, wind_speed, row(growth), row(dissip), row(ice_rate), row(cfl_lon), row(cfl_lat),
        coupling, sea_mask, ice_mask,
    )
    odd_pairs = [(d, (d + 1) % count if d % 2 else (d - 1) % count) for d in range(count)]
    even_pairs = [(d, d - 1 if d % 2 else d + 1) for d in range(count)]
    odd_got = lax.ppermute(odd_msg, AXES, odd_pairs)
    even_got = lax.ppermute(even_msg, AXES, even_pairs)
    by_comp = lax.all_to_all(top, "comp", 0, 0, tiled=True)
    slots = pl.pallas_call(
        functools.partial(reroute_kernel, n_comp, n_geo),
        out_shape=jax.ShapeDtypeStruct((n_geo, lon_dev, lat_w), f32),
        in_specs=[SMEM, SMEM, ANY],
        out_specs=ANY,
        scratch_shapes=[pltpu.SemaphoreType.DMA((2,))],
        name="reroute",
    )(where, fold_partner, by_comp)
    seam = lax.all_to_all(slots, "geo", 0, 0, tiled=True)
    return pl.pallas_call(
        functools.partial(transport_kernel, cap, n_geo),
        out_shape=jax.ShapeDtypeStruct((comps, lon_dev, lats), f32),
        in_specs=[SMEM, SMEM, ANY, ANY, ANY, ANY] + [VMEM] * 4,
        out_specs=ANY,
        scratch_shapes=[
            pltpu.VMEM((lon_dev, comps, lats), f32),
            pltpu.VMEM((lon_dev, comps, lats), f32),
            pltpu.VMEM((2, size, lats), f32),
            pltpu.VMEM((2, lon_dev, lat_w), f32),
            pltpu.VMEM((comps, lats), f32),
            pltpu.VMEM((comps, 128), f32),
            pltpu.VMEM((128, wide), f32),
            pltpu.VMEM((wide, 128), f32),
            pltpu.VMEM((128, lat_w), f32),
            pltpu.SemaphoreType.DMA((5,)),
            pltpu.SemaphoreType.DMA((CHUNKS, lon_dev)),
        ],
        compiler_params=params,
        name="transport",
    )(where, fold_partner, src, odd_got, even_got, seam, places, row(cfl_lon), row(cfl_lat), sea_mask)


def solution(mesh):
    n_comp, n_geo = mesh.shape["comp"], mesh.shape["geo"]
    lon = P(AXES, None)
    placed = (P(None, AXES, None), lon, P(), P(), P(), P(), P(), P(), lon, lon, P())

    def on_device(*args):
        cfl_lon, cfl_lat = args[6], args[7]
        count = lambda flags: jnp.sum(flags.astype(jnp.int32))
        most = jnp.maximum(jnp.maximum(count(cfl_lon > 0.0), count(cfl_lon < 0.0)), count(cfl_lat < 0.0))
        comps = args[0].shape[0]
        return lax.cond(
            most >= CAP,
            lambda *a: exchange(comps, comps, n_comp, n_geo, a),
            lambda *a: exchange(CAP, CAP - 1, n_comp, n_geo, a),
            *args,
        )

    return jax.shard_map(
        on_device, mesh=mesh, in_specs=placed, out_specs=P(None, AXES, None), check_vma=False
    )
```

```python
import functools

import jax
import jax.numpy as jnp
from jax import lax
from jax.experimental import pallas as pl
from jax.experimental.pallas import tpu as pltpu
from jax.sharding import PartitionSpec as P

AXES = ("comp", "geo")
CAP = 256
VMEM = pl.BlockSpec(memory_space=pltpu.VMEM)
SMEM = pl.BlockSpec(memory_space=pltpu.SMEM)
ANY = pl.BlockSpec(memory_space=pl.ANY)
LIMIT = 56 * 1024 * 1024


CHUNKS = 3


def columns_of(rows, stage):
    stage[...] = jnp.zeros(stage.shape, jnp.float32)
    for i, value in enumerate(rows):
        stage[i : i + 1, : value.shape[1]] = value
    return stage[...].T


def position():
    return lax.axis_index("comp"), lax.axis_index("geo")


def halves(value):
    high = value.astype(jnp.bfloat16)
    return high, (value - high.astype(jnp.float32)).astype(jnp.bfloat16)


def dot(a, b, contract=(1, 0)):
    return lax.dot_general(a, b, (((contract[0],), (contract[1],)), ((), ())), preferred_element_type=jnp.float32)


def source_kernel(
    cap, x_hbm, wind, growth, dissip, ice_rate, cfl_lon, cfl_lat, coupling, sea_ref, ice_ref,
    src, odd_msg, even_msg, top, places, xs, ss, stage, cols, top_stage, in_sems, out_sems,
):
    comps, lon_dev, lats = x_hbm.shape
    west, east = 0, lon_dev - 1
    order = (west, east, *range(1, lon_dev - 1))
    copies = [pltpu.make_async_copy(x_hbm.at[:, j, :], xs.at[j], in_sems.at[j]) for j in range(lon_dev)]
    for j in order:
        copies[j].start()
    odd = lax.rem(position()[1], 2)
    cols[...] = columns_of((growth[...], dissip[...], ice_rate[...]), stage)
    grow_c, diss_c, rate_c = (cols[:comps, i : i + 1] for i in range(3))
    coup_hi, coup_lo = halves(coupling[...])
    speed = cfl_lon[...] * jnp.where(odd == 1, 1.0, -1.0)
    pick = lax.broadcasted_iota(jnp.int32, (16, comps), 0)
    flags = jnp.where(pick == 0, speed, jnp.where(pick == 1, -speed, -cfl_lat[...])) > 0.0
    upto = lax.broadcasted_iota(jnp.int32, (comps, comps), 0) <= lax.broadcasted_iota(jnp.int32, (comps, comps), 1)
    ones = jnp.where(upto, 1.0, 0.0).astype(jnp.bfloat16)
    rank = dot(jnp.where(flags, 1.0, 0.0).astype(jnp.bfloat16), ones)
    place = jnp.where(flags, rank - 1.0, -1.0)
    places[...] = place[:8]

    def packing(i, rows):
        at = lax.broadcasted_iota(jnp.int32, (rows, comps), 0).astype(jnp.float32)
        return jnp.where(at == place[i : i + 1, :], 1.0, 0.0).astype(jnp.bfloat16)

    top_stage[comps:, :] = jnp.zeros((top_stage.shape[0] - comps, 128), jnp.float32)
    lane = lax.broadcasted_iota(jnp.int32, (comps, 128), 1)
    tops = jnp.zeros((comps, 128), jnp.float32)
    done = []
    for j in order:
        copies[j].wait()
        x = xs[j]
        mean = jnp.sum(x, axis=0, keepdims=True) / comps
        sat = mean / (1.0 + mean)
        sea = sea_ref[j : j + 1, :].astype(jnp.float32)
        ice = ice_ref[j : j + 1, :].astype(jnp.float32)
        x_hi, x_lo = halves(x)
        coupled = dot(coup_hi, x_hi) + dot(coup_hi, x_lo) + dot(coup_lo, x_hi)
        net = grow_c * wind[j : j + 1, :] - diss_c * sat - rate_c * ice
        value = sea * (x * jnp.exp(net) + 0.5 * coupled)
        ss[j] = value
        out = pltpu.make_async_copy(ss.at[j], src.at[j], out_sems.at[j])
        out.start()
        done.append(out)
        tops = jnp.where(lane == j, pltpu.roll(value[:, lats - 128 :], j + 1, 1), tops)
    top_stage[:comps, :] = tops
    lat_w = top.shape[2]
    top_hi, top_lo = halves(top_stage[...].T[:, :comps])
    top_pack = packing(2, lat_w)
    packed = (dot(top_hi, top_pack, (1, 1)) + dot(top_lo, top_pack, (1, 1)))[:lon_dev]
    sea_top = sea_ref[:, lats - 1 : lats].astype(jnp.float32)
    packed = jnp.where(lax.broadcasted_iota(jnp.int32, (lon_dev, lat_w), 1) == lat_w - 1, sea_top, packed)
    for slot in range(top.shape[0]):
        top[slot] = packed
    sea_w = sea_ref[west : west + 1, :].astype(jnp.float32)
    sea_e = sea_ref[east : east + 1, :].astype(jnp.float32)
    for i, (msg, col, sea) in enumerate((
        (odd_msg, jnp.where(odd == 1, east, west), jnp.where(odd == 1, sea_e, sea_w)),
        (even_msg, jnp.where(odd == 1, west, east), jnp.where(odd == 1, sea_w, sea_e)),
    )):
        hi, lo = halves(ss[col])
        pack = packing(i, cap)
        msg[:cap, :] = dot(pack, hi) + dot(pack, lo)
        msg[cap : cap + 8, :] = jnp.broadcast_to(sea, (8, lats))
    for out in done:
        out.wait()


def reroute_kernel(shape, fold, got, out, sems):
    n_c, n_y, n_h, n_x = shape
    me_c, me_geo = position()
    me_x, me_h, me_y = lax.rem(me_geo, n_x), lax.rem(me_geo // n_x, n_h), me_geo // (n_x * n_h)
    total = n_c * n_y * n_h * n_x
    lon_dev = got.shape[1]
    copies = []
    for i in range(2):
        q = lax.rem(fold[0] // lon_dev - i + total, total)
        q_x, q_h, q_y = lax.rem(q, n_x), lax.rem(q // n_x, n_h), lax.rem(q // (n_x * n_h), n_y)
        to_x = lax.rem(q_x - me_x + n_x, n_x)
        short = q_h - me_h - (to_x > q_x).astype(jnp.int32)
        to_y = lax.rem(q_y - me_y - (short < 0).astype(jnp.int32) + 2 * n_y, n_y)
        to = ((me_c * n_y + to_y) * n_h + me_h) * n_x + to_x
        source = lax.rem(q - to + total, total)
        of_c, of_h = source // (n_y * n_h * n_x), lax.rem(source // n_x, n_h)
        copies.append(pltpu.make_async_copy(got.at[of_c * n_h + of_h], out.at[to_y * n_x + to_x], sems.at[i]))
    for copy in copies:
        copy.start()
    for copy in copies:
        copy.wait()


def transport_kernel(
    cap, shape, fold, over, src_hbm, odd_hbm, even_hbm, seam_hbm, halo_hbm, norths_hbm, places, cfl_lon, cfl_lat, sea_ref,
    out, src, outs, msgs, seam, halo, norths, stage, cols, top_rows, in_sems, out_sems,
):
    lon_dev, comps, lats = src.shape
    me_c, me_geo = position()
    odd = lax.rem(me_geo, 2)
    n_c, n_y, n_h, n_x = shape
    total = n_c * n_y * n_h * n_x
    q = fold[0] // lon_dev
    shift = lax.rem(fold[0], lon_dev)

    def slot_of(q):
        source = lax.rem(q - (me_c * (total // n_c) + me_geo) + 2 * total, total)
        return lax.rem(source // (n_h * n_x), n_y) * n_x + lax.rem(source, n_x)

    slot_0, slot_1 = slot_of(q), slot_of(q - 1)
    copies = [
        pltpu.make_async_copy(seam_hbm.at[slot_0], seam.at[0], in_sems.at[0]),
        pltpu.make_async_copy(seam_hbm.at[slot_1], seam.at[1], in_sems.at[1]),
        pltpu.make_async_copy(odd_hbm, msgs.at[0], in_sems.at[2]),
        pltpu.make_async_copy(even_hbm, msgs.at[1], in_sems.at[3]),
        pltpu.make_async_copy(src_hbm, src, in_sems.at[4]),
    ]
    for copy in copies:
        copy.start()
    cols[...] = columns_of((cfl_lon[...], cfl_lat[...], places[1:2, :], places[0:1, :], places[2:3, :]), stage)
    copies[0].wait()
    copies[1].wait()
    lat_w = seam.shape[2]
    top_rows[...] = jnp.zeros(top_rows.shape, jnp.float32)
    for j in range(lon_dev):
        place = shift - j
        block = jnp.where(place >= 0, 0, 1)
        row = jnp.where(place >= 0, place, place + lon_dev)
        top_rows[j : j + 1, :] = seam[block, pl.ds(row, 1), :]

    def spread(i, width):
        at = lax.broadcasted_iota(jnp.int32, (comps, width), 1).astype(jnp.float32)
        return jnp.where(at == cols[:comps, 2 + i : 3 + i], 1.0, 0.0).astype(jnp.bfloat16)

    top_hi, top_lo = halves(top_rows[...])
    top_spread = spread(2, lat_w)
    norths[...] = dot(top_spread, top_hi, (1, 1)) + dot(top_spread, top_lo, (1, 1))
    copies[2].wait()
    copies[3].wait()
    both = None
    for i in range(2):
        hi, lo = halves(msgs[i, :cap, :])
        part = spread(i, cap)
        part = dot(part, hi) + dot(part, lo)
        both = part if both is None else both + part
    halo[...] = both

    @pl.when(over[0] > 0)
    def _():
        pltpu.sync_copy(halo_hbm, halo)
        pltpu.sync_copy(norths_hbm, norths)

    sea_odd, sea_even = msgs[0, cap : cap + 1, :], msgs[1, cap : cap + 1, :]
    sea_west = jnp.where(odd == 1, sea_even, sea_odd)
    sea_east = jnp.where(odd == 1, sea_odd, sea_even)
    sea = [sea_ref[j : j + 1, :].astype(jnp.float32) for j in range(lon_dev)]
    open_lon = [
        (sea_west if j == 0 else sea[j - 1]) * (sea_east if j == lon_dev else sea[j]) for j in range(lon_dev + 1)
    ]
    step = 8
    lane = lax.broadcasted_iota(jnp.int32, (step, lats), 1)
    first, last = lane == 0, lane == lats - 1
    tall = []
    for j in range(lon_dev):
        own = jnp.broadcast_to(sea[j], (step, lats))
        north = jnp.broadcast_to(top_rows[j : j + 1, lat_w - 1 : lat_w], (step, lats))
        tall.append(own * jnp.where(last, north, pltpu.roll(own, lats - 1, 1)))
    wide = [jnp.broadcast_to(v, (step, lats)) for v in open_lon]
    copies[4].wait()

    def rows(i, carry):
        at = pl.ds(pl.multiple_of(i * step, step), step)
        params = cols[at, :]
        lon_pos = jnp.maximum(params[:, 0:1], 0.0)
        lon_neg = jnp.minimum(params[:, 0:1], 0.0)
        lat_pos = jnp.maximum(params[:, 1:2], 0.0)
        lat_neg = jnp.minimum(params[:, 1:2], 0.0)
        tops = norths[at, :]
        edge = halo[at, :]
        vals = [src[j, at, :] for j in range(lon_dev)]
        ends = [edge, *vals, edge]
        flux = [wide[j] * (lon_pos * ends[j] + lon_neg * ends[j + 1]) for j in range(lon_dev + 1)]
        for j in range(lon_dev):
            up = jnp.where(last, tops[:, j : j + 1], pltpu.roll(vals[j], lats - 1, 1))
            lat = tall[j] * (lat_pos * vals[j] + lat_neg * up)
            south = jnp.where(first, 0.0, pltpu.roll(lat, 1, 1))
            outs[j, at, :] = vals[j] - (flux[j + 1] - flux[j]) - (lat - south)
        return carry

    piece = comps // CHUNKS
    done = []
    for c in range(CHUNKS):
        lax.fori_loop(c * piece // step, (c + 1) * piece // step, rows, 0, unroll=2)
        at = pl.ds(c * piece, piece)
        for j in range(lon_dev):
            copy = pltpu.make_async_copy(outs.at[j, at, :], out.at[at, j, :], out_sems.at[c, j])
            copy.start()
            done.append(copy)
    for copy in done:
        copy.wait()


def whole_edges(cfl_lon, src, fold_partner):
    lon_dev = src.shape[0]
    count = lax.axis_size("comp") * lax.axis_size("geo")
    forward = [(d, (d + 1) % count) for d in range(count)]
    west = lax.ppermute(src[lon_dev - 1], AXES, forward)
    east = lax.ppermute(src[0], AXES, [(b, a) for a, b in forward])
    halo = jnp.where(cfl_lon[:, None] > 0.0, west, east)
    tops = lax.all_gather(src[:, :, -1], AXES, axis=0, tiled=True)
    own = (lax.axis_index("comp") * lax.axis_size("geo") + lax.axis_index("geo")) * lon_dev + jnp.arange(lon_dev)
    norths = jnp.take(tops, jnp.take(fold_partner, own), axis=0).T
    return halo, jnp.pad(norths, ((0, 0), (0, 128 - lon_dev)))


def solution(mesh):
    n_c, n_geo = mesh.shape["comp"], mesh.shape["geo"]
    shape = (n_c, n_geo // 8, 2, 4)
    _, n_y, n_h, n_x = shape
    count = n_c * n_geo
    lon = P(AXES, None)
    placed = (P(None, AXES, None), lon, P(), P(), P(), P(), P(), P(), lon, lon, P())
    f32 = jnp.float32
    params = pltpu.CompilerParams(vmem_limit_bytes=LIMIT)
    flat = lambda c, y, h, x: ((c * n_y + y) * n_h + h) * n_x + x
    columns = [[flat(c, y, h, x) for c in range(n_c) for h in range(n_h)] for y in range(n_y) for x in range(n_x)]
    planes = [[flat(c, y, h, x) for y in range(n_y) for x in range(n_x)] for c in range(n_c) for h in range(n_h)]
    odd_pairs = [(d, (d + 1) % count if d % 2 else (d - 1) % count) for d in range(count)]
    even_pairs = [(d, d - 1 if d % 2 else d + 1) for d in range(count)]

    def on_device(
        spectrum, wind_speed, growth, dissip, ice_rate, coupling, cfl_lon, cfl_lat, sea_mask, ice_mask, fold_partner
    ):
        comps, lon_dev, lats = spectrum.shape
        wide = -(-comps // 128) * 128
        lat_w = CAP
        size = CAP + 8
        row = lambda v: v.reshape(1, comps)
        src, odd_msg, even_msg, top, places = pl.pallas_call(
            functools.partial(source_kernel, CAP),
            out_shape=(
                jax.ShapeDtypeStruct((lon_dev, comps, lats), f32),
                jax.ShapeDtypeStruct((size, lats), f32),
                jax.ShapeDtypeStruct((size, lats), f32),
                jax.ShapeDtypeStruct((n_c * n_h, lon_dev, lat_w), f32),
                jax.ShapeDtypeStruct((8, comps), f32),
            ),
            in_specs=[ANY] + [VMEM] * 9,
            out_specs=(ANY, VMEM, VMEM, VMEM, VMEM),
            scratch_shapes=[
                pltpu.VMEM((lon_dev, comps, lats), f32),
                pltpu.VMEM((lon_dev, comps, lats), f32),
                pltpu.VMEM((128, wide), f32),
                pltpu.VMEM((wide, 128), f32),
                pltpu.VMEM((wide, 128), f32),
                pltpu.SemaphoreType.DMA((lon_dev,)),
                pltpu.SemaphoreType.DMA((lon_dev,)),
            ],
            compiler_params=params,
            name="source",
        )(
            spectrum, wind_speed, row(growth), row(dissip), row(ice_rate), row(cfl_lon), row(cfl_lat),
            coupling, sea_mask, ice_mask,
        )
        odd_got = lax.ppermute(odd_msg, AXES, odd_pairs)
        even_got = lax.ppermute(even_msg, AXES, even_pairs)
        by_column = lax.all_to_all(top, AXES, 0, 0, tiled=True, axis_index_groups=columns)
        slots = pl.pallas_call(
            functools.partial(reroute_kernel, shape),
            out_shape=jax.ShapeDtypeStruct((n_y * n_x, lon_dev, lat_w), f32),
            in_specs=[SMEM, ANY],
            out_specs=ANY,
            scratch_shapes=[pltpu.SemaphoreType.DMA((2,))],
            name="reroute",
        )(fold_partner, by_column)
        seam = lax.all_to_all(slots, AXES, 0, 0, tiled=True, axis_index_groups=planes)
        signs = jnp.stack([cfl_lon, -cfl_lon, -cfl_lat])
        over = jnp.max(jnp.sum((signs > 0.0).astype(jnp.int32), axis=1)) >= CAP
        halo, norths = lax.cond(
            over,
            whole_edges,
            lambda *_: (jnp.zeros((comps, lats), f32), jnp.zeros((comps, 128), f32)),
            cfl_lon, src, fold_partner,
        )
        return pl.pallas_call(
            functools.partial(transport_kernel, CAP, shape),
            out_shape=jax.ShapeDtypeStruct((comps, lon_dev, lats), f32),
            in_specs=[SMEM, SMEM] + [ANY] * 6 + [VMEM] * 4,
            out_specs=ANY,
            scratch_shapes=[
                pltpu.VMEM((lon_dev, comps, lats), f32),
                pltpu.VMEM((lon_dev, comps, lats), f32),
                pltpu.VMEM((2, size, lats), f32),
                pltpu.VMEM((2, lon_dev, lat_w), f32),
                pltpu.VMEM((comps, lats), f32),
                pltpu.VMEM((comps, 128), f32),
                pltpu.VMEM((128, wide), f32),
                pltpu.VMEM((wide, 128), f32),
                pltpu.VMEM((128, lat_w), f32),
                pltpu.SemaphoreType.DMA((5,)),
                pltpu.SemaphoreType.DMA((CHUNKS, lon_dev)),
            ],
            compiler_params=params,
            name="transport",
        )(
            fold_partner, over.astype(jnp.int32).reshape(1), src, odd_got, even_got, seam, halo, norths,
            places, row(cfl_lon), row(cfl_lat), sea_mask,
        )

    return jax.shard_map(
        on_device, mesh=mesh, in_specs=placed, out_specs=P(None, AXES, None), check_vma=False
    )
```

```python
import functools

import jax
import jax.numpy as jnp
from jax import lax
from jax.experimental import pallas as pl
from jax.experimental.pallas import tpu as pltpu
from jax.sharding import PartitionSpec as P

AXES = ("comp", "geo")
CAP = 256
VMEM = pl.BlockSpec(memory_space=pltpu.VMEM)
SMEM = pl.BlockSpec(memory_space=pltpu.SMEM)
ANY = pl.BlockSpec(memory_space=pl.ANY)
LIMIT = 56 * 1024 * 1024


CHUNKS = 3


def columns_of(rows, stage):
    stage[...] = jnp.zeros(stage.shape, jnp.float32)
    for i, value in enumerate(rows):
        stage[i : i + 1, : value.shape[1]] = value
    return stage[...].T


def position():
    return lax.axis_index("comp"), lax.axis_index("geo")


def halves(value):
    high = value.astype(jnp.bfloat16)
    return high, (value - high.astype(jnp.float32)).astype(jnp.bfloat16)


def dot(a, b, contract=(1, 0)):
    return lax.dot_general(a, b, (((contract[0],), (contract[1],)), ((), ())), preferred_element_type=jnp.float32)


def source_kernel(
    cap, x_hbm, wind, growth, dissip, ice_rate, cfl_lon, cfl_lat, coupling, sea_ref, ice_ref,
    src, odd_msg, even_msg, top, places, xs, ss, stage, cols, top_stage, in_sems, out_sems,
):
    comps, lon_dev, lats = x_hbm.shape
    west, east = 0, lon_dev - 1
    order = (west, east, *range(1, lon_dev - 1))
    copies = [pltpu.make_async_copy(x_hbm.at[:, j, :], xs.at[j], in_sems.at[j]) for j in range(lon_dev)]
    for j in order:
        copies[j].start()
    odd = lax.rem(position()[1], 2)
    cols[...] = columns_of((growth[...], dissip[...], ice_rate[...]), stage)
    grow_c, diss_c, rate_c = (cols[:comps, i : i + 1] for i in range(3))
    coup_hi, coup_lo = halves(coupling[...])
    speed = cfl_lon[...] * jnp.where(odd == 1, 1.0, -1.0)
    pick = lax.broadcasted_iota(jnp.int32, (16, comps), 0)
    flags = jnp.where(pick == 0, speed, jnp.where(pick == 1, -speed, -cfl_lat[...])) > 0.0
    upto = lax.broadcasted_iota(jnp.int32, (comps, comps), 0) <= lax.broadcasted_iota(jnp.int32, (comps, comps), 1)
    ones = jnp.where(upto, 1.0, 0.0).astype(jnp.bfloat16)
    rank = dot(jnp.where(flags, 1.0, 0.0).astype(jnp.bfloat16), ones)
    place = jnp.where(flags, rank - 1.0, -1.0)
    places[...] = place[:8]

    def packing(i, rows):
        at = lax.broadcasted_iota(jnp.int32, (rows, comps), 0).astype(jnp.float32)
        return jnp.where(at == place[i : i + 1, :], 1.0, 0.0).astype(jnp.bfloat16)

    top_stage[comps:, :] = jnp.zeros((top_stage.shape[0] - comps, 128), jnp.float32)
    lane = lax.broadcasted_iota(jnp.int32, (comps, 128), 1)
    tops = jnp.zeros((comps, 128), jnp.float32)
    done = []
    for j in order:
        copies[j].wait()
        x = xs[j]
        mean = jnp.sum(x, axis=0, keepdims=True) / comps
        sat = mean / (1.0 + mean)
        sea = sea_ref[j : j + 1, :].astype(jnp.float32)
        ice = ice_ref[j : j + 1, :].astype(jnp.float32)
        x_hi, x_lo = halves(x)
        coupled = dot(coup_hi, x_hi) + dot(coup_hi, x_lo) + dot(coup_lo, x_hi)
        net = grow_c * wind[j : j + 1, :] - diss_c * sat - rate_c * ice
        value = sea * (x * jnp.exp(net) + 0.5 * coupled)
        ss[j] = value
        out = pltpu.make_async_copy(ss.at[j], src.at[j], out_sems.at[j])
        out.start()
        done.append(out)
        tops = jnp.where(lane == j, pltpu.roll(value[:, lats - 128 :], j + 1, 1), tops)
    top_stage[:comps, :] = tops
    lat_w = top.shape[2]
    top_hi, top_lo = halves(top_stage[...].T[:, :comps])
    top_pack = packing(2, lat_w)
    packed = (dot(top_hi, top_pack, (1, 1)) + dot(top_lo, top_pack, (1, 1)))[:lon_dev]
    sea_top = sea_ref[:, lats - 1 : lats].astype(jnp.float32)
    packed = jnp.where(lax.broadcasted_iota(jnp.int32, (lon_dev, lat_w), 1) == lat_w - 1, sea_top, packed)
    for slot in range(top.shape[0]):
        top[slot] = packed
    sea_w = sea_ref[west : west + 1, :].astype(jnp.float32)
    sea_e = sea_ref[east : east + 1, :].astype(jnp.float32)
    for i, (msg, col, sea) in enumerate((
        (odd_msg, jnp.where(odd == 1, east, west), jnp.where(odd == 1, sea_e, sea_w)),
        (even_msg, jnp.where(odd == 1, west, east), jnp.where(odd == 1, sea_w, sea_e)),
    )):
        hi, lo = halves(ss[col])
        pack = packing(i, cap)
        msg[:cap, :] = dot(pack, hi) + dot(pack, lo)
        msg[cap : cap + 8, :] = jnp.broadcast_to(sea, (8, lats))
    for out in done:
        out.wait()


def source_geo(q, me_geo, n_geo):
    return lax.rem(lax.rem(q, n_geo) - me_geo + n_geo, n_geo)


def reroute_kernel(n_comp, n_geo, fold, got, out, sems):
    me_comp, me_geo = position()
    total = n_comp * n_geo
    lon_dev = got.shape[1]
    copies = []
    for i in range(2):
        q = lax.rem(fold[0] // lon_dev - i + total, total)
        to_geo = source_geo(q, me_geo, n_geo)
        source = lax.rem(q - (me_comp * n_geo + to_geo) + total, total)
        copies.append(pltpu.make_async_copy(got.at[source // n_geo], out.at[to_geo], sems.at[i]))
    for copy in copies:
        copy.start()
    for copy in copies:
        copy.wait()


def seam_of(n_comp, n_geo, top, fold_partner):
    by_comp = lax.all_to_all(top, "comp", 0, 0, tiled=True)
    slots = pl.pallas_call(
        functools.partial(reroute_kernel, n_comp, n_geo),
        out_shape=jax.ShapeDtypeStruct((n_geo, *top.shape[1:]), jnp.float32),
        in_specs=[SMEM, ANY],
        out_specs=ANY,
        scratch_shapes=[pltpu.SemaphoreType.DMA((2,))],
        name="reroute",
    )(fold_partner, by_comp)
    return lax.all_to_all(slots, "geo", 0, 0, tiled=True)


def transport_kernel(
    cap, n_geo, fold, over, src_hbm, odd_hbm, even_hbm, seam_hbm, halo_hbm, norths_hbm, places, cfl_lon, cfl_lat, sea_ref,
    out, src, outs, msgs, seam, halo, norths, stage, cols, top_rows, in_sems, out_sems,
):
    lon_dev, comps, lats = src.shape
    _, me_geo = position()
    odd = lax.rem(me_geo, 2)
    q = fold[0] // lon_dev
    shift = lax.rem(fold[0], lon_dev)
    slot_0 = source_geo(q, me_geo, n_geo)
    slot_1 = source_geo(q + n_geo - 1, me_geo, n_geo)
    copies = [
        pltpu.make_async_copy(seam_hbm.at[slot_0], seam.at[0], in_sems.at[0]),
        pltpu.make_async_copy(seam_hbm.at[slot_1], seam.at[1], in_sems.at[1]),
        pltpu.make_async_copy(odd_hbm, msgs.at[0], in_sems.at[2]),
        pltpu.make_async_copy(even_hbm, msgs.at[1], in_sems.at[3]),
        pltpu.make_async_copy(src_hbm, src, in_sems.at[4]),
    ]
    for copy in copies:
        copy.start()
    cols[...] = columns_of((cfl_lon[...], cfl_lat[...], places[1:2, :], places[0:1, :], places[2:3, :]), stage)
    copies[0].wait()
    copies[1].wait()
    lat_w = seam.shape[2]
    top_rows[...] = jnp.zeros(top_rows.shape, jnp.float32)
    for j in range(lon_dev):
        place = shift - j
        block = jnp.where(place >= 0, 0, 1)
        row = jnp.where(place >= 0, place, place + lon_dev)
        top_rows[j : j + 1, :] = seam[block, pl.ds(row, 1), :]

    def spread(i, width):
        at = lax.broadcasted_iota(jnp.int32, (comps, width), 1).astype(jnp.float32)
        return jnp.where(at == cols[:comps, 2 + i : 3 + i], 1.0, 0.0).astype(jnp.bfloat16)

    top_hi, top_lo = halves(top_rows[...])
    top_spread = spread(2, lat_w)
    norths[...] = dot(top_spread, top_hi, (1, 1)) + dot(top_spread, top_lo, (1, 1))
    copies[2].wait()
    copies[3].wait()
    both = None
    for i in range(2):
        hi, lo = halves(msgs[i, :cap, :])
        part = spread(i, cap)
        part = dot(part, hi) + dot(part, lo)
        both = part if both is None else both + part
    halo[...] = both

    @pl.when(over[0] > 0)
    def _():
        pltpu.sync_copy(halo_hbm, halo)
        pltpu.sync_copy(norths_hbm, norths)

    sea_odd, sea_even = msgs[0, cap : cap + 1, :], msgs[1, cap : cap + 1, :]
    sea_west = jnp.where(odd == 1, sea_even, sea_odd)
    sea_east = jnp.where(odd == 1, sea_odd, sea_even)
    sea = [sea_ref[j : j + 1, :].astype(jnp.float32) for j in range(lon_dev)]
    open_lon = [
        (sea_west if j == 0 else sea[j - 1]) * (sea_east if j == lon_dev else sea[j]) for j in range(lon_dev + 1)
    ]
    step = 8
    lane = lax.broadcasted_iota(jnp.int32, (step, lats), 1)
    first, last = lane == 0, lane == lats - 1
    tall = []
    for j in range(lon_dev):
        own = jnp.broadcast_to(sea[j], (step, lats))
        north = jnp.broadcast_to(top_rows[j : j + 1, lat_w - 1 : lat_w], (step, lats))
        tall.append(own * jnp.where(last, north, pltpu.roll(own, lats - 1, 1)))
    wide = [jnp.broadcast_to(v, (step, lats)) for v in open_lon]
    copies[4].wait()

    def rows(i, carry):
        at = pl.ds(pl.multiple_of(i * step, step), step)
        params = cols[at, :]
        lon_pos = jnp.maximum(params[:, 0:1], 0.0)
        lon_neg = jnp.minimum(params[:, 0:1], 0.0)
        lat_pos = jnp.maximum(params[:, 1:2], 0.0)
        lat_neg = jnp.minimum(params[:, 1:2], 0.0)
        tops = norths[at, :]
        edge = halo[at, :]
        vals = [src[j, at, :] for j in range(lon_dev)]
        ends = [edge, *vals, edge]
        flux = [wide[j] * (lon_pos * ends[j] + lon_neg * ends[j + 1]) for j in range(lon_dev + 1)]
        for j in range(lon_dev):
            up = jnp.where(last, tops[:, j : j + 1], pltpu.roll(vals[j], lats - 1, 1))
            lat = tall[j] * (lat_pos * vals[j] + lat_neg * up)
            south = jnp.where(first, 0.0, pltpu.roll(lat, 1, 1))
            outs[j, at, :] = vals[j] - (flux[j + 1] - flux[j]) - (lat - south)
        return carry

    piece = comps // CHUNKS
    done = []
    for c in range(CHUNKS):
        lax.fori_loop(c * piece // step, (c + 1) * piece // step, rows, 0, unroll=2)
        at = pl.ds(c * piece, piece)
        for j in range(lon_dev):
            copy = pltpu.make_async_copy(outs.at[j, at, :], out.at[at, j, :], out_sems.at[c, j])
            copy.start()
            done.append(copy)
    for copy in done:
        copy.wait()


def whole_edges(count, cfl_lon, src, fold_partner):
    lon_dev = src.shape[0]
    forward = [(d, (d + 1) % count) for d in range(count)]
    west = lax.ppermute(src[lon_dev - 1], AXES, forward)
    east = lax.ppermute(src[0], AXES, [(b, a) for a, b in forward])
    halo = jnp.where(cfl_lon[:, None] > 0.0, west, east)
    q, shift = fold_partner[0] // lon_dev, fold_partner[0] % lon_dev
    block = lax.ppermute(src[:, :, -1], AXES, [(d, -d % count) for d in range(count)])
    for bit in range((count - 1).bit_length()):
        moved = lax.ppermute(block, AXES, [(d, (d + (1 << bit)) % count) for d in range(count)])
        block = jnp.where((q >> bit) % 2 == 1, moved, block)
    before = lax.ppermute(block, AXES, [((d + 1) % count, d) for d in range(count)])
    window = jnp.concatenate([before, block], axis=0)
    norths = jnp.take(window, lon_dev + shift - jnp.arange(lon_dev), axis=0).T
    return halo, jnp.pad(norths, ((0, 0), (0, 128 - lon_dev)))


def solution(mesh):
    n_comp, n_geo = mesh.shape["comp"], mesh.shape["geo"]
    count = n_comp * n_geo
    lon = P(AXES, None)
    placed = (P(None, AXES, None), lon, P(), P(), P(), P(), P(), P(), lon, lon, P())
    f32 = jnp.float32
    params = pltpu.CompilerParams(vmem_limit_bytes=LIMIT)
    odd_pairs = [(d, (d + 1) % count if d % 2 else (d - 1) % count) for d in range(count)]
    even_pairs = [(d, d - 1 if d % 2 else d + 1) for d in range(count)]

    def on_device(
        spectrum, wind_speed, growth, dissip, ice_rate, coupling, cfl_lon, cfl_lat, sea_mask, ice_mask, fold_partner
    ):
        comps, lon_dev, lats = spectrum.shape
        wide = -(-comps // 128) * 128
        lat_w = CAP
        size = CAP + 8
        row = lambda v: v.reshape(1, comps)
        src, odd_msg, even_msg, top, places = pl.pallas_call(
            functools.partial(source_kernel, CAP),
            out_shape=(
                jax.ShapeDtypeStruct((lon_dev, comps, lats), f32),
                jax.ShapeDtypeStruct((size, lats), f32),
                jax.ShapeDtypeStruct((size, lats), f32),
                jax.ShapeDtypeStruct((n_comp, lon_dev, lat_w), f32),
                jax.ShapeDtypeStruct((8, comps), f32),
            ),
            in_specs=[ANY] + [VMEM] * 9,
            out_specs=(ANY, VMEM, VMEM, VMEM, VMEM),
            scratch_shapes=[
                pltpu.VMEM((lon_dev, comps, lats), f32),
                pltpu.VMEM((lon_dev, comps, lats), f32),
                pltpu.VMEM((128, wide), f32),
                pltpu.VMEM((wide, 128), f32),
                pltpu.VMEM((wide, 128), f32),
                pltpu.SemaphoreType.DMA((lon_dev,)),
                pltpu.SemaphoreType.DMA((lon_dev,)),
            ],
            compiler_params=params,
            name="source",
        )(
            spectrum, wind_speed, row(growth), row(dissip), row(ice_rate), row(cfl_lon), row(cfl_lat),
            coupling, sea_mask, ice_mask,
        )
        odd_got = lax.ppermute(odd_msg, AXES, odd_pairs)
        even_got = lax.ppermute(even_msg, AXES, even_pairs)
        seam = seam_of(n_comp, n_geo, top, fold_partner)
        signs = jnp.stack([cfl_lon, -cfl_lon, -cfl_lat])
        over = jnp.max(jnp.sum((signs > 0.0).astype(jnp.int32), axis=1)) >= CAP
        halo, norths = lax.cond(
            over,
            functools.partial(whole_edges, count),
            lambda *_: (jnp.zeros((comps, lats), f32), jnp.zeros((comps, 128), f32)),
            cfl_lon, src, fold_partner,
        )
        return pl.pallas_call(
            functools.partial(transport_kernel, CAP, n_geo),
            out_shape=jax.ShapeDtypeStruct((comps, lon_dev, lats), f32),
            in_specs=[SMEM, SMEM] + [ANY] * 6 + [VMEM] * 4,
            out_specs=ANY,
            scratch_shapes=[
                pltpu.VMEM((lon_dev, comps, lats), f32),
                pltpu.VMEM((lon_dev, comps, lats), f32),
                pltpu.VMEM((2, size, lats), f32),
                pltpu.VMEM((2, lon_dev, lat_w), f32),
                pltpu.VMEM((comps, lats), f32),
                pltpu.VMEM((comps, 128), f32),
                pltpu.VMEM((128, wide), f32),
                pltpu.VMEM((wide, 128), f32),
                pltpu.VMEM((128, lat_w), f32),
                pltpu.SemaphoreType.DMA((5,)),
                pltpu.SemaphoreType.DMA((CHUNKS, lon_dev)),
            ],
            compiler_params=params,
            name="transport",
        )(
            fold_partner, over.astype(jnp.int32).reshape(1), src, odd_got, even_got, seam, halo, norths,
            places, row(cfl_lon), row(cfl_lat), sea_mask,
        )

    return jax.shard_map(
        on_device, mesh=mesh, in_specs=placed, out_specs=P(None, AXES, None), check_vma=False
    )
```

```python
import functools

import jax
import jax.numpy as jnp
from jax import lax
from jax.experimental import pallas as pl
from jax.experimental.pallas import tpu as pltpu
from jax.sharding import PartitionSpec as P

AXES = ("comp", "geo")
CAP = 256
VMEM = pl.BlockSpec(memory_space=pltpu.VMEM)
SMEM = pl.BlockSpec(memory_space=pltpu.SMEM)
ANY = pl.BlockSpec(memory_space=pl.ANY)
LIMIT = 56 * 1024 * 1024


CHUNKS = 3


def columns_of(rows, stage):
    stage[...] = jnp.zeros(stage.shape, jnp.float32)
    for i, value in enumerate(rows):
        stage[i : i + 1, : value.shape[1]] = value
    return stage[...].T


def position():
    return lax.axis_index("comp"), lax.axis_index("geo")


def halves(value):
    high = value.astype(jnp.bfloat16)
    return high, (value - high.astype(jnp.float32)).astype(jnp.bfloat16)


def dot(a, b, contract=(1, 0)):
    return lax.dot_general(a, b, (((contract[0],), (contract[1],)), ((), ())), preferred_element_type=jnp.float32)


def start_all(copies):
    for copy in copies:
        copy.start()


def wait_all(copies):
    for copy in copies:
        copy.wait()


def source_terms(x, sea, wind, ice, grow_c, diss_c, rate_c, coup_hi, coup_lo):
    mean = jnp.sum(x, axis=0, keepdims=True) / x.shape[0]
    x_hi, x_lo = halves(x)
    coupled = dot(coup_hi, x_hi) + dot(coup_hi, x_lo) + dot(coup_lo, x_hi)
    net = grow_c * wind - diss_c * (mean / (1.0 + mean)) - rate_c * ice
    return sea * (x * jnp.exp(net) + 0.5 * coupled)


def edges_kernel(
    cap, x_hbm, coup_hbm, wind_hbm, growth_hbm, dissip_hbm, ice_rate_hbm, cfl_lon_hbm, cfl_lat_hbm, sea_hbm, ice_hbm,
    src, own_top, odd_hbm, even_hbm, top_hbm, places_hbm,
    xs, xt, ss, raw_top, stage, cols, top_stage, coupling, wind, growth, dissip, ice_rate, cfl_lon, cfl_lat, sea_ref, ice_ref,
    odd_msg, even_msg, top, places, x_sems, in_sems, out_sems,
):
    comps, lon_dev, lats = x_hbm.shape
    ends = (0, lon_dev - 1)
    last = pl.ds(lats - 128, 128)
    big = [pltpu.make_async_copy(x_hbm.at[:, j, :], xs.at[i], x_sems.at[i]) for i, j in enumerate(ends)]
    slim = [
        pltpu.make_async_copy(x_hbm.at[:, j, last], xt.at[j - 1], x_sems.at[j + 1]) for j in range(1, lon_dev - 1)
    ]
    small = [
        pltpu.make_async_copy(here, there, in_sems.at[i])
        for i, (here, there) in enumerate((
            (cfl_lon_hbm, cfl_lon), (cfl_lat_hbm, cfl_lat), (growth_hbm, growth), (dissip_hbm, dissip),
            (ice_rate_hbm, ice_rate), (coup_hbm, coupling), (wind_hbm, wind), (sea_hbm, sea_ref), (ice_hbm, ice_ref),
        ))
    ]
    start_all((*small[:5], big[0], small[5], big[1], *small[6:], *slim))
    outs = iter(out_sems.at[i] for i in range(out_sems.shape[0]))
    done = []

    def send(here, there):
        copy = pltpu.make_async_copy(here, there, next(outs))
        copy.start()
        done.append(copy)

    odd = lax.rem(position()[1], 2)
    wait_all(small[:5])
    cols[...] = columns_of((growth[...], dissip[...], ice_rate[...]), stage)
    grow_c, diss_c, rate_c = (cols[:comps, i : i + 1] for i in range(3))
    speed = cfl_lon[...] * jnp.where(odd == 1, 1.0, -1.0)
    pick = lax.broadcasted_iota(jnp.int32, (16, comps), 0)
    flags = jnp.where(pick == 0, speed, jnp.where(pick == 1, -speed, -cfl_lat[...])) > 0.0
    upto = lax.broadcasted_iota(jnp.int32, (comps, comps), 0) <= lax.broadcasted_iota(jnp.int32, (comps, comps), 1)
    ones = jnp.where(upto, 1.0, 0.0).astype(jnp.bfloat16)
    rank = dot(jnp.where(flags, 1.0, 0.0).astype(jnp.bfloat16), ones)
    place = jnp.where(flags, rank - 1.0, -1.0)
    places[...] = place[:8]
    send(places, places_hbm)

    def packing(i, rows):
        at = lax.broadcasted_iota(jnp.int32, (rows, comps), 0).astype(jnp.float32)
        return jnp.where(at == place[i : i + 1, :], 1.0, 0.0).astype(jnp.bfloat16)

    wait_all(small[5:])
    coup_hi, coup_lo = halves(coupling[...])
    terms = functools.partial(
        source_terms, grow_c=grow_c, diss_c=diss_c, rate_c=rate_c, coup_hi=coup_hi, coup_lo=coup_lo
    )
    lane = lax.broadcasted_iota(jnp.int32, (comps, 128), 1)
    lane8 = lax.broadcasted_iota(jnp.int32, (8, 128), 1)

    def gather_last(tile_of, lane):
        total = jnp.zeros(lane.shape, jnp.float32)
        for j in range(lon_dev):
            total = jnp.where(lane == j, pltpu.roll(tile_of(j), j + 1, 1), total)
        return total

    row_top = lambda ref: gather_last(
        lambda j: jnp.broadcast_to(ref[j : j + 1, lats - 128 :].astype(jnp.float32), (8, 128)), lane8
    )[:1]
    row = lambda ref, j: ref[j : j + 1, :].astype(jnp.float32)
    wait_all(big)
    wait_all(slim)
    raw_top[...] = gather_last(
        lambda j: xs[ends.index(j), :, lats - 128 :] if j in ends else xt[j - 1], lane
    )
    top_stage[...] = jnp.zeros(top_stage.shape, jnp.float32)
    top_stage[:comps, :] = terms(raw_top[...], row_top(sea_ref), row_top(wind), row_top(ice_ref))
    send(top_stage.at[:comps], own_top)
    lat_w = top.shape[1]
    top_hi, top_lo = halves(top_stage[...].T[:, :comps])
    top_pack = packing(2, lat_w)
    packed = (dot(top_hi, top_pack, (1, 1)) + dot(top_lo, top_pack, (1, 1)))[:lon_dev]
    sea_top = sea_ref[:, lats - 1 : lats].astype(jnp.float32)
    top[...] = jnp.where(lax.broadcasted_iota(jnp.int32, (lon_dev, lat_w), 1) == lat_w - 1, sea_top, packed)
    for slot in range(top_hbm.shape[0]):
        send(top, top_hbm.at[slot])
    for i, j in enumerate(ends):
        ss[i] = terms(xs[i], row(sea_ref, j), row(wind, j), row(ice_ref, j))
        send(ss.at[i], src.at[i])
    for i, (msg, msg_hbm) in enumerate(((odd_msg, odd_hbm), (even_msg, even_hbm))):
        end = odd if i == 0 else 1 - odd
        hi, lo = halves(ss[end])
        pack = packing(i, cap)
        msg[:cap, :] = dot(pack, hi) + dot(pack, lo)
        sea = jnp.where(end == 1, row(sea_ref, ends[1]), row(sea_ref, ends[0]))
        msg[cap : cap + 8, :] = jnp.broadcast_to(sea, (8, lats))
        send(msg, msg_hbm)
    wait_all(done)


def inner_kernel(
    x_hbm, coup_hbm, src_hbm, wind_hbm, growth_hbm, dissip_hbm, ice_rate_hbm, cfl_lon_hbm, cfl_lat_hbm, sea_hbm, ice_hbm,
    out, xs, src, outs, stage, cols, coupling, wind, growth, dissip, ice_rate, cfl_lon, cfl_lat, sea_ref, ice_ref,
    in_sems, out_sems,
):
    comps, lon_dev, lats = x_hbm.shape
    middle = range(1, lon_dev - 1)
    pairs = [
        (cfl_lon_hbm, cfl_lon), (cfl_lat_hbm, cfl_lat), (growth_hbm, growth), (dissip_hbm, dissip),
        (ice_rate_hbm, ice_rate), (coup_hbm, coupling), (wind_hbm, wind), (sea_hbm, sea_ref), (ice_hbm, ice_ref),
        *((x_hbm.at[:, j, :], xs.at[j - 1]) for j in middle),
        (src_hbm.at[0], src.at[0]), (src_hbm.at[1], src.at[lon_dev - 1]),
    ]
    copies = [pltpu.make_async_copy(here, there, in_sems.at[i]) for i, (here, there) in enumerate(pairs)]
    start_all(copies)
    wait_all(copies[:5])
    cols[...] = columns_of((growth[...], dissip[...], ice_rate[...], cfl_lon[...], cfl_lat[...]), stage)
    grow_c, diss_c, rate_c = (cols[:comps, i : i + 1] for i in range(3))
    wait_all(copies[5:])
    coup_hi, coup_lo = halves(coupling[...])
    row = lambda ref, j: ref[j : j + 1, :].astype(jnp.float32)
    for j in middle:
        src[j] = source_terms(
            xs[j - 1], row(sea_ref, j), row(wind, j), row(ice_ref, j), grow_c, diss_c, rate_c, coup_hi, coup_lo
        )
    sea = [row(sea_ref, j) for j in range(lon_dev)]
    step = comps // CHUNKS
    lane = lax.broadcasted_iota(jnp.int32, (step, lats), 1)
    wide = [jnp.broadcast_to(sea[j - 1] * sea[j], (step, lats)) for j in range(1, lon_dev)]
    tall = []
    for j in range(lon_dev):
        own = jnp.broadcast_to(sea[j], (step, lats))
        tall.append(jnp.where(lane == lats - 1, 0.0, own * pltpu.roll(own, lats - 1, 1)))

    def rows(at):
        params = cols[at, :]
        lon_pos = jnp.maximum(params[:, 3:4], 0.0)
        lon_neg = jnp.minimum(params[:, 3:4], 0.0)
        lat_pos = jnp.maximum(params[:, 4:5], 0.0)
        lat_neg = jnp.minimum(params[:, 4:5], 0.0)
        vals = [src[j, at, :] for j in range(lon_dev)]
        flux = [wide[j] * (lon_pos * vals[j] + lon_neg * vals[j + 1]) for j in range(lon_dev - 1)]
        for j in range(lon_dev):
            lat = tall[j] * (lat_pos * vals[j] + lat_neg * pltpu.roll(vals[j], lats - 1, 1))
            value = vals[j] - (lat - pltpu.roll(lat, 1, 1))
            if j > 0:
                value = value + flux[j - 1]
            if j < lon_dev - 1:
                value = value - flux[j]
            outs[j, at, :] = value

    done = []
    for c in range(CHUNKS):
        at = pl.ds(c * step, step)
        rows(at)
        for j in range(lon_dev):
            done.append(pltpu.make_async_copy(outs.at[j, at, :], out.at[at, j, :], out_sems.at[c, j]))
            done[-1].start()
    wait_all(done)


def finish_kernel(
    cap, n_geo, fold, over, part, src_hbm, own_top_hbm, odd_hbm, even_hbm, seam_hbm, halo_hbm, norths_hbm, places_hbm,
    cfl_lon_hbm, cfl_lat_hbm, sea_hbm,
    out, src, acc, acc_top, own_top, msgs, seam, halo, norths, stage, cols, top_rows, places, cfl_lon, cfl_lat, sea_ref,
    in_sems, out_sems,
):
    comps, lon_dev, lats = part.shape
    ends = (0, lon_dev - 1)
    middle = range(1, lon_dev - 1)
    last = pl.ds(lats - 128, 128)
    _, me_geo = position()
    odd = lax.rem(me_geo, 2)
    q = fold[0] // lon_dev
    shift = lax.rem(fold[0], lon_dev)
    slot_0 = source_geo(q, me_geo, n_geo)
    slot_1 = source_geo(q + n_geo - 1, me_geo, n_geo)
    pairs = [
        (places_hbm, places), (cfl_lon_hbm, cfl_lon), (cfl_lat_hbm, cfl_lat), (sea_hbm, sea_ref),
        (seam_hbm.at[slot_0], seam.at[0]), (seam_hbm.at[slot_1], seam.at[1]),
        (odd_hbm, msgs.at[0]), (even_hbm, msgs.at[1]),
        (own_top_hbm, own_top), (src_hbm, src),
        *((part.at[:, j, :], acc.at[i]) for i, j in enumerate(ends)),
        *((part.at[:, j, last], acc_top.at[j - 1]) for j in middle),
    ]
    copies = [pltpu.make_async_copy(here, there, in_sems.at[i]) for i, (here, there) in enumerate(pairs)]
    start_all(copies)
    wait_all(copies[:4])
    cols[...] = columns_of((cfl_lon[...], cfl_lat[...], places[1:2, :], places[0:1, :], places[2:3, :]), stage)

    def spread(i, width):
        at = lax.broadcasted_iota(jnp.int32, (comps, width), 1).astype(jnp.float32)
        return jnp.where(at == cols[:comps, 2 + i : 3 + i], 1.0, 0.0).astype(jnp.bfloat16)

    wait_all(copies[4:8])
    total = None
    for i in range(2):
        hi, lo = halves(msgs[i, :cap, :])
        step = spread(i, cap)
        step = dot(step, hi) + dot(step, lo)
        total = step if total is None else total + step
    halo[...] = total
    lat_w = seam.shape[2]
    top_rows[...] = jnp.zeros(top_rows.shape, jnp.float32)
    for j in range(lon_dev):
        place = shift - j
        block = jnp.where(place >= 0, 0, 1)
        row = jnp.where(place >= 0, place, place + lon_dev)
        top_rows[j : j + 1, :] = seam[block, pl.ds(row, 1), :]
    top_hi, top_lo = halves(top_rows[...])
    top_spread = spread(2, lat_w)
    norths[...] = dot(top_spread, top_hi, (1, 1)) + dot(top_spread, top_lo, (1, 1))

    @pl.when(over[0] > 0)
    def _():
        pltpu.sync_copy(halo_hbm, halo)
        pltpu.sync_copy(norths_hbm, norths)

    sea_odd, sea_even = msgs[0, cap : cap + 1, :], msgs[1, cap : cap + 1, :]
    open_west = jnp.where(odd == 1, sea_even, sea_odd) * sea_ref[0:1, :].astype(jnp.float32)
    open_east = jnp.where(odd == 1, sea_odd, sea_even) * sea_ref[lon_dev - 1 : lon_dev, :].astype(jnp.float32)
    rows_of = comps // CHUNKS
    lane_top = lax.broadcasted_iota(jnp.int32, (rows_of, 128), 1)
    open_top = jnp.zeros((rows_of, 128), jnp.float32)
    for j in range(lon_dev):
        both = top_rows[j : j + 1, lat_w - 1 : lat_w] * sea_ref[j : j + 1, lats - 1 : lats].astype(jnp.float32)
        open_top = jnp.where(lane_top == j, both, open_top)
    wide_west = jnp.broadcast_to(open_west, (rows_of, lats))
    wide_east = jnp.broadcast_to(open_east, (rows_of, lats))
    wait_all(copies[8:])

    def rows(at):
        params = cols[at, :]
        lon_pos = jnp.maximum(params[:, 0:1], 0.0)
        lon_neg = jnp.minimum(params[:, 0:1], 0.0)
        lat_pos = jnp.maximum(params[:, 1:2], 0.0)
        lat_neg = jnp.minimum(params[:, 1:2], 0.0)
        edge = halo[at, :]
        flux_top = open_top * (lat_pos * own_top[at, :] + lat_neg * norths[at, :])
        top_of = lambda j: jnp.where(lane_top == 127, pltpu.roll(flux_top, 127 - j, 1), 0.0)
        west = acc[0, at, :] + wide_west * (lon_pos * edge + lon_neg * src[0, at, :])
        east = acc[1, at, :] - wide_east * (lon_pos * src[1, at, :] + lon_neg * edge)
        for i, value in enumerate((west, east)):
            acc[i, at, : lats - 128] = value[:, : lats - 128]
            acc[i, at, lats - 128 :] = value[:, lats - 128 :] - top_of(ends[i])
        for j in middle:
            acc_top[j - 1, at, :] = acc_top[j - 1, at, :] - top_of(j)

    done = []
    for c in range(CHUNKS):
        at = pl.ds(c * rows_of, rows_of)
        rows(at)
        backs = [(acc.at[i, at, :], out.at[at, j, :]) for i, j in enumerate(ends)]
        backs += [(acc_top.at[j - 1, at, :], out.at[at, j, last]) for j in middle]
        for i, (here, there) in enumerate(backs):
            done.append(pltpu.make_async_copy(here, there, out_sems.at[c, i]))
            done[-1].start()
    wait_all(done)


def source_geo(q, me_geo, n_geo):
    return lax.rem(lax.rem(q, n_geo) - me_geo + n_geo, n_geo)


def reroute_kernel(n_comp, n_geo, fold, got, out, sems):
    me_comp, me_geo = position()
    total = n_comp * n_geo
    lon_dev = got.shape[1]
    copies = []
    for i in range(2):
        q = lax.rem(fold[0] // lon_dev - i + total, total)
        to_geo = source_geo(q, me_geo, n_geo)
        source = lax.rem(q - (me_comp * n_geo + to_geo) + total, total)
        copies.append(pltpu.make_async_copy(got.at[source // n_geo], out.at[to_geo], sems.at[i]))
    for copy in copies:
        copy.start()
    for copy in copies:
        copy.wait()


def seam_of(n_comp, n_geo, top, fold_partner):
    by_comp = lax.all_to_all(top, "comp", 0, 0, tiled=True)
    slots = pl.pallas_call(
        functools.partial(reroute_kernel, n_comp, n_geo),
        out_shape=jax.ShapeDtypeStruct((n_geo, *top.shape[1:]), jnp.float32),
        in_specs=[SMEM, ANY],
        out_specs=ANY,
        scratch_shapes=[pltpu.SemaphoreType.DMA((2,))],
        name="reroute",
    )(fold_partner, by_comp)
    return lax.all_to_all(slots, "geo", 0, 0, tiled=True)


def whole_edges(count, lon_dev, cfl_lon, src, own_top, fold_partner):
    forward = [(d, (d + 1) % count) for d in range(count)]
    west = lax.ppermute(src[1], AXES, forward)
    east = lax.ppermute(src[0], AXES, [(b, a) for a, b in forward])
    halo = jnp.where(cfl_lon[:, None] > 0.0, west, east)
    q, shift = fold_partner[0] // lon_dev, fold_partner[0] % lon_dev
    block = lax.ppermute(own_top[:, :lon_dev].T, AXES, [(d, -d % count) for d in range(count)])
    for bit in range((count - 1).bit_length()):
        moved = lax.ppermute(block, AXES, [(d, (d + (1 << bit)) % count) for d in range(count)])
        block = jnp.where((q >> bit) % 2 == 1, moved, block)
    before = lax.ppermute(block, AXES, [((d + 1) % count, d) for d in range(count)])
    window = jnp.concatenate([before, block], axis=0)
    norths = jnp.take(window, lon_dev + shift - jnp.arange(lon_dev), axis=0).T
    return halo, jnp.pad(norths, ((0, 0), (0, 128 - lon_dev)))


def solution(mesh):
    n_comp, n_geo = mesh.shape["comp"], mesh.shape["geo"]
    count = n_comp * n_geo
    lon = P(AXES, None)
    placed = (P(None, AXES, None), lon, P(), P(), P(), P(), P(), P(), lon, lon, P())
    f32 = jnp.float32
    params = pltpu.CompilerParams(vmem_limit_bytes=LIMIT)
    odd_pairs = [(d, (d + 1) % count if d % 2 else (d - 1) % count) for d in range(count)]
    even_pairs = [(d, d - 1 if d % 2 else d + 1) for d in range(count)]

    def on_device(
        spectrum, wind_speed, growth, dissip, ice_rate, coupling, cfl_lon, cfl_lat, sea_mask, ice_mask, fold_partner
    ):
        comps, lon_dev, lats = spectrum.shape
        wide = -(-comps // 128) * 128
        lat_w = CAP
        size = CAP + 8
        row = lambda v: v.reshape(1, comps)
        shaped = lambda *dims: jax.ShapeDtypeStruct(dims, f32)
        vmem = lambda *dims: pltpu.VMEM(dims, f32)
        dmas = lambda *dims: pltpu.SemaphoreType.DMA(dims)
        mask = pltpu.VMEM((lon_dev, lats), jnp.int32)
        rates = (row(growth), row(dissip), row(ice_rate), row(cfl_lon), row(cfl_lat))
        src, own_top, odd_msg, even_msg, top, places = pl.pallas_call(
            functools.partial(edges_kernel, CAP),
            out_shape=(
                shaped(2, comps, lats), shaped(comps, 128), shaped(size, lats), shaped(size, lats),
                shaped(n_comp, lon_dev, lat_w), shaped(8, comps),
            ),
            in_specs=[ANY] * 10,
            out_specs=(ANY,) * 6,
            scratch_shapes=[
                vmem(2, comps, lats), vmem(lon_dev - 2, comps, 128), vmem(2, comps, lats), vmem(comps, 128),
                vmem(128, wide), vmem(wide, 128), vmem(wide, 128), vmem(comps, comps), vmem(lon_dev, lats),
                *[vmem(1, comps)] * 5, mask, mask, vmem(size, lats), vmem(size, lats), vmem(lon_dev, lat_w),
                vmem(8, comps), dmas(lon_dev), dmas(9), dmas(n_comp + 6),
            ],
            compiler_params=params,
            name="edges",
        )(spectrum, coupling, wind_speed, *rates, sea_mask, ice_mask)
        odd_got = lax.ppermute(odd_msg, AXES, odd_pairs)
        even_got = lax.ppermute(even_msg, AXES, even_pairs)
        seam = seam_of(n_comp, n_geo, top, fold_partner)
        part = pl.pallas_call(
            inner_kernel,
            out_shape=shaped(comps, lon_dev, lats),
            in_specs=[ANY] * 11,
            out_specs=ANY,
            scratch_shapes=[
                vmem(lon_dev - 2, comps, lats), vmem(lon_dev, comps, lats), vmem(lon_dev, comps, lats),
                vmem(128, wide), vmem(wide, 128), vmem(comps, comps), vmem(lon_dev, lats),
                *[vmem(1, comps)] * 5, mask, mask, dmas(lon_dev + 9), dmas(CHUNKS, lon_dev),
            ],
            compiler_params=params,
            cost_estimate=pl.CostEstimate(flops=2_000_000_000, bytes_accessed=8_000_000, transcendentals=500_000),
            name="inner",
        )(spectrum, coupling, src, wind_speed, *rates, sea_mask, ice_mask)
        signs = jnp.stack([cfl_lon, -cfl_lon, -cfl_lat])
        over = jnp.max(jnp.sum((signs > 0.0).astype(jnp.int32), axis=1)) >= CAP
        halo, norths = lax.cond(
            over,
            functools.partial(whole_edges, count, lon_dev),
            lambda *_: (jnp.zeros((comps, lats), f32), jnp.zeros((comps, 128), f32)),
            cfl_lon, src, own_top, fold_partner,
        )
        return pl.pallas_call(
            functools.partial(finish_kernel, CAP, n_geo),
            out_shape=shaped(comps, lon_dev, lats),
            in_specs=[SMEM, SMEM] + [ANY] * 12,
            out_specs=ANY,
            input_output_aliases={2: 0},
            scratch_shapes=[
                vmem(2, comps, lats), vmem(2, comps, lats), vmem(lon_dev - 2, comps, 128), vmem(comps, 128),
                vmem(2, size, lats), vmem(2, lon_dev, lat_w), vmem(comps, lats), vmem(comps, 128), vmem(128, wide),
                vmem(wide, 128), vmem(128, lat_w), vmem(8, comps), vmem(1, comps), vmem(1, comps), mask,
                dmas(lon_dev + 10), dmas(CHUNKS, lon_dev),
            ],
            compiler_params=params,
            name="finish",
        )(
            fold_partner, over.astype(jnp.int32).reshape(1), part, src, own_top, odd_got, even_got, seam, halo, norths,
            places, row(cfl_lon), row(cfl_lat), sea_mask,
        )

    return jax.shard_map(
        on_device, mesh=mesh, in_specs=placed, out_specs=P(None, AXES, None), check_vma=False
    )
```

```python
import functools

import jax
import jax.numpy as jnp
from jax import lax
from jax.experimental import pallas as pl
from jax.experimental.pallas import tpu as pltpu
from jax.sharding import PartitionSpec as P

AXES = ("comp", "geo")
CAP = 256
VMEM = pl.BlockSpec(memory_space=pltpu.VMEM)
SMEM = pl.BlockSpec(memory_space=pltpu.SMEM)
ANY = pl.BlockSpec(memory_space=pl.ANY)
LIMIT = 56 * 1024 * 1024
ROOMY = 24 * 1024 * 1024


CHUNKS = 3


def columns_of(rows, stage):
    stage[...] = jnp.zeros(stage.shape, jnp.float32)
    for i, value in enumerate(rows):
        stage[i : i + 1, : value.shape[1]] = value
    return stage[...].T


def position():
    return lax.axis_index("comp"), lax.axis_index("geo")


def halves(value):
    high = value.astype(jnp.bfloat16)
    return high, (value - high.astype(jnp.float32)).astype(jnp.bfloat16)


def dot(a, b, contract=(1, 0)):
    return lax.dot_general(a, b, (((contract[0],), (contract[1],)), ((), ())), preferred_element_type=jnp.float32)


def start_all(copies):
    for copy in copies:
        copy.start()


def wait_all(copies):
    for copy in copies:
        copy.wait()


def source_terms(x, sea, wind, ice, grow_c, diss_c, rate_c, coup_hi, coup_lo):
    mean = jnp.sum(x, axis=0, keepdims=True) / x.shape[0]
    x_hi, x_lo = halves(x)
    coupled = dot(coup_hi, x_hi) + dot(coup_hi, x_lo) + dot(coup_lo, x_hi)
    net = grow_c * wind - diss_c * (mean / (1.0 + mean)) - rate_c * ice
    return sea * (x * jnp.exp(net) + 0.5 * coupled)


def edges_kernel(
    cap, x_hbm, coup_hbm, wind_hbm, growth_hbm, dissip_hbm, ice_rate_hbm, cfl_lon_hbm, cfl_lat_hbm, sea_hbm, ice_hbm,
    src, own_top, odd_hbm, even_hbm, top_hbm, places_hbm,
    xs, xt, ss, raw_top, stage, cols, top_stage, coupling, wind, growth, dissip, ice_rate, cfl_lon, cfl_lat, sea_ref, ice_ref,
    odd_msg, even_msg, top, places, x_sems, in_sems, out_sems,
):
    comps, lon_dev, lats = x_hbm.shape
    ends = (0, lon_dev - 1)
    last = pl.ds(lats - 128, 128)
    big = [pltpu.make_async_copy(x_hbm.at[:, j, :], xs.at[i], x_sems.at[i]) for i, j in enumerate(ends)]
    slim = [
        pltpu.make_async_copy(x_hbm.at[:, j, last], xt.at[j - 1], x_sems.at[j + 1]) for j in range(1, lon_dev - 1)
    ]
    small = [
        pltpu.make_async_copy(here, there, in_sems.at[i])
        for i, (here, there) in enumerate((
            (cfl_lon_hbm, cfl_lon), (cfl_lat_hbm, cfl_lat), (growth_hbm, growth), (dissip_hbm, dissip),
            (ice_rate_hbm, ice_rate), (coup_hbm, coupling), (wind_hbm, wind), (sea_hbm, sea_ref), (ice_hbm, ice_ref),
        ))
    ]
    start_all((*small[:5], small[5], *small[6:], *big, *slim))
    outs = iter(out_sems.at[i] for i in range(out_sems.shape[0]))
    done = []

    def send(here, there):
        copy = pltpu.make_async_copy(here, there, next(outs))
        copy.start()
        done.append(copy)

    odd = lax.rem(position()[1], 2)
    wait_all(small[:5])
    cols[...] = columns_of((growth[...], dissip[...], ice_rate[...]), stage)
    grow_c, diss_c, rate_c = (cols[:comps, i : i + 1] for i in range(3))
    speed = cfl_lon[...] * jnp.where(odd == 1, 1.0, -1.0)
    pick = lax.broadcasted_iota(jnp.int32, (16, comps), 0)
    flags = jnp.where(pick == 0, speed, jnp.where(pick == 1, -speed, -cfl_lat[...])) > 0.0
    upto = lax.broadcasted_iota(jnp.int32, (comps, comps), 0) <= lax.broadcasted_iota(jnp.int32, (comps, comps), 1)
    ones = jnp.where(upto, 1.0, 0.0).astype(jnp.bfloat16)
    rank = dot(jnp.where(flags, 1.0, 0.0).astype(jnp.bfloat16), ones)
    place = jnp.where(flags, rank - 1.0, -1.0)
    places[...] = place[:8]
    send(places, places_hbm)

    def packing(i, rows):
        at = lax.broadcasted_iota(jnp.int32, (rows, comps), 0).astype(jnp.float32)
        return jnp.where(at == place[i : i + 1, :], 1.0, 0.0).astype(jnp.bfloat16)

    wait_all(small[5:])
    coup_hi, coup_lo = halves(coupling[...])
    terms = functools.partial(
        source_terms, grow_c=grow_c, diss_c=diss_c, rate_c=rate_c, coup_hi=coup_hi, coup_lo=coup_lo
    )
    lane = lax.broadcasted_iota(jnp.int32, (comps, 128), 1)
    lane8 = lax.broadcasted_iota(jnp.int32, (8, 128), 1)

    def gather_last(tile_of, lane):
        total = jnp.zeros(lane.shape, jnp.float32)
        for j in range(lon_dev):
            total = jnp.where(lane == j, pltpu.roll(tile_of(j), j + 1, 1), total)
        return total

    row_top = lambda ref: gather_last(
        lambda j: jnp.broadcast_to(ref[j : j + 1, lats - 128 :].astype(jnp.float32), (8, 128)), lane8
    )[:1]
    row = lambda ref, j: ref[j : j + 1, :].astype(jnp.float32)
    for i, j in enumerate(ends):
        big[i].wait()
        ss[i] = terms(xs[i], row(sea_ref, j), row(wind, j), row(ice_ref, j))
        send(ss.at[i], src.at[i])
    for i, (msg, msg_hbm) in enumerate(((odd_msg, odd_hbm), (even_msg, even_hbm))):
        end = odd if i == 0 else 1 - odd
        hi, lo = halves(ss[end])
        pack = packing(i, cap)
        msg[:cap, :] = dot(pack, hi) + dot(pack, lo)
        sea = jnp.where(end == 1, row(sea_ref, ends[1]), row(sea_ref, ends[0]))
        msg[cap : cap + 8, :] = jnp.broadcast_to(sea, (8, lats))
        send(msg, msg_hbm)
    wait_all(slim)
    raw_top[...] = gather_last(
        lambda j: xs[ends.index(j), :, lats - 128 :] if j in ends else xt[j - 1], lane
    )
    top_stage[:comps, :] = terms(raw_top[...], row_top(sea_ref), row_top(wind), row_top(ice_ref))
    send(top_stage.at[:comps], own_top)
    lat_w = top.shape[1]
    top_hi, top_lo = halves(top_stage[:comps, :])
    top_pack = packing(2, lat_w)
    packed = (dot(top_pack, top_hi) + dot(top_pack, top_lo)).T[:lon_dev]
    sea_top = sea_ref[:, lats - 1 : lats].astype(jnp.float32)
    top[...] = jnp.where(lax.broadcasted_iota(jnp.int32, (lon_dev, lat_w), 1) == lat_w - 1, sea_top, packed)
    for slot in range(top_hbm.shape[0]):
        send(top, top_hbm.at[slot])
    wait_all(done)


def inner_kernel(
    x_hbm, coup_hbm, src_hbm, wind_hbm, growth_hbm, dissip_hbm, ice_rate_hbm, cfl_lon_hbm, cfl_lat_hbm, sea_hbm, ice_hbm,
    out, xs, src, outs, stage, cols, coupling, wind, growth, dissip, ice_rate, cfl_lon, cfl_lat, sea_ref, ice_ref,
    in_sems, out_sems,
):
    comps, lon_dev, lats = x_hbm.shape
    middle = range(1, lon_dev - 1)
    pairs = [
        (cfl_lon_hbm, cfl_lon), (cfl_lat_hbm, cfl_lat), (growth_hbm, growth), (dissip_hbm, dissip),
        (ice_rate_hbm, ice_rate), (coup_hbm, coupling), (wind_hbm, wind), (sea_hbm, sea_ref), (ice_hbm, ice_ref),
        *((x_hbm.at[:, j, :], xs.at[j - 1]) for j in middle),
        (src_hbm.at[0], src.at[0]), (src_hbm.at[1], src.at[lon_dev - 1]),
    ]
    copies = [pltpu.make_async_copy(here, there, in_sems.at[i]) for i, (here, there) in enumerate(pairs)]
    start_all(copies)
    wait_all(copies[:5])
    cols[...] = columns_of((growth[...], dissip[...], ice_rate[...], cfl_lon[...], cfl_lat[...]), stage)
    grow_c, diss_c, rate_c = (cols[:comps, i : i + 1] for i in range(3))
    wait_all(copies[5:])
    coup_hi, coup_lo = halves(coupling[...])
    row = lambda ref, j: ref[j : j + 1, :].astype(jnp.float32)
    for j in middle:
        src[j] = source_terms(
            xs[j - 1], row(sea_ref, j), row(wind, j), row(ice_ref, j), grow_c, diss_c, rate_c, coup_hi, coup_lo
        )
    sea = [row(sea_ref, j) for j in range(lon_dev)]
    step = comps // CHUNKS
    lane = lax.broadcasted_iota(jnp.int32, (step, lats), 1)
    wide = [jnp.broadcast_to(sea[j - 1] * sea[j], (step, lats)) for j in range(1, lon_dev)]
    tall = []
    for j in range(lon_dev):
        own = jnp.broadcast_to(sea[j], (step, lats))
        tall.append(jnp.where(lane == lats - 1, 0.0, own * pltpu.roll(own, lats - 1, 1)))

    def rows(at):
        params = cols[at, :]
        lon_pos = jnp.maximum(params[:, 3:4], 0.0)
        lon_neg = jnp.minimum(params[:, 3:4], 0.0)
        lat_pos = jnp.maximum(params[:, 4:5], 0.0)
        lat_neg = jnp.minimum(params[:, 4:5], 0.0)
        vals = [src[j, at, :] for j in range(lon_dev)]
        flux = [wide[j] * (lon_pos * vals[j] + lon_neg * vals[j + 1]) for j in range(lon_dev - 1)]
        for j in range(lon_dev):
            lat = tall[j] * (lat_pos * vals[j] + lat_neg * pltpu.roll(vals[j], lats - 1, 1))
            value = vals[j] - (lat - pltpu.roll(lat, 1, 1))
            if j > 0:
                value = value + flux[j - 1]
            if j < lon_dev - 1:
                value = value - flux[j]
            outs[j, at, :] = value

    done = []
    for c in range(CHUNKS):
        at = pl.ds(c * step, step)
        rows(at)
        for j in range(lon_dev):
            done.append(pltpu.make_async_copy(outs.at[j, at, :], out.at[at, j, :], out_sems.at[c, j]))
            done[-1].start()
    wait_all(done)


def finish_kernel(
    cap, n_geo, fold, over, part, src_hbm, own_top_hbm, odd_hbm, even_hbm, seam_hbm, halo_hbm, norths_hbm, places_hbm,
    cfl_lon_hbm, cfl_lat_hbm, sea_hbm,
    out, src, acc, acc_top, own_top, msgs, seam, halo, norths, stage, cols, top_rows, places, cfl_lon, cfl_lat, sea_ref,
    in_sems, out_sems,
):
    comps, lon_dev, lats = part.shape
    ends = (0, lon_dev - 1)
    middle = range(1, lon_dev - 1)
    last = pl.ds(lats - 128, 128)
    _, me_geo = position()
    odd = lax.rem(me_geo, 2)
    q = fold[0] // lon_dev
    shift = lax.rem(fold[0], lon_dev)
    slot_0 = source_geo(q, me_geo, n_geo)
    slot_1 = source_geo(q + n_geo - 1, me_geo, n_geo)
    pairs = [
        (places_hbm, places), (cfl_lon_hbm, cfl_lon), (cfl_lat_hbm, cfl_lat), (sea_hbm, sea_ref),
        (seam_hbm.at[slot_0], seam.at[0]), (seam_hbm.at[slot_1], seam.at[1]),
        (odd_hbm, msgs.at[0]), (even_hbm, msgs.at[1]),
        (own_top_hbm, own_top), (src_hbm, src),
        *((part.at[:, j, :], acc.at[i]) for i, j in enumerate(ends)),
        *((part.at[:, j, last], acc_top.at[j - 1]) for j in middle),
    ]
    copies = [pltpu.make_async_copy(here, there, in_sems.at[i]) for i, (here, there) in enumerate(pairs)]
    start_all(copies)
    wait_all(copies[:4])
    cols[...] = columns_of((cfl_lon[...], cfl_lat[...], places[1:2, :], places[0:1, :], places[2:3, :]), stage)

    def spread(i, width):
        at = lax.broadcasted_iota(jnp.int32, (comps, width), 1).astype(jnp.float32)
        return jnp.where(at == cols[:comps, 2 + i : 3 + i], 1.0, 0.0).astype(jnp.bfloat16)

    wait_all(copies[4:8])
    total = None
    for i in range(2):
        hi, lo = halves(msgs[i, :cap, :])
        step = spread(i, cap)
        step = dot(step, hi) + dot(step, lo)
        total = step if total is None else total + step
    halo[...] = total
    lat_w = seam.shape[2]
    top_rows[...] = jnp.zeros(top_rows.shape, jnp.float32)
    for j in range(lon_dev):
        place = shift - j
        block = jnp.where(place >= 0, 0, 1)
        row = jnp.where(place >= 0, place, place + lon_dev)
        top_rows[j : j + 1, :] = seam[block, pl.ds(row, 1), :]
    top_hi, top_lo = halves(top_rows[...])
    top_spread = spread(2, lat_w)
    norths[...] = dot(top_spread, top_hi, (1, 1)) + dot(top_spread, top_lo, (1, 1))

    @pl.when(over[0] > 0)
    def _():
        pltpu.sync_copy(halo_hbm, halo)
        pltpu.sync_copy(norths_hbm, norths)

    sea_odd, sea_even = msgs[0, cap : cap + 1, :], msgs[1, cap : cap + 1, :]
    open_west = jnp.where(odd == 1, sea_even, sea_odd) * sea_ref[0:1, :].astype(jnp.float32)
    open_east = jnp.where(odd == 1, sea_odd, sea_even) * sea_ref[lon_dev - 1 : lon_dev, :].astype(jnp.float32)
    rows_of = comps // CHUNKS
    lane_top = lax.broadcasted_iota(jnp.int32, (rows_of, 128), 1)
    open_top = jnp.zeros((rows_of, 128), jnp.float32)
    for j in range(lon_dev):
        both = top_rows[j : j + 1, lat_w - 1 : lat_w] * sea_ref[j : j + 1, lats - 1 : lats].astype(jnp.float32)
        open_top = jnp.where(lane_top == j, both, open_top)
    wide_west = jnp.broadcast_to(open_west, (rows_of, lats))
    wide_east = jnp.broadcast_to(open_east, (rows_of, lats))
    wait_all(copies[8:])

    def rows(at):
        params = cols[at, :]
        lon_pos = jnp.maximum(params[:, 0:1], 0.0)
        lon_neg = jnp.minimum(params[:, 0:1], 0.0)
        lat_pos = jnp.maximum(params[:, 1:2], 0.0)
        lat_neg = jnp.minimum(params[:, 1:2], 0.0)
        edge = halo[at, :]
        flux_top = open_top * (lat_pos * own_top[at, :] + lat_neg * norths[at, :])
        top_of = lambda j: jnp.where(lane_top == 127, pltpu.roll(flux_top, 127 - j, 1), 0.0)
        west = acc[0, at, :] + wide_west * (lon_pos * edge + lon_neg * src[0, at, :])
        east = acc[1, at, :] - wide_east * (lon_pos * src[1, at, :] + lon_neg * edge)
        for i, value in enumerate((west, east)):
            acc[i, at, : lats - 128] = value[:, : lats - 128]
            acc[i, at, lats - 128 :] = value[:, lats - 128 :] - top_of(ends[i])
        for j in middle:
            acc_top[j - 1, at, :] = acc_top[j - 1, at, :] - top_of(j)

    done = []
    for c in range(CHUNKS):
        at = pl.ds(c * rows_of, rows_of)
        rows(at)
        backs = [(acc.at[i, at, :], out.at[at, j, :]) for i, j in enumerate(ends)]
        backs += [(acc_top.at[j - 1, at, :], out.at[at, j, last]) for j in middle]
        for i, (here, there) in enumerate(backs):
            done.append(pltpu.make_async_copy(here, there, out_sems.at[c, i]))
            done[-1].start()
    wait_all(done)


def source_geo(q, me_geo, n_geo):
    return lax.rem(lax.rem(q, n_geo) - me_geo + n_geo, n_geo)


def reroute_kernel(n_comp, n_geo, fold, got, out, sems):
    me_comp, me_geo = position()
    total = n_comp * n_geo
    lon_dev = got.shape[1]
    copies = []
    for i in range(2):
        q = lax.rem(fold[0] // lon_dev - i + total, total)
        to_geo = source_geo(q, me_geo, n_geo)
        source = lax.rem(q - (me_comp * n_geo + to_geo) + total, total)
        copies.append(pltpu.make_async_copy(got.at[source // n_geo], out.at[to_geo], sems.at[i]))
    for copy in copies:
        copy.start()
    for copy in copies:
        copy.wait()


def seam_of(n_comp, n_geo, top, fold_partner):
    by_comp = lax.all_to_all(top, "comp", 0, 0, tiled=True)
    slots = pl.pallas_call(
        functools.partial(reroute_kernel, n_comp, n_geo),
        out_shape=jax.ShapeDtypeStruct((n_geo, *top.shape[1:]), jnp.float32),
        in_specs=[SMEM, ANY],
        out_specs=ANY,
        scratch_shapes=[pltpu.SemaphoreType.DMA((2,))],
        compiler_params=pltpu.CompilerParams(vmem_limit_bytes=1024 * 1024),
        name="reroute",
    )(fold_partner, by_comp)
    return lax.all_to_all(slots, "geo", 0, 0, tiled=True)


def whole_edges(count, lon_dev, cfl_lon, src, own_top, fold_partner):
    forward = [(d, (d + 1) % count) for d in range(count)]
    west = lax.ppermute(src[1], AXES, forward)
    east = lax.ppermute(src[0], AXES, [(b, a) for a, b in forward])
    halo = jnp.where(cfl_lon[:, None] > 0.0, west, east)
    q, shift = fold_partner[0] // lon_dev, fold_partner[0] % lon_dev
    block = lax.ppermute(own_top[:, :lon_dev].T, AXES, [(d, -d % count) for d in range(count)])
    for bit in range((count - 1).bit_length()):
        moved = lax.ppermute(block, AXES, [(d, (d + (1 << bit)) % count) for d in range(count)])
        block = jnp.where((q >> bit) % 2 == 1, moved, block)
    before = lax.ppermute(block, AXES, [((d + 1) % count, d) for d in range(count)])
    window = jnp.concatenate([before, block], axis=0)
    norths = jnp.take(window, lon_dev + shift - jnp.arange(lon_dev), axis=0).T
    return halo, jnp.pad(norths, ((0, 0), (0, 128 - lon_dev)))


def solution(mesh):
    n_comp, n_geo = mesh.shape["comp"], mesh.shape["geo"]
    count = n_comp * n_geo
    lon = P(AXES, None)
    placed = (P(None, AXES, None), lon, P(), P(), P(), P(), P(), P(), lon, lon, P())
    f32 = jnp.float32
    params = pltpu.CompilerParams(vmem_limit_bytes=LIMIT)
    odd_pairs = [(d, (d + 1) % count if d % 2 else (d - 1) % count) for d in range(count)]
    even_pairs = [(d, d - 1 if d % 2 else d + 1) for d in range(count)]

    def on_device(
        spectrum, wind_speed, growth, dissip, ice_rate, coupling, cfl_lon, cfl_lat, sea_mask, ice_mask, fold_partner
    ):
        comps, lon_dev, lats = spectrum.shape
        wide = -(-comps // 128) * 128
        lat_w = CAP
        size = CAP + 8
        row = lambda v: v.reshape(1, comps)
        shaped = lambda *dims: jax.ShapeDtypeStruct(dims, f32)
        vmem = lambda *dims: pltpu.VMEM(dims, f32)
        dmas = lambda *dims: pltpu.SemaphoreType.DMA(dims)
        mask = pltpu.VMEM((lon_dev, lats), jnp.int32)
        rates = (row(growth), row(dissip), row(ice_rate), row(cfl_lon), row(cfl_lat))
        src, own_top, odd_msg, even_msg, top, places = pl.pallas_call(
            functools.partial(edges_kernel, CAP),
            out_shape=(
                shaped(2, comps, lats), shaped(comps, 128), shaped(size, lats), shaped(size, lats),
                shaped(n_comp, lon_dev, lat_w), shaped(8, comps),
            ),
            in_specs=[ANY] * 10,
            out_specs=(ANY,) * 6,
            scratch_shapes=[
                vmem(2, comps, lats), vmem(lon_dev - 2, comps, 128), vmem(2, comps, lats), vmem(comps, 128),
                vmem(128, wide), vmem(wide, 128), vmem(wide, 128), vmem(comps, comps), vmem(lon_dev, lats),
                *[vmem(1, comps)] * 5, mask, mask, vmem(size, lats), vmem(size, lats), vmem(lon_dev, lat_w),
                vmem(8, comps), dmas(lon_dev), dmas(9), dmas(n_comp + 6),
            ],
            compiler_params=params,
            name="edges",
        )(spectrum, coupling, wind_speed, *rates, sea_mask, ice_mask)
        odd_got = lax.ppermute(odd_msg, AXES, odd_pairs)
        even_got = lax.ppermute(even_msg, AXES, even_pairs)
        seam = seam_of(n_comp, n_geo, top, fold_partner)
        part = pl.pallas_call(
            inner_kernel,
            out_shape=shaped(comps, lon_dev, lats),
            in_specs=[ANY] * 11,
            out_specs=ANY,
            scratch_shapes=[
                vmem(lon_dev - 2, comps, lats), vmem(lon_dev, comps, lats), vmem(lon_dev, comps, lats),
                vmem(128, wide), vmem(wide, 128), vmem(comps, comps), vmem(lon_dev, lats),
                *[vmem(1, comps)] * 5, mask, mask, dmas(lon_dev + 9), dmas(CHUNKS, lon_dev),
            ],
            compiler_params=params,
            cost_estimate=pl.CostEstimate(flops=2_000_000_000, bytes_accessed=8_000_000, transcendentals=500_000),
            name="inner",
        )(spectrum, coupling, src, wind_speed, *rates, sea_mask, ice_mask)
        signs = jnp.stack([cfl_lon, -cfl_lon, -cfl_lat])
        over = jnp.max(jnp.sum((signs > 0.0).astype(jnp.int32), axis=1)) >= CAP
        halo, norths = lax.cond(
            over,
            functools.partial(whole_edges, count, lon_dev),
            lambda *_: (jnp.zeros((comps, lats), f32), jnp.zeros((comps, 128), f32)),
            cfl_lon, src, own_top, fold_partner,
        )
        return pl.pallas_call(
            functools.partial(finish_kernel, CAP, n_geo),
            out_shape=shaped(comps, lon_dev, lats),
            in_specs=[SMEM, SMEM] + [ANY] * 12,
            out_specs=ANY,
            input_output_aliases={2: 0},
            scratch_shapes=[
                vmem(2, comps, lats), vmem(2, comps, lats), vmem(lon_dev - 2, comps, 128), vmem(comps, 128),
                vmem(2, size, lats), vmem(2, lon_dev, lat_w), vmem(comps, lats), vmem(comps, 128), vmem(128, wide),
                vmem(wide, 128), vmem(128, lat_w), vmem(8, comps), vmem(1, comps), vmem(1, comps), mask,
                dmas(lon_dev + 10), dmas(CHUNKS, lon_dev),
            ],
            compiler_params=pltpu.CompilerParams(vmem_limit_bytes=ROOMY),
            name="finish",
        )(
            fold_partner, over.astype(jnp.int32).reshape(1), part, src, own_top, odd_got, even_got, seam, halo, norths,
            places, row(cfl_lon), row(cfl_lat), sea_mask,
        )

    return jax.shard_map(
        on_device, mesh=mesh, in_specs=placed, out_specs=P(None, AXES, None), check_vma=False
    )
```

```python
import functools

import jax
import jax.numpy as jnp
from jax import lax
from jax.experimental import pallas as pl
from jax.experimental.pallas import tpu as pltpu
from jax.sharding import PartitionSpec as P

AXES = ("comp", "geo")
CAP = 256
VMEM = pl.BlockSpec(memory_space=pltpu.VMEM)
SMEM = pl.BlockSpec(memory_space=pltpu.SMEM)
ANY = pl.BlockSpec(memory_space=pl.ANY)
LIMIT = 56 * 1024 * 1024
ROOMY = 24 * 1024 * 1024


CHUNKS = 3
PAD = 1


def columns_of(rows, stage):
    stage[...] = jnp.zeros(stage.shape, jnp.float32)
    for i, value in enumerate(rows):
        stage[i : i + 1, : value.shape[1]] = value
    return stage[...].T


def position():
    return lax.axis_index("comp"), lax.axis_index("geo")


def halves(value):
    high = value.astype(jnp.bfloat16)
    return high, (value - high.astype(jnp.float32)).astype(jnp.bfloat16)


def dot(a, b, contract=(1, 0)):
    return lax.dot_general(a, b, (((contract[0],), (contract[1],)), ((), ())), preferred_element_type=jnp.float32)


def start_all(copies):
    for copy in copies:
        copy.start()


def wait_all(copies):
    for copy in copies:
        copy.wait()


def source_terms(x, sea, wind, ice, grow_c, diss_c, rate_c, coup_hi, coup_lo):
    mean = jnp.sum(x, axis=0, keepdims=True) / x.shape[0]
    x_hi, x_lo = halves(x)
    coupled = dot(coup_hi, x_hi) + dot(coup_hi, x_lo) + dot(coup_lo, x_hi)
    net = grow_c * wind - diss_c * (mean / (1.0 + mean)) - rate_c * ice
    return sea * (x * jnp.exp(net) + 0.5 * coupled)


def edges_kernel(
    cap, x_hbm, coup_hbm, wind_hbm, growth_hbm, dissip_hbm, ice_rate_hbm, cfl_lon_hbm, cfl_lat_hbm, sea_hbm, ice_hbm,
    src, own_top, odd_hbm, even_hbm, top_hbm, places_hbm,
    xs, xt, ss, raw_top, stage, cols, top_stage, coupling, wind, growth, dissip, ice_rate, cfl_lon, cfl_lat, sea_ref, ice_ref,
    odd_msg, even_msg, top, places, x_sems, in_sems, out_sems,
):
    comps, lon_dev, lats = x_hbm.shape
    ends = (0, lon_dev - 1)
    last = pl.ds(lats - 128, 128)
    big = [pltpu.make_async_copy(x_hbm.at[:, j, :], xs.at[i], x_sems.at[i]) for i, j in enumerate(ends)]
    slim = [
        pltpu.make_async_copy(x_hbm.at[:, j, last], xt.at[j - 1], x_sems.at[j + 1]) for j in range(1, lon_dev - 1)
    ]
    small = [
        pltpu.make_async_copy(here, there, in_sems.at[i])
        for i, (here, there) in enumerate((
            (cfl_lon_hbm, cfl_lon), (cfl_lat_hbm, cfl_lat), (growth_hbm, growth), (dissip_hbm, dissip),
            (ice_rate_hbm, ice_rate), (coup_hbm, coupling), (wind_hbm, wind), (sea_hbm, sea_ref), (ice_hbm, ice_ref),
        ))
    ]
    start_all((*small[:5], small[5], *small[6:], *big, *slim))
    outs = iter(out_sems.at[i] for i in range(out_sems.shape[0]))
    done = []

    def send(here, there):
        copy = pltpu.make_async_copy(here, there, next(outs))
        copy.start()
        done.append(copy)

    odd = lax.rem(position()[1], 2)
    wait_all(small[:5])
    cols[...] = columns_of((growth[...], dissip[...], ice_rate[...]), stage)
    grow_c, diss_c, rate_c = (cols[:comps, i : i + 1] for i in range(3))
    speed = cfl_lon[...] * jnp.where(odd == 1, 1.0, -1.0)
    pick = lax.broadcasted_iota(jnp.int32, (16, comps), 0)
    flags = jnp.where(pick == 0, speed, jnp.where(pick == 1, -speed, -cfl_lat[...])) > 0.0
    upto = lax.broadcasted_iota(jnp.int32, (comps, comps), 0) <= lax.broadcasted_iota(jnp.int32, (comps, comps), 1)
    ones = jnp.where(upto, 1.0, 0.0).astype(jnp.bfloat16)
    rank = dot(jnp.where(flags, 1.0, 0.0).astype(jnp.bfloat16), ones)
    place = jnp.where(flags, rank - 1.0, -1.0)
    places[...] = place[:8]
    send(places, places_hbm)

    def packing(i, rows):
        at = lax.broadcasted_iota(jnp.int32, (rows, comps), 0).astype(jnp.float32)
        return jnp.where(at == place[i : i + 1, :], 1.0, 0.0).astype(jnp.bfloat16)

    wait_all(small[5:])
    coup_hi, coup_lo = halves(coupling[...])
    terms = functools.partial(
        source_terms, grow_c=grow_c, diss_c=diss_c, rate_c=rate_c, coup_hi=coup_hi, coup_lo=coup_lo
    )
    lane = lax.broadcasted_iota(jnp.int32, (comps, 128), 1)
    lane8 = lax.broadcasted_iota(jnp.int32, (8, 128), 1)

    def gather_last(tile_of, lane):
        total = jnp.zeros(lane.shape, jnp.float32)
        for j in range(lon_dev):
            total = jnp.where(lane == j, pltpu.roll(tile_of(j), j + 1, 1), total)
        return total

    row_top = lambda ref: gather_last(
        lambda j: jnp.broadcast_to(ref[j : j + 1, lats - 128 :].astype(jnp.float32), (8, 128)), lane8
    )[:1]
    row = lambda ref, j: ref[j : j + 1, :].astype(jnp.float32)
    for i, j in enumerate(ends):
        big[i].wait()
        ss[i] = terms(xs[i], row(sea_ref, j), row(wind, j), row(ice_ref, j))
        send(ss.at[i], src.at[i])
    for i, (msg, msg_hbm) in enumerate(((odd_msg, odd_hbm), (even_msg, even_hbm))):
        end = odd if i == 0 else 1 - odd
        hi, lo = halves(ss[end])
        pack = packing(i, cap)
        msg[:cap, :] = dot(pack, hi) + dot(pack, lo)
        sea = jnp.where(end == 1, row(sea_ref, ends[1]), row(sea_ref, ends[0]))
        msg[cap : cap + 8, :] = jnp.broadcast_to(sea, (8, lats))
        send(msg, msg_hbm)
    wait_all(slim)
    raw_top[...] = gather_last(
        lambda j: xs[ends.index(j), :, lats - 128 :] if j in ends else xt[j - 1], lane
    )
    top_stage[:comps, :] = terms(raw_top[...], row_top(sea_ref), row_top(wind), row_top(ice_ref))
    send(top_stage.at[:comps], own_top)
    lat_w = top.shape[1]
    top_hi, top_lo = halves(top_stage[:comps, :])
    top_pack = packing(2, lat_w)
    packed = (dot(top_pack, top_hi) + dot(top_pack, top_lo)).T[:lon_dev]
    sea_top = sea_ref[:, lats - 1 : lats].astype(jnp.float32)
    top[...] = jnp.where(lax.broadcasted_iota(jnp.int32, (lon_dev, lat_w), 1) == lat_w - 1, sea_top, packed)
    for slot in range(top_hbm.shape[0]):
        send(top, top_hbm.at[slot])
    wait_all(done)


def inner_kernel(
    x_hbm, coup_hbm, src_hbm, wind_hbm, growth_hbm, dissip_hbm, ice_rate_hbm, cfl_lon_hbm, cfl_lat_hbm, sea_hbm, ice_hbm,
    out, xs, src, outs, stage, cols, coupling, wind, growth, dissip, ice_rate, cfl_lon, cfl_lat, sea_ref, ice_ref,
    in_sems, out_sems,
):
    comps, lon_dev, lats = x_hbm.shape
    middle = range(1, lon_dev - 1)
    pairs = [
        (cfl_lon_hbm, cfl_lon), (cfl_lat_hbm, cfl_lat), (growth_hbm, growth), (dissip_hbm, dissip),
        (ice_rate_hbm, ice_rate), (coup_hbm, coupling), (wind_hbm, wind), (sea_hbm, sea_ref), (ice_hbm, ice_ref),
        *((x_hbm.at[:, j, :], xs.at[j - 1]) for j in middle),
        (src_hbm.at[0], src.at[0]), (src_hbm.at[1], src.at[lon_dev - 1]),
    ]
    copies = [pltpu.make_async_copy(here, there, in_sems.at[i]) for i, (here, there) in enumerate(pairs)]
    start_all(copies)
    wait_all(copies[:5])
    cols[...] = columns_of((growth[...], dissip[...], ice_rate[...], cfl_lon[...], cfl_lat[...]), stage)
    grow_c, diss_c, rate_c = (cols[:comps, i : i + 1] for i in range(3))
    wait_all(copies[5:])
    coup_hi, coup_lo = halves(coupling[...])
    row = lambda ref, j: ref[j : j + 1, :].astype(jnp.float32)
    for j in middle:
        src[j] = source_terms(
            xs[j - 1], row(sea_ref, j), row(wind, j), row(ice_ref, j), grow_c, diss_c, rate_c, coup_hi, coup_lo
        )
    sea = [row(sea_ref, j) for j in range(lon_dev)]
    step = comps // CHUNKS
    lane = lax.broadcasted_iota(jnp.int32, (step, lats), 1)
    wide = [jnp.broadcast_to(sea[j - 1] * sea[j], (step, lats)) for j in range(1, lon_dev)]
    tall = []
    for j in range(lon_dev):
        own = jnp.broadcast_to(sea[j], (step, lats))
        tall.append(jnp.where(lane == lats - 1, 0.0, own * pltpu.roll(own, lats - 1, 1)))

    def rows(at):
        params = cols[at, :]
        lon_pos = jnp.maximum(params[:, 3:4], 0.0)
        lon_neg = jnp.minimum(params[:, 3:4], 0.0)
        lat_pos = jnp.maximum(params[:, 4:5], 0.0)
        lat_neg = jnp.minimum(params[:, 4:5], 0.0)
        vals = [src[j, at, :] for j in range(lon_dev)]
        flux = [wide[j] * (lon_pos * vals[j] + lon_neg * vals[j + 1]) for j in range(lon_dev - 1)]
        for j in range(lon_dev):
            lat = tall[j] * (lat_pos * vals[j] + lat_neg * pltpu.roll(vals[j], lats - 1, 1))
            value = vals[j] - (lat - pltpu.roll(lat, 1, 1))
            if j > 0:
                value = value + flux[j - 1]
            if j < lon_dev - 1:
                value = value - flux[j]
            outs[j, at, :] = value

    done = []
    for c in range(CHUNKS):
        at = pl.ds(c * step, step)
        rows(at)
        for j in range(lon_dev):
            done.append(pltpu.make_async_copy(outs.at[j, at, :], out.at[at, j, :], out_sems.at[c, j]))
            done[-1].start()
    wait_all(done)


def finish_kernel(
    cap, n_comp, n_geo, fold, over, part, src_hbm, own_top_hbm, odd_hbm, even_hbm, seam_hbm, halo_hbm, norths_hbm, places_hbm,
    cfl_lon_hbm, cfl_lat_hbm, sea_hbm,
    out, src, acc, acc_top, own_top, msgs, seam, halo, norths, stage, cols, top_rows, places, cfl_lon, cfl_lat, sea_ref,
    in_sems, out_sems,
):
    comps, lon_dev, lats = part.shape
    ends = (0, lon_dev - 1)
    middle = range(1, lon_dev - 1)
    last = pl.ds(lats - 128, 128)
    me_comp, me_geo = position()
    odd = lax.rem(me_geo, 2)
    q = fold[0] // lon_dev
    shift = lax.rem(fold[0], lon_dev)

    def slot_of(q):
        source = lax.rem(q - (me_comp * n_geo + me_geo) + 2 * n_comp * n_geo, n_comp * n_geo)
        return source // n_geo * 2 + lax.rem(source, 2)

    slot_0, slot_1 = slot_of(q), slot_of(q - 1)
    pairs = [
        (places_hbm, places), (cfl_lon_hbm, cfl_lon), (cfl_lat_hbm, cfl_lat), (sea_hbm, sea_ref),
        (seam_hbm.at[slot_0], seam.at[0]), (seam_hbm.at[slot_1], seam.at[1]),
        (odd_hbm, msgs.at[0]), (even_hbm, msgs.at[1]),
        (own_top_hbm, own_top), (src_hbm, src),
        *((part.at[:, j, :], acc.at[i]) for i, j in enumerate(ends)),
        *((part.at[:, j, last], acc_top.at[j - 1]) for j in middle),
    ]
    copies = [pltpu.make_async_copy(here, there, in_sems.at[i]) for i, (here, there) in enumerate(pairs)]
    start_all(copies)
    wait_all(copies[:4])
    cols[...] = columns_of((cfl_lon[...], cfl_lat[...], places[1:2, :], places[0:1, :], places[2:3, :]), stage)

    def spread(i, width):
        at = lax.broadcasted_iota(jnp.int32, (comps, width), 1).astype(jnp.float32)
        return jnp.where(at == cols[:comps, 2 + i : 3 + i], 1.0, 0.0).astype(jnp.bfloat16)

    wait_all(copies[4:8])
    total = None
    for i in range(2):
        hi, lo = halves(msgs[i, :cap, :])
        step = spread(i, cap)
        step = dot(step, hi) + dot(step, lo)
        total = step if total is None else total + step
    halo[...] = total
    lat_w = seam.shape[2]
    top_rows[...] = jnp.zeros(top_rows.shape, jnp.float32)
    for j in range(lon_dev):
        place = shift - j
        block = jnp.where(place >= 0, 0, 1)
        row = jnp.where(place >= 0, place, place + lon_dev)
        top_rows[j : j + 1, :] = seam[block, pl.ds(row, 1), :]
    top_hi, top_lo = halves(top_rows[...])
    top_spread = spread(2, lat_w)
    norths[...] = dot(top_spread, top_hi, (1, 1)) + dot(top_spread, top_lo, (1, 1))

    @pl.when(over[0] > 0)
    def _():
        pltpu.sync_copy(halo_hbm, halo)
        pltpu.sync_copy(norths_hbm, norths)

    sea_odd, sea_even = msgs[0, cap : cap + 1, :], msgs[1, cap : cap + 1, :]
    open_west = jnp.where(odd == 1, sea_even, sea_odd) * sea_ref[0:1, :].astype(jnp.float32)
    open_east = jnp.where(odd == 1, sea_odd, sea_even) * sea_ref[lon_dev - 1 : lon_dev, :].astype(jnp.float32)
    rows_of = comps // CHUNKS
    lane_top = lax.broadcasted_iota(jnp.int32, (rows_of, 128), 1)
    open_top = jnp.zeros((rows_of, 128), jnp.float32)
    for j in range(lon_dev):
        both = top_rows[j : j + 1, lat_w - 1 : lat_w] * sea_ref[j : j + 1, lats - 1 : lats].astype(jnp.float32)
        open_top = jnp.where(lane_top == j, both, open_top)
    wide_west = jnp.broadcast_to(open_west, (rows_of, lats))
    wide_east = jnp.broadcast_to(open_east, (rows_of, lats))
    wait_all(copies[8:])

    def rows(at):
        params = cols[at, :]
        lon_pos = jnp.maximum(params[:, 0:1], 0.0)
        lon_neg = jnp.minimum(params[:, 0:1], 0.0)
        lat_pos = jnp.maximum(params[:, 1:2], 0.0)
        lat_neg = jnp.minimum(params[:, 1:2], 0.0)
        edge = halo[at, :]
        flux_top = open_top * (lat_pos * own_top[at, :] + lat_neg * norths[at, :])
        top_of = lambda j: jnp.where(lane_top == 127, pltpu.roll(flux_top, 127 - j, 1), 0.0)
        west = acc[0, at, :] + wide_west * (lon_pos * edge + lon_neg * src[0, at, :])
        east = acc[1, at, :] - wide_east * (lon_pos * src[1, at, :] + lon_neg * edge)
        for i, value in enumerate((west, east)):
            acc[i, at, : lats - 128] = value[:, : lats - 128]
            acc[i, at, lats - 128 :] = value[:, lats - 128 :] - top_of(ends[i])
        for j in middle:
            acc_top[j - 1, at, :] = acc_top[j - 1, at, :] - top_of(j)

    done = []
    for c in range(CHUNKS):
        at = pl.ds(c * rows_of, rows_of)
        rows(at)
        backs = [(acc.at[i, at, :], out.at[at, j, :]) for i, j in enumerate(ends)]
        backs += [(acc_top.at[j - 1, at, :], out.at[at, j, last]) for j in middle]
        for i, (here, there) in enumerate(backs):
            done.append(pltpu.make_async_copy(here, there, out_sems.at[c, i]))
            done[-1].start()
    wait_all(done)


def reroute_kernel(n_comp, n_geo, fold, got, out, sems):
    me_comp, me_geo = position()
    half = n_geo // 2
    total = n_comp * n_geo
    lon_dev = got.shape[1]
    me_low, me_high = lax.rem(me_geo, 2), me_geo // 2
    copies = []
    for i in range(2):
        q = lax.rem(fold[0] // lon_dev - i + total, total)
        q_low, q_high, q_comp = lax.rem(q, 2), lax.rem(q // 2, half), q // n_geo
        to_low = lax.rem(q_low - me_low + 2, 2)
        high = q_high - me_high - (to_low > q_low).astype(jnp.int32)
        to_comp = lax.rem(q_comp - me_comp - (high < 0).astype(jnp.int32) + 2 * n_comp, n_comp)
        copies.append(pltpu.make_async_copy(got.at[lax.rem(high + n_geo, half)], out.at[to_comp * 2 + to_low], sems.at[i]))
    start_all(copies)
    wait_all(copies)


def seam_of(n_comp, n_geo, top, fold_partner):
    half = n_geo // 2
    flat = lambda c, high, low: c * n_geo + 2 * high + low
    far = [[flat(c, k, low) for k in range(half)] for c in range(n_comp) for low in range(2)]
    near = [[flat(c, k, low) for c in range(n_comp) for low in range(2)] for k in range(half)]
    by_geo = lax.all_to_all(top, AXES, 0, 0, tiled=True, axis_index_groups=far)
    slots = pl.pallas_call(
        functools.partial(reroute_kernel, n_comp, n_geo),
        out_shape=jax.ShapeDtypeStruct((2 * n_comp, PAD * top.shape[1], top.shape[2]), jnp.float32),
        in_specs=[SMEM, ANY],
        out_specs=ANY,
        scratch_shapes=[pltpu.SemaphoreType.DMA((2,))],
        compiler_params=pltpu.CompilerParams(vmem_limit_bytes=1024 * 1024),
        name="reroute",
    )(fold_partner, by_geo)
    return lax.all_to_all(slots, AXES, 0, 0, tiled=True, axis_index_groups=near)


def whole_edges(count, lon_dev, cfl_lon, src, own_top, fold_partner):
    forward = [(d, (d + 1) % count) for d in range(count)]
    west = lax.ppermute(src[1], AXES, forward)
    east = lax.ppermute(src[0], AXES, [(b, a) for a, b in forward])
    halo = jnp.where(cfl_lon[:, None] > 0.0, west, east)
    q, shift = fold_partner[0] // lon_dev, fold_partner[0] % lon_dev
    block = lax.ppermute(own_top[:, :lon_dev].T, AXES, [(d, -d % count) for d in range(count)])
    for bit in range((count - 1).bit_length()):
        moved = lax.ppermute(block, AXES, [(d, (d + (1 << bit)) % count) for d in range(count)])
        block = jnp.where((q >> bit) % 2 == 1, moved, block)
    before = lax.ppermute(block, AXES, [((d + 1) % count, d) for d in range(count)])
    window = jnp.concatenate([before, block], axis=0)
    norths = jnp.take(window, lon_dev + shift - jnp.arange(lon_dev), axis=0).T
    return halo, jnp.pad(norths, ((0, 0), (0, 128 - lon_dev)))


def solution(mesh):
    n_comp, n_geo = mesh.shape["comp"], mesh.shape["geo"]
    count = n_comp * n_geo
    lon = P(AXES, None)
    placed = (P(None, AXES, None), lon, P(), P(), P(), P(), P(), P(), lon, lon, P())
    f32 = jnp.float32
    params = pltpu.CompilerParams(vmem_limit_bytes=LIMIT)
    odd_pairs = [(d, (d + 1) % count if d % 2 else (d - 1) % count) for d in range(count)]
    even_pairs = [(d, d - 1 if d % 2 else d + 1) for d in range(count)]

    def on_device(
        spectrum, wind_speed, growth, dissip, ice_rate, coupling, cfl_lon, cfl_lat, sea_mask, ice_mask, fold_partner
    ):
        comps, lon_dev, lats = spectrum.shape
        wide = -(-comps // 128) * 128
        lat_w = CAP
        size = CAP + 8
        row = lambda v: v.reshape(1, comps)
        shaped = lambda *dims: jax.ShapeDtypeStruct(dims, f32)
        vmem = lambda *dims: pltpu.VMEM(dims, f32)
        dmas = lambda *dims: pltpu.SemaphoreType.DMA(dims)
        mask = pltpu.VMEM((lon_dev, lats), jnp.int32)
        rates = (row(growth), row(dissip), row(ice_rate), row(cfl_lon), row(cfl_lat))
        src, own_top, odd_msg, even_msg, top, places = pl.pallas_call(
            functools.partial(edges_kernel, CAP),
            out_shape=(
                shaped(2, comps, lats), shaped(comps, 128), shaped(size, lats), shaped(size, lats),
                shaped(n_geo // 2, lon_dev, lat_w), shaped(8, comps),
            ),
            in_specs=[ANY] * 10,
            out_specs=(ANY,) * 6,
            scratch_shapes=[
                vmem(2, comps, lats), vmem(lon_dev - 2, comps, 128), vmem(2, comps, lats), vmem(comps, 128),
                vmem(128, wide), vmem(wide, 128), vmem(wide, 128), vmem(comps, comps), vmem(lon_dev, lats),
                *[vmem(1, comps)] * 5, mask, mask, vmem(size, lats), vmem(size, lats), vmem(lon_dev, lat_w),
                vmem(8, comps), dmas(lon_dev), dmas(9), dmas(n_geo // 2 + 6),
            ],
            compiler_params=params,
            name="edges",
        )(spectrum, coupling, wind_speed, *rates, sea_mask, ice_mask)
        odd_got = lax.ppermute(odd_msg, AXES, odd_pairs)
        even_got = lax.ppermute(even_msg, AXES, even_pairs)
        seam = seam_of(n_comp, n_geo, top, fold_partner)
        part = pl.pallas_call(
            inner_kernel,
            out_shape=shaped(comps, lon_dev, lats),
            in_specs=[ANY] * 11,
            out_specs=ANY,
            scratch_shapes=[
                vmem(lon_dev - 2, comps, lats), vmem(lon_dev, comps, lats), vmem(lon_dev, comps, lats),
                vmem(128, wide), vmem(wide, 128), vmem(comps, comps), vmem(lon_dev, lats),
                *[vmem(1, comps)] * 5, mask, mask, dmas(lon_dev + 9), dmas(CHUNKS, lon_dev),
            ],
            compiler_params=params,
            cost_estimate=pl.CostEstimate(flops=2_000_000_000, bytes_accessed=8_000_000, transcendentals=500_000),
            name="inner",
        )(spectrum, coupling, src, wind_speed, *rates, sea_mask, ice_mask)
        signs = jnp.stack([cfl_lon, -cfl_lon, -cfl_lat])
        over = jnp.max(jnp.sum((signs > 0.0).astype(jnp.int32), axis=1)) >= CAP
        halo, norths = lax.cond(
            over,
            functools.partial(whole_edges, count, lon_dev),
            lambda *_: (jnp.zeros((comps, lats), f32), jnp.zeros((comps, 128), f32)),
            cfl_lon, src, own_top, fold_partner,
        )
        return pl.pallas_call(
            functools.partial(finish_kernel, CAP, n_comp, n_geo),
            out_shape=shaped(comps, lon_dev, lats),
            in_specs=[SMEM, SMEM] + [ANY] * 12,
            out_specs=ANY,
            input_output_aliases={2: 0},
            scratch_shapes=[
                vmem(2, comps, lats), vmem(2, comps, lats), vmem(lon_dev - 2, comps, 128), vmem(comps, 128),
                vmem(2, size, lats), vmem(2, lon_dev, lat_w), vmem(comps, lats), vmem(comps, 128), vmem(128, wide),
                vmem(wide, 128), vmem(128, lat_w), vmem(8, comps), vmem(1, comps), vmem(1, comps), mask,
                dmas(lon_dev + 10), dmas(CHUNKS, lon_dev),
            ],
            compiler_params=pltpu.CompilerParams(vmem_limit_bytes=ROOMY),
            name="finish",
        )(
            fold_partner, over.astype(jnp.int32).reshape(1), part, src, own_top, odd_got, even_got, seam, halo, norths,
            places, row(cfl_lon), row(cfl_lat), sea_mask,
        )

    return jax.shard_map(
        on_device, mesh=mesh, in_specs=placed, out_specs=P(None, AXES, None), check_vma=False
    )
```

```python
import functools

import jax
import jax.numpy as jnp
from jax import lax
from jax.experimental import pallas as pl
from jax.experimental.pallas import tpu as pltpu
from jax.sharding import PartitionSpec as P

AXES = ("comp", "geo")
CAP = 256
VMEM = pl.BlockSpec(memory_space=pltpu.VMEM)
SMEM = pl.BlockSpec(memory_space=pltpu.SMEM)
ANY = pl.BlockSpec(memory_space=pl.ANY)
LIMIT = 56 * 1024 * 1024
ROOMY = 24 * 1024 * 1024


CHUNKS = 3


def columns_of(rows, stage):
    stage[...] = jnp.zeros(stage.shape, jnp.float32)
    for i, value in enumerate(rows):
        stage[i : i + 1, : value.shape[1]] = value
    return stage[...].T


def position():
    return lax.axis_index("comp"), lax.axis_index("geo")


def halves(value):
    high = value.astype(jnp.bfloat16)
    return high, (value - high.astype(jnp.float32)).astype(jnp.bfloat16)


def dot(a, b, contract=(1, 0)):
    return lax.dot_general(a, b, (((contract[0],), (contract[1],)), ((), ())), preferred_element_type=jnp.float32)


def start_all(copies):
    for copy in copies:
        copy.start()


def wait_all(copies):
    for copy in copies:
        copy.wait()


def source_terms(x, sea, wind, ice, grow_c, diss_c, rate_c, coup_hi, coup_lo):
    mean = jnp.sum(x, axis=0, keepdims=True) / x.shape[0]
    x_hi, x_lo = halves(x)
    coupled = dot(coup_hi, x_hi) + dot(coup_hi, x_lo) + dot(coup_lo, x_hi)
    net = grow_c * wind - diss_c * (mean / (1.0 + mean)) - rate_c * ice
    return sea * (x * jnp.exp(net) + 0.5 * coupled)


def edges_kernel(
    cap, x_hbm, coup_hbm, wind_hbm, growth_hbm, dissip_hbm, ice_rate_hbm, cfl_lon_hbm, cfl_lat_hbm, sea_hbm, ice_hbm,
    src, own_top, odd_hbm, even_hbm, top_hbm, places_hbm,
    xs, xt, ss, raw_top, stage, cols, top_stage, coupling, wind, growth, dissip, ice_rate, cfl_lon, cfl_lat, sea_ref, ice_ref,
    odd_msg, even_msg, top, places, x_sems, in_sems, out_sems,
):
    comps, lon_dev, lats = x_hbm.shape
    ends = (0, lon_dev - 1)
    last = pl.ds(lats - 128, 128)
    big = [pltpu.make_async_copy(x_hbm.at[:, j, :], xs.at[i], x_sems.at[i]) for i, j in enumerate(ends)]
    slim = [
        pltpu.make_async_copy(x_hbm.at[:, j, last], xt.at[j - 1], x_sems.at[j + 1]) for j in range(1, lon_dev - 1)
    ]
    small = [
        pltpu.make_async_copy(here, there, in_sems.at[i])
        for i, (here, there) in enumerate((
            (cfl_lon_hbm, cfl_lon), (cfl_lat_hbm, cfl_lat), (growth_hbm, growth), (dissip_hbm, dissip),
            (ice_rate_hbm, ice_rate), (coup_hbm, coupling), (wind_hbm, wind), (sea_hbm, sea_ref), (ice_hbm, ice_ref),
        ))
    ]
    start_all((*small[:5], small[5], *small[6:], *big, *slim))
    outs = iter(out_sems.at[i] for i in range(out_sems.shape[0]))
    done = []

    def send(here, there):
        copy = pltpu.make_async_copy(here, there, next(outs))
        copy.start()
        done.append(copy)

    odd = lax.rem(position()[1], 2)
    wait_all(small[:5])
    cols[...] = columns_of((growth[...], dissip[...], ice_rate[...]), stage)
    grow_c, diss_c, rate_c = (cols[:comps, i : i + 1] for i in range(3))
    speed = cfl_lon[...] * jnp.where(odd == 1, 1.0, -1.0)
    pick = lax.broadcasted_iota(jnp.int32, (16, comps), 0)
    flags = jnp.where(pick == 0, speed, jnp.where(pick == 1, -speed, -cfl_lat[...])) > 0.0
    upto = lax.broadcasted_iota(jnp.int32, (comps, comps), 0) <= lax.broadcasted_iota(jnp.int32, (comps, comps), 1)
    ones = jnp.where(upto, 1.0, 0.0).astype(jnp.bfloat16)
    rank = dot(jnp.where(flags, 1.0, 0.0).astype(jnp.bfloat16), ones)
    place = jnp.where(flags, rank - 1.0, -1.0)
    places[...] = place[:8]
    send(places, places_hbm)

    def packing(i, rows):
        at = lax.broadcasted_iota(jnp.int32, (rows, comps), 0).astype(jnp.float32)
        return jnp.where(at == place[i : i + 1, :], 1.0, 0.0).astype(jnp.bfloat16)

    wait_all(small[5:])
    coup_hi, coup_lo = halves(coupling[...])
    terms = functools.partial(
        source_terms, grow_c=grow_c, diss_c=diss_c, rate_c=rate_c, coup_hi=coup_hi, coup_lo=coup_lo
    )
    lane = lax.broadcasted_iota(jnp.int32, (comps, 128), 1)
    lane8 = lax.broadcasted_iota(jnp.int32, (8, 128), 1)

    def gather_last(tile_of, lane):
        total = jnp.zeros(lane.shape, jnp.float32)
        for j in range(lon_dev):
            total = jnp.where(lane == j, pltpu.roll(tile_of(j), j + 1, 1), total)
        return total

    row_top = lambda ref: gather_last(
        lambda j: jnp.broadcast_to(ref[j : j + 1, lats - 128 :].astype(jnp.float32), (8, 128)), lane8
    )[:1]
    row = lambda ref, j: ref[j : j + 1, :].astype(jnp.float32)
    for i, j in enumerate(ends):
        big[i].wait()
        ss[i] = terms(xs[i], row(sea_ref, j), row(wind, j), row(ice_ref, j))
        send(ss.at[i], src.at[i])
    for i, (msg, msg_hbm) in enumerate(((odd_msg, odd_hbm), (even_msg, even_hbm))):
        end = odd if i == 0 else 1 - odd
        hi, lo = halves(ss[end])
        pack = packing(i, cap)
        msg[:cap, :] = dot(pack, hi) + dot(pack, lo)
        sea = jnp.where(end == 1, row(sea_ref, ends[1]), row(sea_ref, ends[0]))
        msg[cap : cap + 8, :] = jnp.broadcast_to(sea, (8, lats))
        send(msg, msg_hbm)
    wait_all(slim)
    raw_top[...] = gather_last(
        lambda j: xs[ends.index(j), :, lats - 128 :] if j in ends else xt[j - 1], lane
    )
    top_stage[:comps, :] = terms(raw_top[...], row_top(sea_ref), row_top(wind), row_top(ice_ref))
    send(top_stage.at[:comps], own_top)
    lat_w = top.shape[1]
    top_hi, top_lo = halves(top_stage[:comps, :])
    top_pack = packing(2, lat_w)
    packed = (dot(top_pack, top_hi) + dot(top_pack, top_lo)).T[:lon_dev]
    sea_top = sea_ref[:, lats - 1 : lats].astype(jnp.float32)
    top[...] = jnp.where(lax.broadcasted_iota(jnp.int32, (lon_dev, lat_w), 1) == lat_w - 1, sea_top, packed)
    for slot in range(top_hbm.shape[0]):
        send(top, top_hbm.at[slot])
    wait_all(done)


def inner_kernel(
    x_hbm, coup_hbm, src_hbm, wind_hbm, growth_hbm, dissip_hbm, ice_rate_hbm, cfl_lon_hbm, cfl_lat_hbm, sea_hbm, ice_hbm,
    out, xs, src, outs, stage, cols, coupling, wind, growth, dissip, ice_rate, cfl_lon, cfl_lat, sea_ref, ice_ref,
    in_sems, out_sems,
):
    comps, lon_dev, lats = x_hbm.shape
    middle = range(1, lon_dev - 1)
    pairs = [
        (cfl_lon_hbm, cfl_lon), (cfl_lat_hbm, cfl_lat), (growth_hbm, growth), (dissip_hbm, dissip),
        (ice_rate_hbm, ice_rate), (coup_hbm, coupling), (wind_hbm, wind), (sea_hbm, sea_ref), (ice_hbm, ice_ref),
        *((x_hbm.at[:, j, :], xs.at[j - 1]) for j in middle),
        (src_hbm.at[0], src.at[0]), (src_hbm.at[1], src.at[lon_dev - 1]),
    ]
    copies = [pltpu.make_async_copy(here, there, in_sems.at[i]) for i, (here, there) in enumerate(pairs)]
    start_all(copies)
    wait_all(copies[:5])
    cols[...] = columns_of((growth[...], dissip[...], ice_rate[...], cfl_lon[...], cfl_lat[...]), stage)
    grow_c, diss_c, rate_c = (cols[:comps, i : i + 1] for i in range(3))
    wait_all(copies[5:])
    coup_hi, coup_lo = halves(coupling[...])
    row = lambda ref, j: ref[j : j + 1, :].astype(jnp.float32)
    for j in middle:
        src[j] = source_terms(
            xs[j - 1], row(sea_ref, j), row(wind, j), row(ice_ref, j), grow_c, diss_c, rate_c, coup_hi, coup_lo
        )
    sea = [row(sea_ref, j) for j in range(lon_dev)]
    step = comps // CHUNKS
    lane = lax.broadcasted_iota(jnp.int32, (step, lats), 1)
    wide = [jnp.broadcast_to(sea[j - 1] * sea[j], (step, lats)) for j in range(1, lon_dev)]
    tall = []
    for j in range(lon_dev):
        own = jnp.broadcast_to(sea[j], (step, lats))
        tall.append(jnp.where(lane == lats - 1, 0.0, own * pltpu.roll(own, lats - 1, 1)))

    def rows(at):
        params = cols[at, :]
        lon_pos = jnp.maximum(params[:, 3:4], 0.0)
        lon_neg = jnp.minimum(params[:, 3:4], 0.0)
        lat_pos = jnp.maximum(params[:, 4:5], 0.0)
        lat_neg = jnp.minimum(params[:, 4:5], 0.0)
        vals = [src[j, at, :] for j in range(lon_dev)]
        flux = [wide[j] * (lon_pos * vals[j] + lon_neg * vals[j + 1]) for j in range(lon_dev - 1)]
        for j in range(lon_dev):
            lat = tall[j] * (lat_pos * vals[j] + lat_neg * pltpu.roll(vals[j], lats - 1, 1))
            value = vals[j] - (lat - pltpu.roll(lat, 1, 1))
            if j > 0:
                value = value + flux[j - 1]
            if j < lon_dev - 1:
                value = value - flux[j]
            outs[j, at, :] = value

    done = []
    for c in range(CHUNKS):
        at = pl.ds(c * step, step)
        rows(at)
        for j in range(lon_dev):
            done.append(pltpu.make_async_copy(outs.at[j, at, :], out.at[at, j, :], out_sems.at[c, j]))
            done[-1].start()
    wait_all(done)


def finish_kernel(
    cap, n_comp, n_geo, fold, over, part, src_hbm, own_top_hbm, odd_hbm, even_hbm, seam_hbm, halo_hbm, norths_hbm, places_hbm,
    cfl_lon_hbm, cfl_lat_hbm, sea_hbm,
    out, src, acc, acc_top, own_top, msgs, seam, halo, norths, stage, cols, top_rows, places, cfl_lon, cfl_lat, sea_ref,
    in_sems, out_sems,
):
    comps, lon_dev, lats = part.shape
    ends = (0, lon_dev - 1)
    middle = range(1, lon_dev - 1)
    last = pl.ds(lats - 128, 128)
    me_comp, me_geo = position()
    odd = lax.rem(me_geo, 2)
    q = fold[0] // lon_dev
    shift = lax.rem(fold[0], lon_dev)

    def slot_of(q):
        source = lax.rem(q - (me_comp * n_geo + me_geo) + 2 * n_comp * n_geo, n_comp * n_geo)
        y, _, x = digits(lax.rem(source, n_geo))
        return y * 4 + x

    slot_0, slot_1 = slot_of(q), slot_of(q - 1)
    pairs = [
        (places_hbm, places), (cfl_lon_hbm, cfl_lon), (cfl_lat_hbm, cfl_lat), (sea_hbm, sea_ref),
        (seam_hbm.at[slot_0], seam.at[0]), (seam_hbm.at[slot_1], seam.at[1]),
        (odd_hbm, msgs.at[0]), (even_hbm, msgs.at[1]),
        (own_top_hbm, own_top), (src_hbm, src),
        *((part.at[:, j, :], acc.at[i]) for i, j in enumerate(ends)),
        *((part.at[:, j, last], acc_top.at[j - 1]) for j in middle),
    ]
    copies = [pltpu.make_async_copy(here, there, in_sems.at[i]) for i, (here, there) in enumerate(pairs)]
    start_all(copies)
    wait_all(copies[:4])
    cols[...] = columns_of((cfl_lon[...], cfl_lat[...], places[1:2, :], places[0:1, :], places[2:3, :]), stage)

    def spread(i, width):
        at = lax.broadcasted_iota(jnp.int32, (comps, width), 1).astype(jnp.float32)
        return jnp.where(at == cols[:comps, 2 + i : 3 + i], 1.0, 0.0).astype(jnp.bfloat16)

    wait_all(copies[4:8])
    total = None
    for i in range(2):
        hi, lo = halves(msgs[i, :cap, :])
        step = spread(i, cap)
        step = dot(step, hi) + dot(step, lo)
        total = step if total is None else total + step
    halo[...] = total
    lat_w = seam.shape[2]
    top_rows[...] = jnp.zeros(top_rows.shape, jnp.float32)
    for j in range(lon_dev):
        place = shift - j
        block = jnp.where(place >= 0, 0, 1)
        row = jnp.where(place >= 0, place, place + lon_dev)
        top_rows[j : j + 1, :] = seam[block, pl.ds(row, 1), :]
    top_hi, top_lo = halves(top_rows[...])
    top_spread = spread(2, lat_w)
    norths[...] = dot(top_spread, top_hi, (1, 1)) + dot(top_spread, top_lo, (1, 1))

    @pl.when(over[0] > 0)
    def _():
        pltpu.sync_copy(halo_hbm, halo)
        pltpu.sync_copy(norths_hbm, norths)

    sea_odd, sea_even = msgs[0, cap : cap + 1, :], msgs[1, cap : cap + 1, :]
    open_west = jnp.where(odd == 1, sea_even, sea_odd) * sea_ref[0:1, :].astype(jnp.float32)
    open_east = jnp.where(odd == 1, sea_odd, sea_even) * sea_ref[lon_dev - 1 : lon_dev, :].astype(jnp.float32)
    rows_of = comps // CHUNKS
    lane_top = lax.broadcasted_iota(jnp.int32, (rows_of, 128), 1)
    open_top = jnp.zeros((rows_of, 128), jnp.float32)
    for j in range(lon_dev):
        both = top_rows[j : j + 1, lat_w - 1 : lat_w] * sea_ref[j : j + 1, lats - 1 : lats].astype(jnp.float32)
        open_top = jnp.where(lane_top == j, both, open_top)
    wide_west = jnp.broadcast_to(open_west, (rows_of, lats))
    wide_east = jnp.broadcast_to(open_east, (rows_of, lats))
    wait_all(copies[8:])

    def rows(at):
        params = cols[at, :]
        lon_pos = jnp.maximum(params[:, 0:1], 0.0)
        lon_neg = jnp.minimum(params[:, 0:1], 0.0)
        lat_pos = jnp.maximum(params[:, 1:2], 0.0)
        lat_neg = jnp.minimum(params[:, 1:2], 0.0)
        edge = halo[at, :]
        flux_top = open_top * (lat_pos * own_top[at, :] + lat_neg * norths[at, :])
        top_of = lambda j: jnp.where(lane_top == 127, pltpu.roll(flux_top, 127 - j, 1), 0.0)
        west = acc[0, at, :] + wide_west * (lon_pos * edge + lon_neg * src[0, at, :])
        east = acc[1, at, :] - wide_east * (lon_pos * src[1, at, :] + lon_neg * edge)
        for i, value in enumerate((west, east)):
            acc[i, at, : lats - 128] = value[:, : lats - 128]
            acc[i, at, lats - 128 :] = value[:, lats - 128 :] - top_of(ends[i])
        for j in middle:
            acc_top[j - 1, at, :] = acc_top[j - 1, at, :] - top_of(j)

    done = []
    for c in range(CHUNKS):
        at = pl.ds(c * rows_of, rows_of)
        rows(at)
        backs = [(acc.at[i, at, :], out.at[at, j, :]) for i, j in enumerate(ends)]
        backs += [(acc_top.at[j - 1, at, :], out.at[at, j, last]) for j in middle]
        for i, (here, there) in enumerate(backs):
            done.append(pltpu.make_async_copy(here, there, out_sems.at[c, i]))
            done[-1].start()
    wait_all(done)


def digits(place):
    return place // 8, lax.rem(place // 4, 2), lax.rem(place, 4)


def reroute_kernel(n_comp, n_geo, fold, got, out, sems):
    me_comp, me_geo = position()
    me_y, me_h, me_x = digits(me_geo)
    n_y = n_geo // 8
    total = n_comp * n_geo
    lon_dev = got.shape[1]
    copies = []
    for i in range(2):
        q = lax.rem(fold[0] // lon_dev - i + total, total)
        q_y, q_h, q_x = digits(lax.rem(q, n_geo))
        to_x = lax.rem(q_x - me_x + 4, 4)
        short = q_h - me_h - (to_x > q_x).astype(jnp.int32)
        to_y = lax.rem(q_y - me_y - (short < 0).astype(jnp.int32) + 2 * n_y, n_y)
        source = lax.rem(q - (me_comp * n_geo + to_y * 8 + me_h * 4 + to_x) + total, total)
        held = source // n_geo * 2 + lax.rem(source // 4, 2)
        copies.append(pltpu.make_async_copy(got.at[held], out.at[to_y * 4 + to_x], sems.at[i]))
    start_all(copies)
    wait_all(copies)


def seam_of(n_comp, n_geo, top, fold_partner):
    n_y = n_geo // 8
    flat = lambda c, y, h, x: c * n_geo + y * 8 + h * 4 + x
    lines = [[flat(c, y, h, x) for c in range(n_comp) for h in range(2)] for y in range(n_y) for x in range(4)]
    planes = [[flat(c, y, h, x) for y in range(n_y) for x in range(4)] for c in range(n_comp) for h in range(2)]
    by_line = lax.all_to_all(top, AXES, 0, 0, tiled=True, axis_index_groups=lines)
    slots = pl.pallas_call(
        functools.partial(reroute_kernel, n_comp, n_geo),
        out_shape=jax.ShapeDtypeStruct((n_y * 4, *top.shape[1:]), jnp.float32),
        in_specs=[SMEM, ANY],
        out_specs=ANY,
        scratch_shapes=[pltpu.SemaphoreType.DMA((2,))],
        compiler_params=pltpu.CompilerParams(vmem_limit_bytes=1024 * 1024),
        name="reroute",
    )(fold_partner, by_line)
    return lax.all_to_all(slots, AXES, 0, 0, tiled=True, axis_index_groups=planes)


def whole_edges(count, lon_dev, cfl_lon, src, own_top, fold_partner):
    forward = [(d, (d + 1) % count) for d in range(count)]
    west = lax.ppermute(src[1], AXES, forward)
    east = lax.ppermute(src[0], AXES, [(b, a) for a, b in forward])
    halo = jnp.where(cfl_lon[:, None] > 0.0, west, east)
    q, shift = fold_partner[0] // lon_dev, fold_partner[0] % lon_dev
    block = lax.ppermute(own_top[:, :lon_dev].T, AXES, [(d, -d % count) for d in range(count)])
    for bit in range((count - 1).bit_length()):
        moved = lax.ppermute(block, AXES, [(d, (d + (1 << bit)) % count) for d in range(count)])
        block = jnp.where((q >> bit) % 2 == 1, moved, block)
    before = lax.ppermute(block, AXES, [((d + 1) % count, d) for d in range(count)])
    window = jnp.concatenate([before, block], axis=0)
    norths = jnp.take(window, lon_dev + shift - jnp.arange(lon_dev), axis=0).T
    return halo, jnp.pad(norths, ((0, 0), (0, 128 - lon_dev)))


def solution(mesh):
    n_comp, n_geo = mesh.shape["comp"], mesh.shape["geo"]
    count = n_comp * n_geo
    lon = P(AXES, None)
    placed = (P(None, AXES, None), lon, P(), P(), P(), P(), P(), P(), lon, lon, P())
    f32 = jnp.float32
    params = pltpu.CompilerParams(vmem_limit_bytes=LIMIT)
    odd_pairs = [(d, (d + 1) % count if d % 2 else (d - 1) % count) for d in range(count)]
    even_pairs = [(d, d - 1 if d % 2 else d + 1) for d in range(count)]

    def on_device(
        spectrum, wind_speed, growth, dissip, ice_rate, coupling, cfl_lon, cfl_lat, sea_mask, ice_mask, fold_partner
    ):
        comps, lon_dev, lats = spectrum.shape
        wide = -(-comps // 128) * 128
        lat_w = CAP
        size = CAP + 8
        row = lambda v: v.reshape(1, comps)
        shaped = lambda *dims: jax.ShapeDtypeStruct(dims, f32)
        vmem = lambda *dims: pltpu.VMEM(dims, f32)
        dmas = lambda *dims: pltpu.SemaphoreType.DMA(dims)
        mask = pltpu.VMEM((lon_dev, lats), jnp.int32)
        rates = (row(growth), row(dissip), row(ice_rate), row(cfl_lon), row(cfl_lat))
        src, own_top, odd_msg, even_msg, top, places = pl.pallas_call(
            functools.partial(edges_kernel, CAP),
            out_shape=(
                shaped(2, comps, lats), shaped(comps, 128), shaped(size, lats), shaped(size, lats),
                shaped(2 * n_comp, lon_dev, lat_w), shaped(8, comps),
            ),
            in_specs=[ANY] * 10,
            out_specs=(ANY,) * 6,
            scratch_shapes=[
                vmem(2, comps, lats), vmem(lon_dev - 2, comps, 128), vmem(2, comps, lats), vmem(comps, 128),
                vmem(128, wide), vmem(wide, 128), vmem(wide, 128), vmem(comps, comps), vmem(lon_dev, lats),
                *[vmem(1, comps)] * 5, mask, mask, vmem(size, lats), vmem(size, lats), vmem(lon_dev, lat_w),
                vmem(8, comps), dmas(lon_dev), dmas(9), dmas(2 * n_comp + 6),
            ],
            compiler_params=params,
            name="edges",
        )(spectrum, coupling, wind_speed, *rates, sea_mask, ice_mask)
        odd_got = lax.ppermute(odd_msg, AXES, odd_pairs)
        even_got = lax.ppermute(even_msg, AXES, even_pairs)
        seam = seam_of(n_comp, n_geo, top, fold_partner)
        part = pl.pallas_call(
            inner_kernel,
            out_shape=shaped(comps, lon_dev, lats),
            in_specs=[ANY] * 11,
            out_specs=ANY,
            scratch_shapes=[
                vmem(lon_dev - 2, comps, lats), vmem(lon_dev, comps, lats), vmem(lon_dev, comps, lats),
                vmem(128, wide), vmem(wide, 128), vmem(comps, comps), vmem(lon_dev, lats),
                *[vmem(1, comps)] * 5, mask, mask, dmas(lon_dev + 9), dmas(CHUNKS, lon_dev),
            ],
            compiler_params=params,
            cost_estimate=pl.CostEstimate(flops=2_000_000_000, bytes_accessed=8_000_000, transcendentals=500_000),
            name="inner",
        )(spectrum, coupling, src, wind_speed, *rates, sea_mask, ice_mask)
        signs = jnp.stack([cfl_lon, -cfl_lon, -cfl_lat])
        over = jnp.max(jnp.sum((signs > 0.0).astype(jnp.int32), axis=1)) >= CAP
        halo, norths = lax.cond(
            over,
            functools.partial(whole_edges, count, lon_dev),
            lambda *_: (jnp.zeros((comps, lats), f32), jnp.zeros((comps, 128), f32)),
            cfl_lon, src, own_top, fold_partner,
        )
        return pl.pallas_call(
            functools.partial(finish_kernel, CAP, n_comp, n_geo),
            out_shape=shaped(comps, lon_dev, lats),
            in_specs=[SMEM, SMEM] + [ANY] * 12,
            out_specs=ANY,
            input_output_aliases={2: 0},
            scratch_shapes=[
                vmem(2, comps, lats), vmem(2, comps, lats), vmem(lon_dev - 2, comps, 128), vmem(comps, 128),
                vmem(2, size, lats), vmem(2, lon_dev, lat_w), vmem(comps, lats), vmem(comps, 128), vmem(128, wide),
                vmem(wide, 128), vmem(128, lat_w), vmem(8, comps), vmem(1, comps), vmem(1, comps), mask,
                dmas(lon_dev + 10), dmas(CHUNKS, lon_dev),
            ],
            compiler_params=pltpu.CompilerParams(vmem_limit_bytes=ROOMY),
            name="finish",
        )(
            fold_partner, over.astype(jnp.int32).reshape(1), part, src, own_top, odd_got, even_got, seam, halo, norths,
            places, row(cfl_lon), row(cfl_lat), sea_mask,
        )

    return jax.shard_map(
        on_device, mesh=mesh, in_specs=placed, out_specs=P(None, AXES, None), check_vma=False
    )
```

```python
import functools

import jax
import jax.numpy as jnp
from jax import lax
from jax.experimental import pallas as pl
from jax.experimental.pallas import tpu as pltpu
from jax.sharding import PartitionSpec as P

AXES = ("comp", "geo")
CAP = 256
VMEM = pl.BlockSpec(memory_space=pltpu.VMEM)
SMEM = pl.BlockSpec(memory_space=pltpu.SMEM)
ANY = pl.BlockSpec(memory_space=pl.ANY)
LIMIT = 56 * 1024 * 1024
ROOMY = 24 * 1024 * 1024


CHUNKS = 3


def columns_of(rows, stage):
    stage[...] = jnp.zeros(stage.shape, jnp.float32)
    for i, value in enumerate(rows):
        stage[i : i + 1, : value.shape[1]] = value
    return stage[...].T


def position():
    return lax.axis_index("comp"), lax.axis_index("geo")


def halves(value):
    high = value.astype(jnp.bfloat16)
    return high, (value - high.astype(jnp.float32)).astype(jnp.bfloat16)


def dot(a, b, contract=(1, 0)):
    return lax.dot_general(a, b, (((contract[0],), (contract[1],)), ((), ())), preferred_element_type=jnp.float32)


def start_all(copies):
    for copy in copies:
        copy.start()


def wait_all(copies):
    for copy in copies:
        copy.wait()


def source_terms(x, sea, wind, ice, grow_c, diss_c, rate_c, coup_hi, coup_lo):
    mean = jnp.sum(x, axis=0, keepdims=True) / x.shape[0]
    x_hi, x_lo = halves(x)
    coupled = dot(coup_hi, x_hi) + dot(coup_hi, x_lo) + dot(coup_lo, x_hi)
    net = grow_c * wind - diss_c * (mean / (1.0 + mean)) - rate_c * ice
    return sea * (x * jnp.exp(net) + 0.5 * coupled)


def edges_kernel(
    cap, x_hbm, coup_hbm, wind_hbm, growth_hbm, dissip_hbm, ice_rate_hbm, cfl_lon_hbm, cfl_lat_hbm, sea_hbm, ice_hbm,
    src, own_top, odd_hbm, even_hbm, top_hbm, places_hbm,
    xs, xt, ss, raw_top, stage, cols, top_stage, coupling, wind, growth, dissip, ice_rate, cfl_lon, cfl_lat, sea_ref, ice_ref,
    odd_msg, even_msg, top, places, x_sems, in_sems, out_sems,
):
    comps, lon_dev, lats = x_hbm.shape
    ends = (0, lon_dev - 1)
    last = pl.ds(lats - 128, 128)
    big = [pltpu.make_async_copy(x_hbm.at[:, j, :], xs.at[i], x_sems.at[i]) for i, j in enumerate(ends)]
    slim = [
        pltpu.make_async_copy(x_hbm.at[:, j, last], xt.at[j - 1], x_sems.at[j + 1]) for j in range(1, lon_dev - 1)
    ]
    small = [
        pltpu.make_async_copy(here, there, in_sems.at[i])
        for i, (here, there) in enumerate((
            (cfl_lon_hbm, cfl_lon), (cfl_lat_hbm, cfl_lat), (growth_hbm, growth), (dissip_hbm, dissip),
            (ice_rate_hbm, ice_rate), (coup_hbm, coupling), (wind_hbm, wind), (sea_hbm, sea_ref), (ice_hbm, ice_ref),
        ))
    ]
    start_all((*small[:5], small[5], *small[6:], *big, *slim))
    outs = iter(out_sems.at[i] for i in range(out_sems.shape[0]))
    done = []

    def send(here, there):
        copy = pltpu.make_async_copy(here, there, next(outs))
        copy.start()
        done.append(copy)

    odd = lax.rem(position()[1], 2)
    wait_all(small[:5])
    cols[...] = columns_of((growth[...], dissip[...], ice_rate[...]), stage)
    grow_c, diss_c, rate_c = (cols[:comps, i : i + 1] for i in range(3))
    speed = cfl_lon[...] * jnp.where(odd == 1, 1.0, -1.0)
    pick = lax.broadcasted_iota(jnp.int32, (16, comps), 0)
    flags = jnp.where(pick == 0, speed, jnp.where(pick == 1, -speed, -cfl_lat[...])) > 0.0
    upto = lax.broadcasted_iota(jnp.int32, (comps, comps), 0) <= lax.broadcasted_iota(jnp.int32, (comps, comps), 1)
    ones = jnp.where(upto, 1.0, 0.0).astype(jnp.bfloat16)
    rank = dot(jnp.where(flags, 1.0, 0.0).astype(jnp.bfloat16), ones)
    place = jnp.where(flags, rank - 1.0, -1.0)
    places[...] = place[:8]
    send(places, places_hbm)

    def packing(i, rows):
        at = lax.broadcasted_iota(jnp.int32, (rows, comps), 0).astype(jnp.float32)
        return jnp.where(at == place[i : i + 1, :], 1.0, 0.0).astype(jnp.bfloat16)

    wait_all(small[5:])
    coup_hi, coup_lo = halves(coupling[...])
    terms = functools.partial(
        source_terms, grow_c=grow_c, diss_c=diss_c, rate_c=rate_c, coup_hi=coup_hi, coup_lo=coup_lo
    )
    lane = lax.broadcasted_iota(jnp.int32, (comps, 128), 1)
    lane8 = lax.broadcasted_iota(jnp.int32, (8, 128), 1)

    def gather_last(tile_of, lane):
        total = jnp.zeros(lane.shape, jnp.float32)
        for j in range(lon_dev):
            total = jnp.where(lane == j, pltpu.roll(tile_of(j), j + 1, 1), total)
        return total

    row_top = lambda ref: gather_last(
        lambda j: jnp.broadcast_to(ref[j : j + 1, lats - 128 :].astype(jnp.float32), (8, 128)), lane8
    )[:1]
    row = lambda ref, j: ref[j : j + 1, :].astype(jnp.float32)
    for i, j in enumerate(ends):
        big[i].wait()
        ss[i] = terms(xs[i], row(sea_ref, j), row(wind, j), row(ice_ref, j))
        send(ss.at[i], src.at[i])
    for i, (msg, msg_hbm) in enumerate(((odd_msg, odd_hbm), (even_msg, even_hbm))):
        end = odd if i == 0 else 1 - odd
        hi, lo = halves(ss[end])
        pack = packing(i, cap)
        msg[:cap, :] = dot(pack, hi) + dot(pack, lo)
        sea = jnp.where(end == 1, row(sea_ref, ends[1]), row(sea_ref, ends[0]))
        msg[cap : cap + 8, :] = jnp.broadcast_to(sea, (8, lats))
        send(msg, msg_hbm)
    wait_all(slim)
    raw_top[...] = gather_last(
        lambda j: xs[ends.index(j), :, lats - 128 :] if j in ends else xt[j - 1], lane
    )
    top_stage[:comps, :] = terms(raw_top[...], row_top(sea_ref), row_top(wind), row_top(ice_ref))
    send(top_stage.at[:comps], own_top)
    lat_w = top.shape[1]
    top_hi, top_lo = halves(top_stage[:comps, :])
    top_pack = packing(2, lat_w)
    packed = (dot(top_pack, top_hi) + dot(top_pack, top_lo)).T[:lon_dev]
    sea_top = sea_ref[:, lats - 1 : lats].astype(jnp.float32)
    top[...] = jnp.where(lax.broadcasted_iota(jnp.int32, (lon_dev, lat_w), 1) == lat_w - 1, sea_top, packed)
    for slot in range(top_hbm.shape[0]):
        send(top, top_hbm.at[slot])
    wait_all(done)


def inner_kernel(
    x_hbm, coup_hbm, src_hbm, wind_hbm, growth_hbm, dissip_hbm, ice_rate_hbm, cfl_lon_hbm, cfl_lat_hbm, sea_hbm, ice_hbm,
    out, xs, src, outs, stage, cols, coupling, wind, growth, dissip, ice_rate, cfl_lon, cfl_lat, sea_ref, ice_ref,
    in_sems, out_sems,
):
    comps, lon_dev, lats = x_hbm.shape
    middle = range(1, lon_dev - 1)
    pairs = [
        (cfl_lon_hbm, cfl_lon), (cfl_lat_hbm, cfl_lat), (growth_hbm, growth), (dissip_hbm, dissip),
        (ice_rate_hbm, ice_rate), (coup_hbm, coupling), (wind_hbm, wind), (sea_hbm, sea_ref), (ice_hbm, ice_ref),
        *((x_hbm.at[:, j, :], xs.at[j - 1]) for j in middle),
        (src_hbm.at[0], src.at[0]), (src_hbm.at[1], src.at[lon_dev - 1]),
    ]
    copies = [pltpu.make_async_copy(here, there, in_sems.at[i]) for i, (here, there) in enumerate(pairs)]
    start_all(copies)
    wait_all(copies[:5])
    cols[...] = columns_of((growth[...], dissip[...], ice_rate[...], cfl_lon[...], cfl_lat[...]), stage)
    grow_c, diss_c, rate_c = (cols[:comps, i : i + 1] for i in range(3))
    wait_all(copies[5:])
    coup_hi, coup_lo = halves(coupling[...])
    row = lambda ref, j: ref[j : j + 1, :].astype(jnp.float32)
    for j in middle:
        src[j] = source_terms(
            xs[j - 1], row(sea_ref, j), row(wind, j), row(ice_ref, j), grow_c, diss_c, rate_c, coup_hi, coup_lo
        )
    sea = [row(sea_ref, j) for j in range(lon_dev)]
    step = comps // CHUNKS
    lane = lax.broadcasted_iota(jnp.int32, (step, lats), 1)
    wide = [jnp.broadcast_to(sea[j - 1] * sea[j], (step, lats)) for j in range(1, lon_dev)]
    tall = []
    for j in range(lon_dev):
        own = jnp.broadcast_to(sea[j], (step, lats))
        tall.append(jnp.where(lane == lats - 1, 0.0, own * pltpu.roll(own, lats - 1, 1)))

    def rows(at):
        params = cols[at, :]
        lon_pos = jnp.maximum(params[:, 3:4], 0.0)
        lon_neg = jnp.minimum(params[:, 3:4], 0.0)
        lat_pos = jnp.maximum(params[:, 4:5], 0.0)
        lat_neg = jnp.minimum(params[:, 4:5], 0.0)
        vals = [src[j, at, :] for j in range(lon_dev)]
        flux = [wide[j] * (lon_pos * vals[j] + lon_neg * vals[j + 1]) for j in range(lon_dev - 1)]
        for j in range(lon_dev):
            lat = tall[j] * (lat_pos * vals[j] + lat_neg * pltpu.roll(vals[j], lats - 1, 1))
            value = vals[j] - (lat - pltpu.roll(lat, 1, 1))
            if j > 0:
                value = value + flux[j - 1]
            if j < lon_dev - 1:
                value = value - flux[j]
            outs[j, at, :] = value

    done = []
    for c in range(CHUNKS):
        at = pl.ds(c * step, step)
        rows(at)
        for j in range(lon_dev):
            done.append(pltpu.make_async_copy(outs.at[j, at, :], out.at[at, j, :], out_sems.at[c, j]))
            done[-1].start()
    wait_all(done)


def finish_kernel(
    cap, n_comp, n_geo, fold, over, part, src_hbm, own_top_hbm, odd_hbm, even_hbm, seam_hbm, halo_hbm, norths_hbm, places_hbm,
    cfl_lon_hbm, cfl_lat_hbm, sea_hbm,
    out, src, acc, acc_top, own_top, msgs, seam, halo, norths, stage, cols, top_rows, places, cfl_lon, cfl_lat, sea_ref,
    in_sems, out_sems,
):
    comps, lon_dev, lats = part.shape
    ends = (0, lon_dev - 1)
    middle = range(1, lon_dev - 1)
    last = pl.ds(lats - 128, 128)
    me_comp, me_geo = position()
    odd = lax.rem(me_geo, 2)
    q = fold[0] // lon_dev
    shift = lax.rem(fold[0], lon_dev)

    def slot_of(q):
        source = lax.rem(q - (me_comp * n_geo + me_geo) + 2 * n_comp * n_geo, n_comp * n_geo)
        y, _, x = digits(lax.rem(source, n_geo))
        return y * 4 + x

    slot_0, slot_1 = slot_of(q), slot_of(q - 1)
    pairs = [
        (places_hbm, places), (cfl_lon_hbm, cfl_lon), (cfl_lat_hbm, cfl_lat), (sea_hbm, sea_ref),
        (seam_hbm.at[slot_0], seam.at[0]), (seam_hbm.at[slot_1], seam.at[1]),
        (odd_hbm, msgs.at[0]), (even_hbm, msgs.at[1]),
        (own_top_hbm, own_top), (src_hbm, src),
        *((part.at[:, j, :], acc.at[i]) for i, j in enumerate(ends)),
        *((part.at[:, j, last], acc_top.at[j - 1]) for j in middle),
    ]
    copies = [pltpu.make_async_copy(here, there, in_sems.at[i]) for i, (here, there) in enumerate(pairs)]
    start_all(copies)
    wait_all(copies[:4])
    cols[...] = columns_of((cfl_lon[...], cfl_lat[...], places[1:2, :], places[0:1, :], places[2:3, :]), stage)

    def spread(i, width):
        at = lax.broadcasted_iota(jnp.int32, (comps, width), 1).astype(jnp.float32)
        return jnp.where(at == cols[:comps, 2 + i : 3 + i], 1.0, 0.0).astype(jnp.bfloat16)

    wait_all(copies[4:8])
    total = None
    for i in range(2):
        hi, lo = halves(msgs[i, :cap, :])
        step = spread(i, cap)
        step = dot(step, hi) + dot(step, lo)
        total = step if total is None else total + step
    halo[...] = total
    lat_w = seam.shape[2]
    top_rows[...] = jnp.zeros(top_rows.shape, jnp.float32)
    for j in range(lon_dev):
        place = shift - j
        block = jnp.where(place >= 0, 0, 1)
        row = jnp.where(place >= 0, place, place + lon_dev)
        top_rows[j : j + 1, :] = seam[block, pl.ds(row, 1), :]
    top_hi, top_lo = halves(top_rows[...])
    top_spread = spread(2, lat_w)
    norths[...] = dot(top_spread, top_hi, (1, 1)) + dot(top_spread, top_lo, (1, 1))

    @pl.when(over[0] > 0)
    def _():
        pltpu.sync_copy(halo_hbm, halo)
        pltpu.sync_copy(norths_hbm, norths)

    sea_odd, sea_even = msgs[0, cap : cap + 1, :], msgs[1, cap : cap + 1, :]
    open_west = jnp.where(odd == 1, sea_even, sea_odd) * sea_ref[0:1, :].astype(jnp.float32)
    open_east = jnp.where(odd == 1, sea_odd, sea_even) * sea_ref[lon_dev - 1 : lon_dev, :].astype(jnp.float32)
    rows_of = comps // CHUNKS
    lane_top = lax.broadcasted_iota(jnp.int32, (rows_of, 128), 1)
    open_top = jnp.zeros((rows_of, 128), jnp.float32)
    for j in range(lon_dev):
        both = top_rows[j : j + 1, lat_w - 1 : lat_w] * sea_ref[j : j + 1, lats - 1 : lats].astype(jnp.float32)
        open_top = jnp.where(lane_top == j, both, open_top)
    wide_west = jnp.broadcast_to(open_west, (rows_of, lats))
    wide_east = jnp.broadcast_to(open_east, (rows_of, lats))
    wait_all(copies[8:])

    def rows(at):
        params = cols[at, :]
        lon_pos = jnp.maximum(params[:, 0:1], 0.0)
        lon_neg = jnp.minimum(params[:, 0:1], 0.0)
        lat_pos = jnp.maximum(params[:, 1:2], 0.0)
        lat_neg = jnp.minimum(params[:, 1:2], 0.0)
        edge = halo[at, :]
        flux_top = open_top * (lat_pos * own_top[at, :] + lat_neg * norths[at, :])
        top_of = lambda j: jnp.where(lane_top == 127, pltpu.roll(flux_top, 127 - j, 1), 0.0)
        west = acc[0, at, :] + wide_west * (lon_pos * edge + lon_neg * src[0, at, :])
        east = acc[1, at, :] - wide_east * (lon_pos * src[1, at, :] + lon_neg * edge)
        for i, value in enumerate((west, east)):
            acc[i, at, : lats - 128] = value[:, : lats - 128]
            acc[i, at, lats - 128 :] = value[:, lats - 128 :] - top_of(ends[i])
        for j in middle:
            acc_top[j - 1, at, :] = acc_top[j - 1, at, :] - top_of(j)

    done = []
    for c in range(CHUNKS):
        at = pl.ds(c * rows_of, rows_of)
        rows(at)
        backs = [(acc.at[i, at, :], out.at[at, j, :]) for i, j in enumerate(ends)]
        backs += [(acc_top.at[j - 1, at, :], out.at[at, j, last]) for j in middle]
        for i, (here, there) in enumerate(backs):
            done.append(pltpu.make_async_copy(here, there, out_sems.at[c, i]))
            done[-1].start()
    wait_all(done)


def digits(place):
    return place // 8, lax.rem(place // 4, 2), lax.rem(place, 4)


def reroute_kernel(n_comp, n_geo, fold, got, out, sems):
    me_comp, me_geo = position()
    me_y, me_h, me_x = digits(me_geo)
    n_y = n_geo // 8
    total = n_comp * n_geo
    lon_dev = got.shape[1]
    copies = []
    for i in range(2):
        q = lax.rem(fold[0] // lon_dev - i + total, total)
        q_y, q_h, q_x = digits(lax.rem(q, n_geo))
        to_x = lax.rem(q_x - me_x + 4, 4)
        short = q_h - me_h - (to_x > q_x).astype(jnp.int32)
        to_y = lax.rem(q_y - me_y - (short < 0).astype(jnp.int32) + 2 * n_y, n_y)
        source = lax.rem(q - (me_comp * n_geo + to_y * 8 + me_h * 4 + to_x) + total, total)
        held = source // n_geo * 2 + lax.rem(source // 4, 2)
        copies.append(pltpu.make_async_copy(got.at[held], out.at[to_y * 4 + to_x], sems.at[i]))
    start_all(copies)
    wait_all(copies)


def seam_of(n_comp, n_geo, top, fold_partner, messages):
    n_y = n_geo // 8
    flat = lambda c, y, h, x: c * n_geo + y * 8 + h * 4 + x
    lines = [[flat(c, y, h, x) for c in range(n_comp) for h in range(2)] for y in range(n_y) for x in range(4)]
    planes = [[flat(c, y, h, x) for y in range(n_y) for x in range(4)] for c in range(n_comp) for h in range(2)]
    by_line = lax.all_to_all(top, AXES, 0, 0, tiled=True, axis_index_groups=lines)
    by_line, messages = lax.optimization_barrier((by_line, messages))
    slots = pl.pallas_call(
        functools.partial(reroute_kernel, n_comp, n_geo),
        out_shape=jax.ShapeDtypeStruct((n_y * 4, *top.shape[1:]), jnp.float32),
        in_specs=[SMEM, ANY],
        out_specs=ANY,
        scratch_shapes=[pltpu.SemaphoreType.DMA((2,))],
        compiler_params=pltpu.CompilerParams(vmem_limit_bytes=1024 * 1024),
        name="reroute",
    )(fold_partner, by_line)
    return lax.all_to_all(slots, AXES, 0, 0, tiled=True, axis_index_groups=planes), messages


def whole_edges(count, lon_dev, cfl_lon, src, own_top, fold_partner):
    forward = [(d, (d + 1) % count) for d in range(count)]
    west = lax.ppermute(src[1], AXES, forward)
    east = lax.ppermute(src[0], AXES, [(b, a) for a, b in forward])
    halo = jnp.where(cfl_lon[:, None] > 0.0, west, east)
    q, shift = fold_partner[0] // lon_dev, fold_partner[0] % lon_dev
    block = lax.ppermute(own_top[:, :lon_dev].T, AXES, [(d, -d % count) for d in range(count)])
    for bit in range((count - 1).bit_length()):
        moved = lax.ppermute(block, AXES, [(d, (d + (1 << bit)) % count) for d in range(count)])
        block = jnp.where((q >> bit) % 2 == 1, moved, block)
    before = lax.ppermute(block, AXES, [((d + 1) % count, d) for d in range(count)])
    window = jnp.concatenate([before, block], axis=0)
    norths = jnp.take(window, lon_dev + shift - jnp.arange(lon_dev), axis=0).T
    return halo, jnp.pad(norths, ((0, 0), (0, 128 - lon_dev)))


def solution(mesh):
    n_comp, n_geo = mesh.shape["comp"], mesh.shape["geo"]
    count = n_comp * n_geo
    lon = P(AXES, None)
    placed = (P(None, AXES, None), lon, P(), P(), P(), P(), P(), P(), lon, lon, P())
    f32 = jnp.float32
    params = pltpu.CompilerParams(vmem_limit_bytes=LIMIT)
    odd_pairs = [(d, (d + 1) % count if d % 2 else (d - 1) % count) for d in range(count)]
    even_pairs = [(d, d - 1 if d % 2 else d + 1) for d in range(count)]

    def on_device(
        spectrum, wind_speed, growth, dissip, ice_rate, coupling, cfl_lon, cfl_lat, sea_mask, ice_mask, fold_partner
    ):
        comps, lon_dev, lats = spectrum.shape
        wide = -(-comps // 128) * 128
        lat_w = CAP
        size = CAP + 8
        row = lambda v: v.reshape(1, comps)
        shaped = lambda *dims: jax.ShapeDtypeStruct(dims, f32)
        vmem = lambda *dims: pltpu.VMEM(dims, f32)
        dmas = lambda *dims: pltpu.SemaphoreType.DMA(dims)
        mask = pltpu.VMEM((lon_dev, lats), jnp.int32)
        rates = (row(growth), row(dissip), row(ice_rate), row(cfl_lon), row(cfl_lat))
        src, own_top, odd_msg, even_msg, top, places = pl.pallas_call(
            functools.partial(edges_kernel, CAP),
            out_shape=(
                shaped(2, comps, lats), shaped(comps, 128), shaped(size, lats), shaped(size, lats),
                shaped(2 * n_comp, lon_dev, lat_w), shaped(8, comps),
            ),
            in_specs=[ANY] * 10,
            out_specs=(ANY,) * 6,
            scratch_shapes=[
                vmem(2, comps, lats), vmem(lon_dev - 2, comps, 128), vmem(2, comps, lats), vmem(comps, 128),
                vmem(128, wide), vmem(wide, 128), vmem(wide, 128), vmem(comps, comps), vmem(lon_dev, lats),
                *[vmem(1, comps)] * 5, mask, mask, vmem(size, lats), vmem(size, lats), vmem(lon_dev, lat_w),
                vmem(8, comps), dmas(lon_dev), dmas(9), dmas(2 * n_comp + 6),
            ],
            compiler_params=params,
            name="edges",
        )(spectrum, coupling, wind_speed, *rates, sea_mask, ice_mask)
        seam, odd_msg = seam_of(n_comp, n_geo, top, fold_partner, odd_msg)
        odd_got = lax.ppermute(odd_msg, AXES, odd_pairs)
        even_got = lax.ppermute(even_msg, AXES, even_pairs)
        part = pl.pallas_call(
            inner_kernel,
            out_shape=shaped(comps, lon_dev, lats),
            in_specs=[ANY] * 11,
            out_specs=ANY,
            scratch_shapes=[
                vmem(lon_dev - 2, comps, lats), vmem(lon_dev, comps, lats), vmem(lon_dev, comps, lats),
                vmem(128, wide), vmem(wide, 128), vmem(comps, comps), vmem(lon_dev, lats),
                *[vmem(1, comps)] * 5, mask, mask, dmas(lon_dev + 9), dmas(CHUNKS, lon_dev),
            ],
            compiler_params=params,
            cost_estimate=pl.CostEstimate(flops=2_000_000_000, bytes_accessed=8_000_000, transcendentals=500_000),
            name="inner",
        )(spectrum, coupling, src, wind_speed, *rates, sea_mask, ice_mask)
        signs = jnp.stack([cfl_lon, -cfl_lon, -cfl_lat])
        over = jnp.max(jnp.sum((signs > 0.0).astype(jnp.int32), axis=1)) >= CAP
        halo, norths = lax.cond(
            over,
            functools.partial(whole_edges, count, lon_dev),
            lambda *_: (jnp.zeros((comps, lats), f32), jnp.zeros((comps, 128), f32)),
            cfl_lon, src, own_top, fold_partner,
        )
        return pl.pallas_call(
            functools.partial(finish_kernel, CAP, n_comp, n_geo),
            out_shape=shaped(comps, lon_dev, lats),
            in_specs=[SMEM, SMEM] + [ANY] * 12,
            out_specs=ANY,
            input_output_aliases={2: 0},
            scratch_shapes=[
                vmem(2, comps, lats), vmem(2, comps, lats), vmem(lon_dev - 2, comps, 128), vmem(comps, 128),
                vmem(2, size, lats), vmem(2, lon_dev, lat_w), vmem(comps, lats), vmem(comps, 128), vmem(128, wide),
                vmem(wide, 128), vmem(128, lat_w), vmem(8, comps), vmem(1, comps), vmem(1, comps), mask,
                dmas(lon_dev + 10), dmas(CHUNKS, lon_dev),
            ],
            compiler_params=pltpu.CompilerParams(vmem_limit_bytes=ROOMY),
            name="finish",
        )(
            fold_partner, over.astype(jnp.int32).reshape(1), part, src, own_top, odd_got, even_got, seam, halo, norths,
            places, row(cfl_lon), row(cfl_lat), sea_mask,
        )

    return jax.shard_map(
        on_device, mesh=mesh, in_specs=placed, out_specs=P(None, AXES, None), check_vma=False
    )
```

```python
import functools

import jax
import jax.numpy as jnp
from jax import lax
from jax.experimental import pallas as pl
from jax.experimental.pallas import tpu as pltpu
from jax.sharding import PartitionSpec as P

AXES = ("comp", "geo")
CAP = 256
VMEM = pl.BlockSpec(memory_space=pltpu.VMEM)
SMEM = pl.BlockSpec(memory_space=pltpu.SMEM)
ANY = pl.BlockSpec(memory_space=pl.ANY)
LIMIT = 56 * 1024 * 1024
ROOMY = 24 * 1024 * 1024


CHUNKS = 3


def columns_of(rows, stage):
    stage[...] = jnp.zeros(stage.shape, jnp.float32)
    for i, value in enumerate(rows):
        stage[i : i + 1, : value.shape[1]] = value
    return stage[...].T


def position():
    return lax.axis_index("comp"), lax.axis_index("geo")


def halves(value):
    high = value.astype(jnp.bfloat16)
    return high, (value - high.astype(jnp.float32)).astype(jnp.bfloat16)


def dot(a, b, contract=(1, 0)):
    return lax.dot_general(a, b, (((contract[0],), (contract[1],)), ((), ())), preferred_element_type=jnp.float32)


def start_all(copies):
    for copy in copies:
        copy.start()


def wait_all(copies):
    for copy in copies:
        copy.wait()


def source_terms(x, sea, wind, ice, grow_c, diss_c, rate_c, coup_hi, coup_lo):
    mean = jnp.sum(x, axis=0, keepdims=True) / x.shape[0]
    x_hi, x_lo = halves(x)
    coupled = dot(coup_hi, x_hi) + dot(coup_hi, x_lo) + dot(coup_lo, x_hi)
    net = grow_c * wind - diss_c * (mean / (1.0 + mean)) - rate_c * ice
    return sea * (x * jnp.exp(net) + 0.5 * coupled)


def sender(sems):
    outs = iter(sems.at[i] for i in range(sems.shape[0]))
    done = []

    def send(here, there):
        copy = pltpu.make_async_copy(here, there, next(outs))
        copy.start()
        done.append(copy)

    return send, done


def places_of(flags):
    comps = flags.shape[1]
    upto = lax.broadcasted_iota(jnp.int32, (comps, comps), 0) <= lax.broadcasted_iota(jnp.int32, (comps, comps), 1)
    ones = jnp.where(upto, 1.0, 0.0).astype(jnp.bfloat16)
    rank = dot(jnp.where(flags, 1.0, 0.0).astype(jnp.bfloat16), ones)
    return jnp.where(flags, rank - 1.0, -1.0)


def packing(place, rows):
    at = lax.broadcasted_iota(jnp.int32, (rows, place.shape[1]), 0).astype(jnp.float32)
    return jnp.where(at == place, 1.0, 0.0).astype(jnp.bfloat16)


def row_of(ref, j):
    return ref[j : j + 1, :].astype(jnp.float32)


def tops_kernel(
    x_hbm, coup_hbm, wind_hbm, growth_hbm, dissip_hbm, ice_rate_hbm, cfl_lat_hbm, sea_hbm, ice_hbm,
    own_top, top_hbm,
    xt, raw_top, stage, cols, top_stage, coupling, wind, growth, dissip, ice_rate, cfl_lat, sea_ref, ice_ref, top,
    x_sems, in_sems, out_sems,
):
    comps, lon_dev, lats = x_hbm.shape
    last = pl.ds(lats - 128, 128)
    tiles = [pltpu.make_async_copy(x_hbm.at[:, j, last], xt.at[j], x_sems.at[j]) for j in range(lon_dev)]
    small = [
        pltpu.make_async_copy(here, there, in_sems.at[i])
        for i, (here, there) in enumerate((
            (cfl_lat_hbm, cfl_lat), (growth_hbm, growth), (dissip_hbm, dissip), (ice_rate_hbm, ice_rate),
            (coup_hbm, coupling), (wind_hbm, wind), (sea_hbm, sea_ref), (ice_hbm, ice_ref),
        ))
    ]
    start_all((*small, *tiles))
    send, done = sender(out_sems)
    wait_all(small[:4])
    cols[...] = columns_of((growth[...], dissip[...], ice_rate[...]), stage)
    grow_c, diss_c, rate_c = (cols[:comps, i : i + 1] for i in range(3))
    place = places_of(jnp.broadcast_to(cfl_lat[...] < 0.0, (16, comps)))[:1]
    lat_w = top.shape[1]
    top_pack = packing(place, lat_w)
    wait_all(small[4:])
    coup_hi, coup_lo = halves(coupling[...])
    lane = lax.broadcasted_iota(jnp.int32, (comps, 128), 1)
    lane8 = lax.broadcasted_iota(jnp.int32, (8, 128), 1)

    def gather_last(tile_of, lane):
        total = jnp.zeros(lane.shape, jnp.float32)
        for j in range(lon_dev):
            total = jnp.where(lane == j, pltpu.roll(tile_of(j), j + 1, 1), total)
        return total

    row_top = lambda ref: gather_last(
        lambda j: jnp.broadcast_to(ref[j : j + 1, lats - 128 :].astype(jnp.float32), (8, 128)), lane8
    )[:1]
    rows = [row_top(ref) for ref in (sea_ref, wind, ice_ref)]
    wait_all(tiles)
    raw_top[...] = gather_last(lambda j: xt[j], lane)
    top_stage[...] = source_terms(raw_top[...], *rows, grow_c, diss_c, rate_c, coup_hi, coup_lo)
    send(top_stage, own_top)
    top_hi, top_lo = halves(top_stage[...])
    packed = (dot(top_pack, top_hi) + dot(top_pack, top_lo)).T[:lon_dev]
    sea_top = sea_ref[:, lats - 1 : lats].astype(jnp.float32)
    top[...] = jnp.where(lax.broadcasted_iota(jnp.int32, (lon_dev, lat_w), 1) == lat_w - 1, sea_top, packed)
    for slot in range(top_hbm.shape[0]):
        send(top, top_hbm.at[slot])
    wait_all(done)


def edges_kernel(
    cap, x_hbm, coup_hbm, wind_hbm, growth_hbm, dissip_hbm, ice_rate_hbm, cfl_lon_hbm, cfl_lat_hbm, sea_hbm, ice_hbm,
    src, odd_hbm, even_hbm, places_hbm,
    xs, ss, stage, cols, coupling, wind, growth, dissip, ice_rate, cfl_lon, cfl_lat, sea_ref, ice_ref,
    odd_msg, even_msg, places, x_sems, in_sems, out_sems,
):
    comps, lon_dev, lats = x_hbm.shape
    ends = (0, lon_dev - 1)
    big = [pltpu.make_async_copy(x_hbm.at[:, j, :], xs.at[i], x_sems.at[i]) for i, j in enumerate(ends)]
    small = [
        pltpu.make_async_copy(here, there, in_sems.at[i])
        for i, (here, there) in enumerate((
            (cfl_lon_hbm, cfl_lon), (cfl_lat_hbm, cfl_lat), (growth_hbm, growth), (dissip_hbm, dissip),
            (ice_rate_hbm, ice_rate), (coup_hbm, coupling), (wind_hbm, wind), (sea_hbm, sea_ref), (ice_hbm, ice_ref),
        ))
    ]
    start_all((*small, *big))
    send, done = sender(out_sems)
    odd = lax.rem(position()[1], 2)
    wait_all(small[:5])
    cols[...] = columns_of((growth[...], dissip[...], ice_rate[...]), stage)
    grow_c, diss_c, rate_c = (cols[:comps, i : i + 1] for i in range(3))
    speed = cfl_lon[...] * jnp.where(odd == 1, 1.0, -1.0)
    pick = lax.broadcasted_iota(jnp.int32, (16, comps), 0)
    place = places_of(jnp.where(pick == 0, speed, jnp.where(pick == 1, -speed, -cfl_lat[...])) > 0.0)
    places[...] = place[:8]
    send(places, places_hbm)
    wait_all(small[5:])
    coup_hi, coup_lo = halves(coupling[...])
    for i, j in enumerate(ends):
        big[i].wait()
        ss[i] = source_terms(
            xs[i], row_of(sea_ref, j), row_of(wind, j), row_of(ice_ref, j), grow_c, diss_c, rate_c, coup_hi, coup_lo
        )
        send(ss.at[i], src.at[i])
    for i, (msg, msg_hbm) in enumerate(((odd_msg, odd_hbm), (even_msg, even_hbm))):
        end = odd if i == 0 else 1 - odd
        hi, lo = halves(ss[end])
        pack = packing(place[i : i + 1, :], cap)
        msg[:cap, :] = dot(pack, hi) + dot(pack, lo)
        sea = jnp.where(end == 1, row_of(sea_ref, ends[1]), row_of(sea_ref, ends[0]))
        msg[cap : cap + 8, :] = jnp.broadcast_to(sea, (8, lats))
        send(msg, msg_hbm)
    wait_all(done)


def inner_kernel(
    x_hbm, coup_hbm, src_hbm, wind_hbm, growth_hbm, dissip_hbm, ice_rate_hbm, cfl_lon_hbm, cfl_lat_hbm, sea_hbm, ice_hbm,
    out, xs, src, outs, stage, cols, coupling, wind, growth, dissip, ice_rate, cfl_lon, cfl_lat, sea_ref, ice_ref,
    in_sems, out_sems,
):
    comps, lon_dev, lats = x_hbm.shape
    middle = range(1, lon_dev - 1)
    pairs = [
        (cfl_lon_hbm, cfl_lon), (cfl_lat_hbm, cfl_lat), (growth_hbm, growth), (dissip_hbm, dissip),
        (ice_rate_hbm, ice_rate), (coup_hbm, coupling), (wind_hbm, wind), (sea_hbm, sea_ref), (ice_hbm, ice_ref),
        *((x_hbm.at[:, j, :], xs.at[j - 1]) for j in middle),
        (src_hbm.at[0], src.at[0]), (src_hbm.at[1], src.at[lon_dev - 1]),
    ]
    copies = [pltpu.make_async_copy(here, there, in_sems.at[i]) for i, (here, there) in enumerate(pairs)]
    start_all(copies)
    wait_all(copies[:5])
    cols[...] = columns_of((growth[...], dissip[...], ice_rate[...], cfl_lon[...], cfl_lat[...]), stage)
    grow_c, diss_c, rate_c = (cols[:comps, i : i + 1] for i in range(3))
    wait_all(copies[5:])
    coup_hi, coup_lo = halves(coupling[...])
    row = lambda ref, j: ref[j : j + 1, :].astype(jnp.float32)
    for j in middle:
        src[j] = source_terms(
            xs[j - 1], row(sea_ref, j), row(wind, j), row(ice_ref, j), grow_c, diss_c, rate_c, coup_hi, coup_lo
        )
    sea = [row(sea_ref, j) for j in range(lon_dev)]
    step = comps // CHUNKS
    lane = lax.broadcasted_iota(jnp.int32, (step, lats), 1)
    wide = [jnp.broadcast_to(sea[j - 1] * sea[j], (step, lats)) for j in range(1, lon_dev)]
    tall = []
    for j in range(lon_dev):
        own = jnp.broadcast_to(sea[j], (step, lats))
        tall.append(jnp.where(lane == lats - 1, 0.0, own * pltpu.roll(own, lats - 1, 1)))

    def rows(at):
        params = cols[at, :]
        lon_pos = jnp.maximum(params[:, 3:4], 0.0)
        lon_neg = jnp.minimum(params[:, 3:4], 0.0)
        lat_pos = jnp.maximum(params[:, 4:5], 0.0)
        lat_neg = jnp.minimum(params[:, 4:5], 0.0)
        vals = [src[j, at, :] for j in range(lon_dev)]
        flux = [wide[j] * (lon_pos * vals[j] + lon_neg * vals[j + 1]) for j in range(lon_dev - 1)]
        for j in range(lon_dev):
            lat = tall[j] * (lat_pos * vals[j] + lat_neg * pltpu.roll(vals[j], lats - 1, 1))
            value = vals[j] - (lat - pltpu.roll(lat, 1, 1))
            if j > 0:
                value = value + flux[j - 1]
            if j < lon_dev - 1:
                value = value - flux[j]
            outs[j, at, :] = value

    done = []
    for c in range(CHUNKS):
        at = pl.ds(c * step, step)
        rows(at)
        for j in range(lon_dev):
            done.append(pltpu.make_async_copy(outs.at[j, at, :], out.at[at, j, :], out_sems.at[c, j]))
            done[-1].start()
    wait_all(done)


def finish_kernel(
    cap, n_comp, n_geo, fold, over, part, src_hbm, own_top_hbm, odd_hbm, even_hbm, seam_hbm, halo_hbm, norths_hbm, places_hbm,
    cfl_lon_hbm, cfl_lat_hbm, sea_hbm,
    out, src, acc, acc_top, own_top, msgs, seam, halo, norths, stage, cols, top_rows, places, cfl_lon, cfl_lat, sea_ref,
    in_sems, out_sems,
):
    comps, lon_dev, lats = part.shape
    ends = (0, lon_dev - 1)
    middle = range(1, lon_dev - 1)
    last = pl.ds(lats - 128, 128)
    me_comp, me_geo = position()
    odd = lax.rem(me_geo, 2)
    q = fold[0] // lon_dev
    shift = lax.rem(fold[0], lon_dev)

    def slot_of(q):
        source = lax.rem(q - (me_comp * n_geo + me_geo) + 2 * n_comp * n_geo, n_comp * n_geo)
        y, _, x = digits(lax.rem(source, n_geo))
        return y * 4 + x

    slot_0, slot_1 = slot_of(q), slot_of(q - 1)
    pairs = [
        (places_hbm, places), (cfl_lon_hbm, cfl_lon), (cfl_lat_hbm, cfl_lat), (sea_hbm, sea_ref),
        (seam_hbm.at[slot_0], seam.at[0]), (seam_hbm.at[slot_1], seam.at[1]),
        (odd_hbm, msgs.at[0]), (even_hbm, msgs.at[1]),
        (own_top_hbm, own_top), (src_hbm, src),
        *((part.at[:, j, :], acc.at[i]) for i, j in enumerate(ends)),
        *((part.at[:, j, last], acc_top.at[j - 1]) for j in middle),
    ]
    copies = [pltpu.make_async_copy(here, there, in_sems.at[i]) for i, (here, there) in enumerate(pairs)]
    start_all(copies)
    wait_all(copies[:4])
    cols[...] = columns_of((cfl_lon[...], cfl_lat[...], places[1:2, :], places[0:1, :], places[2:3, :]), stage)

    def spread(i, width):
        at = lax.broadcasted_iota(jnp.int32, (comps, width), 1).astype(jnp.float32)
        return jnp.where(at == cols[:comps, 2 + i : 3 + i], 1.0, 0.0).astype(jnp.bfloat16)

    wait_all(copies[4:8])
    total = None
    for i in range(2):
        hi, lo = halves(msgs[i, :cap, :])
        step = spread(i, cap)
        step = dot(step, hi) + dot(step, lo)
        total = step if total is None else total + step
    halo[...] = total
    lat_w = seam.shape[2]
    top_rows[...] = jnp.zeros(top_rows.shape, jnp.float32)
    for j in range(lon_dev):
        place = shift - j
        block = jnp.where(place >= 0, 0, 1)
        row = jnp.where(place >= 0, place, place + lon_dev)
        top_rows[j : j + 1, :] = seam[block, pl.ds(row, 1), :]
    top_hi, top_lo = halves(top_rows[...])
    top_spread = spread(2, lat_w)
    norths[...] = dot(top_spread, top_hi, (1, 1)) + dot(top_spread, top_lo, (1, 1))

    @pl.when(over[0] > 0)
    def _():
        pltpu.sync_copy(halo_hbm, halo)
        pltpu.sync_copy(norths_hbm, norths)

    sea_odd, sea_even = msgs[0, cap : cap + 1, :], msgs[1, cap : cap + 1, :]
    open_west = jnp.where(odd == 1, sea_even, sea_odd) * sea_ref[0:1, :].astype(jnp.float32)
    open_east = jnp.where(odd == 1, sea_odd, sea_even) * sea_ref[lon_dev - 1 : lon_dev, :].astype(jnp.float32)
    rows_of = comps // CHUNKS
    lane_top = lax.broadcasted_iota(jnp.int32, (rows_of, 128), 1)
    open_top = jnp.zeros((rows_of, 128), jnp.float32)
    for j in range(lon_dev):
        both = top_rows[j : j + 1, lat_w - 1 : lat_w] * sea_ref[j : j + 1, lats - 1 : lats].astype(jnp.float32)
        open_top = jnp.where(lane_top == j, both, open_top)
    wide_west = jnp.broadcast_to(open_west, (rows_of, lats))
    wide_east = jnp.broadcast_to(open_east, (rows_of, lats))
    wait_all(copies[8:])

    def rows(at):
        params = cols[at, :]
        lon_pos = jnp.maximum(params[:, 0:1], 0.0)
        lon_neg = jnp.minimum(params[:, 0:1], 0.0)
        lat_pos = jnp.maximum(params[:, 1:2], 0.0)
        lat_neg = jnp.minimum(params[:, 1:2], 0.0)
        edge = halo[at, :]
        flux_top = open_top * (lat_pos * own_top[at, :] + lat_neg * norths[at, :])
        top_of = lambda j: jnp.where(lane_top == 127, pltpu.roll(flux_top, 127 - j, 1), 0.0)
        west = acc[0, at, :] + wide_west * (lon_pos * edge + lon_neg * src[0, at, :])
        east = acc[1, at, :] - wide_east * (lon_pos * src[1, at, :] + lon_neg * edge)
        for i, value in enumerate((west, east)):
            acc[i, at, : lats - 128] = value[:, : lats - 128]
            acc[i, at, lats - 128 :] = value[:, lats - 128 :] - top_of(ends[i])
        for j in middle:
            acc_top[j - 1, at, :] = acc_top[j - 1, at, :] - top_of(j)

    done = []
    for c in range(CHUNKS):
        at = pl.ds(c * rows_of, rows_of)
        rows(at)
        backs = [(acc.at[i, at, :], out.at[at, j, :]) for i, j in enumerate(ends)]
        backs += [(acc_top.at[j - 1, at, :], out.at[at, j, last]) for j in middle]
        for i, (here, there) in enumerate(backs):
            done.append(pltpu.make_async_copy(here, there, out_sems.at[c, i]))
            done[-1].start()
    wait_all(done)


def digits(place):
    return place // 8, lax.rem(place // 4, 2), lax.rem(place, 4)


def reroute_kernel(n_comp, n_geo, fold, got, out, sems):
    me_comp, me_geo = position()
    me_y, me_h, me_x = digits(me_geo)
    n_y = n_geo // 8
    total = n_comp * n_geo
    lon_dev = got.shape[1]
    copies = []
    for i in range(2):
        q = lax.rem(fold[0] // lon_dev - i + total, total)
        q_y, q_h, q_x = digits(lax.rem(q, n_geo))
        to_x = lax.rem(q_x - me_x + 4, 4)
        short = q_h - me_h - (to_x > q_x).astype(jnp.int32)
        to_y = lax.rem(q_y - me_y - (short < 0).astype(jnp.int32) + 2 * n_y, n_y)
        source = lax.rem(q - (me_comp * n_geo + to_y * 8 + me_h * 4 + to_x) + total, total)
        held = source // n_geo * 2 + lax.rem(source // 4, 2)
        copies.append(pltpu.make_async_copy(got.at[held], out.at[to_y * 4 + to_x], sems.at[i]))
    start_all(copies)
    wait_all(copies)


def seam_of(n_comp, n_geo, top, fold_partner, messages):
    n_y = n_geo // 8
    flat = lambda c, y, h, x: c * n_geo + y * 8 + h * 4 + x
    lines = [[flat(c, y, h, x) for c in range(n_comp) for h in range(2)] for y in range(n_y) for x in range(4)]
    planes = [[flat(c, y, h, x) for y in range(n_y) for x in range(4)] for c in range(n_comp) for h in range(2)]
    by_line = lax.all_to_all(top, AXES, 0, 0, tiled=True, axis_index_groups=lines)
    by_line, messages = lax.optimization_barrier((by_line, messages))
    slots = pl.pallas_call(
        functools.partial(reroute_kernel, n_comp, n_geo),
        out_shape=jax.ShapeDtypeStruct((n_y * 4, *top.shape[1:]), jnp.float32),
        in_specs=[SMEM, ANY],
        out_specs=ANY,
        scratch_shapes=[pltpu.SemaphoreType.DMA((2,))],
        compiler_params=pltpu.CompilerParams(vmem_limit_bytes=1024 * 1024),
        name="reroute",
    )(fold_partner, by_line)
    return lax.all_to_all(slots, AXES, 0, 0, tiled=True, axis_index_groups=planes), messages


def whole_edges(count, lon_dev, cfl_lon, src, own_top, fold_partner):
    forward = [(d, (d + 1) % count) for d in range(count)]
    west = lax.ppermute(src[1], AXES, forward)
    east = lax.ppermute(src[0], AXES, [(b, a) for a, b in forward])
    halo = jnp.where(cfl_lon[:, None] > 0.0, west, east)
    q, shift = fold_partner[0] // lon_dev, fold_partner[0] % lon_dev
    block = lax.ppermute(own_top[:, :lon_dev].T, AXES, [(d, -d % count) for d in range(count)])
    for bit in range((count - 1).bit_length()):
        moved = lax.ppermute(block, AXES, [(d, (d + (1 << bit)) % count) for d in range(count)])
        block = jnp.where((q >> bit) % 2 == 1, moved, block)
    before = lax.ppermute(block, AXES, [((d + 1) % count, d) for d in range(count)])
    window = jnp.concatenate([before, block], axis=0)
    norths = jnp.take(window, lon_dev + shift - jnp.arange(lon_dev), axis=0).T
    return halo, jnp.pad(norths, ((0, 0), (0, 128 - lon_dev)))


def solution(mesh):
    n_comp, n_geo = mesh.shape["comp"], mesh.shape["geo"]
    count = n_comp * n_geo
    lon = P(AXES, None)
    placed = (P(None, AXES, None), lon, P(), P(), P(), P(), P(), P(), lon, lon, P())
    f32 = jnp.float32
    params = pltpu.CompilerParams(vmem_limit_bytes=LIMIT)
    odd_pairs = [(d, (d + 1) % count if d % 2 else (d - 1) % count) for d in range(count)]
    even_pairs = [(d, d - 1 if d % 2 else d + 1) for d in range(count)]

    def on_device(
        spectrum, wind_speed, growth, dissip, ice_rate, coupling, cfl_lon, cfl_lat, sea_mask, ice_mask, fold_partner
    ):
        comps, lon_dev, lats = spectrum.shape
        wide = -(-comps // 128) * 128
        lat_w = CAP
        size = CAP + 8
        row = lambda v: v.reshape(1, comps)
        shaped = lambda *dims: jax.ShapeDtypeStruct(dims, f32)
        vmem = lambda *dims: pltpu.VMEM(dims, f32)
        dmas = lambda *dims: pltpu.SemaphoreType.DMA(dims)
        mask = pltpu.VMEM((lon_dev, lats), jnp.int32)
        rates = (row(growth), row(dissip), row(ice_rate), row(cfl_lon), row(cfl_lat))
        own_top, top = pl.pallas_call(
            tops_kernel,
            out_shape=(shaped(comps, 128), shaped(2 * n_comp, lon_dev, lat_w)),
            in_specs=[ANY] * 9,
            out_specs=(ANY,) * 2,
            scratch_shapes=[
                vmem(lon_dev, comps, 128), vmem(comps, 128), vmem(128, wide), vmem(wide, 128), vmem(comps, 128),
                vmem(comps, comps), vmem(lon_dev, lats), *[vmem(1, comps)] * 4, mask, mask, vmem(lon_dev, lat_w),
                dmas(lon_dev), dmas(8), dmas(2 * n_comp + 1),
            ],
            compiler_params=params,
            name="tops",
        )(spectrum, coupling, wind_speed, *rates[:3], rates[4], sea_mask, ice_mask)
        src, odd_msg, even_msg, places = pl.pallas_call(
            functools.partial(edges_kernel, CAP),
            out_shape=(shaped(2, comps, lats), shaped(size, lats), shaped(size, lats), shaped(8, comps)),
            in_specs=[ANY] * 10,
            out_specs=(ANY,) * 4,
            scratch_shapes=[
                vmem(2, comps, lats), vmem(2, comps, lats), vmem(128, wide), vmem(wide, 128), vmem(comps, comps),
                vmem(lon_dev, lats), *[vmem(1, comps)] * 5, mask, mask, vmem(size, lats), vmem(size, lats),
                vmem(8, comps), dmas(2), dmas(9), dmas(5),
            ],
            compiler_params=params,
            cost_estimate=pl.CostEstimate(flops=2_000_000_000, bytes_accessed=4_000_000, transcendentals=300_000),
            name="edges",
        )(spectrum, coupling, wind_speed, *rates, sea_mask, ice_mask)
        seam, odd_msg = seam_of(n_comp, n_geo, top, fold_partner, odd_msg)
        odd_got = lax.ppermute(odd_msg, AXES, odd_pairs)
        even_got = lax.ppermute(even_msg, AXES, even_pairs)
        part = pl.pallas_call(
            inner_kernel,
            out_shape=shaped(comps, lon_dev, lats),
            in_specs=[ANY] * 11,
            out_specs=ANY,
            scratch_shapes=[
                vmem(lon_dev - 2, comps, lats), vmem(lon_dev, comps, lats), vmem(lon_dev, comps, lats),
                vmem(128, wide), vmem(wide, 128), vmem(comps, comps), vmem(lon_dev, lats),
                *[vmem(1, comps)] * 5, mask, mask, dmas(lon_dev + 9), dmas(CHUNKS, lon_dev),
            ],
            compiler_params=params,
            cost_estimate=pl.CostEstimate(flops=2_000_000_000, bytes_accessed=8_000_000, transcendentals=500_000),
            name="inner",
        )(spectrum, coupling, src, wind_speed, *rates, sea_mask, ice_mask)
        signs = jnp.stack([cfl_lon, -cfl_lon, -cfl_lat])
        over = jnp.max(jnp.sum((signs > 0.0).astype(jnp.int32), axis=1)) >= CAP
        halo, norths = lax.cond(
            over,
            functools.partial(whole_edges, count, lon_dev),
            lambda *_: (jnp.zeros((comps, lats), f32), jnp.zeros((comps, 128), f32)),
            cfl_lon, src, own_top, fold_partner,
        )
        return pl.pallas_call(
            functools.partial(finish_kernel, CAP, n_comp, n_geo),
            out_shape=shaped(comps, lon_dev, lats),
            in_specs=[SMEM, SMEM] + [ANY] * 12,
            out_specs=ANY,
            input_output_aliases={2: 0},
            scratch_shapes=[
                vmem(2, comps, lats), vmem(2, comps, lats), vmem(lon_dev - 2, comps, 128), vmem(comps, 128),
                vmem(2, size, lats), vmem(2, lon_dev, lat_w), vmem(comps, lats), vmem(comps, 128), vmem(128, wide),
                vmem(wide, 128), vmem(128, lat_w), vmem(8, comps), vmem(1, comps), vmem(1, comps), mask,
                dmas(lon_dev + 10), dmas(CHUNKS, lon_dev),
            ],
            compiler_params=pltpu.CompilerParams(vmem_limit_bytes=ROOMY),
            name="finish",
        )(
            fold_partner, over.astype(jnp.int32).reshape(1), part, src, own_top, odd_got, even_got, seam, halo, norths,
            places, row(cfl_lon), row(cfl_lat), sea_mask,
        )

    return jax.shard_map(
        on_device, mesh=mesh, in_specs=placed, out_specs=P(None, AXES, None), check_vma=False
    )
```

```python
import functools

import jax
import jax.numpy as jnp
from jax import lax
from jax.experimental import pallas as pl
from jax.experimental.pallas import tpu as pltpu
from jax.sharding import PartitionSpec as P

AXES = ("comp", "geo")
CAP = 256
VMEM = pl.BlockSpec(memory_space=pltpu.VMEM)
SMEM = pl.BlockSpec(memory_space=pltpu.SMEM)
ANY = pl.BlockSpec(memory_space=pl.ANY)
LIMIT = 56 * 1024 * 1024
ROOMY = 24 * 1024 * 1024


CHUNKS = 3


def columns_of(rows, stage):
    stage[...] = jnp.zeros(stage.shape, jnp.float32)
    for i, value in enumerate(rows):
        stage[i : i + 1, : value.shape[1]] = value
    return stage[...].T


def position():
    return lax.axis_index("comp"), lax.axis_index("geo")


def halves(value):
    high = value.astype(jnp.bfloat16)
    return high, (value - high.astype(jnp.float32)).astype(jnp.bfloat16)


def dot(a, b, contract=(1, 0)):
    return lax.dot_general(a, b, (((contract[0],), (contract[1],)), ((), ())), preferred_element_type=jnp.float32)


def start_all(copies):
    for copy in copies:
        copy.start()


def wait_all(copies):
    for copy in copies:
        copy.wait()


def source_terms(x, sea, wind, ice, grow_c, diss_c, rate_c, coup_hi, coup_lo):
    mean = jnp.sum(x, axis=0, keepdims=True) / x.shape[0]
    x_hi, x_lo = halves(x)
    coupled = dot(coup_hi, x_hi) + dot(coup_hi, x_lo) + dot(coup_lo, x_hi)
    net = grow_c * wind - diss_c * (mean / (1.0 + mean)) - rate_c * ice
    return sea * (x * jnp.exp(net) + 0.5 * coupled)


def packing(place, rows):
    at = lax.broadcasted_iota(jnp.int32, (rows, place.shape[1]), 0).astype(jnp.float32)
    return jnp.where(at == place, 1.0, 0.0).astype(jnp.bfloat16)


def edges_kernel(
    x_hbm, coup_hbm, wind_hbm, growth_hbm, dissip_hbm, ice_rate_hbm, cfl_lon_hbm, cfl_lat_hbm, sea_hbm, ice_hbm,
    src, own_top, top_hbm, places_hbm,
    xs, xt, ss, raw_top, stage, cols, top_stage, coupling, wind, growth, dissip, ice_rate, cfl_lon, cfl_lat, sea_ref, ice_ref,
    top, places, x_sems, in_sems, out_sems,
):
    comps, lon_dev, lats = x_hbm.shape
    ends = (0, lon_dev - 1)
    last = pl.ds(lats - 128, 128)
    big = [pltpu.make_async_copy(x_hbm.at[:, j, :], xs.at[i], x_sems.at[i]) for i, j in enumerate(ends)]
    slim = [
        pltpu.make_async_copy(x_hbm.at[:, j, last], xt.at[j - 1], x_sems.at[j + 1]) for j in range(1, lon_dev - 1)
    ]
    small = [
        pltpu.make_async_copy(here, there, in_sems.at[i])
        for i, (here, there) in enumerate((
            (cfl_lon_hbm, cfl_lon), (cfl_lat_hbm, cfl_lat), (growth_hbm, growth), (dissip_hbm, dissip),
            (ice_rate_hbm, ice_rate), (coup_hbm, coupling), (wind_hbm, wind), (sea_hbm, sea_ref), (ice_hbm, ice_ref),
        ))
    ]
    start_all((*small[:5], small[5], *small[6:], *big, *slim))
    outs = iter(out_sems.at[i] for i in range(out_sems.shape[0]))
    done = []

    def send(here, there):
        copy = pltpu.make_async_copy(here, there, next(outs))
        copy.start()
        done.append(copy)

    odd = lax.rem(position()[1], 2)
    wait_all(small[:5])
    cols[...] = columns_of((growth[...], dissip[...], ice_rate[...]), stage)
    grow_c, diss_c, rate_c = (cols[:comps, i : i + 1] for i in range(3))
    speed = cfl_lon[...] * jnp.where(odd == 1, 1.0, -1.0)
    pick = lax.broadcasted_iota(jnp.int32, (16, comps), 0)
    flags = jnp.where(pick == 0, speed, jnp.where(pick == 1, -speed, -cfl_lat[...])) > 0.0
    upto = lax.broadcasted_iota(jnp.int32, (comps, comps), 0) <= lax.broadcasted_iota(jnp.int32, (comps, comps), 1)
    ones = jnp.where(upto, 1.0, 0.0).astype(jnp.bfloat16)
    rank = dot(jnp.where(flags, 1.0, 0.0).astype(jnp.bfloat16), ones)
    place = jnp.where(flags, rank - 1.0, -1.0)
    places[...] = place[:8]
    send(places, places_hbm)

    wait_all(small[5:])
    coup_hi, coup_lo = halves(coupling[...])
    terms = functools.partial(
        source_terms, grow_c=grow_c, diss_c=diss_c, rate_c=rate_c, coup_hi=coup_hi, coup_lo=coup_lo
    )
    lane = lax.broadcasted_iota(jnp.int32, (comps, 128), 1)
    lane8 = lax.broadcasted_iota(jnp.int32, (8, 128), 1)

    def gather_last(tile_of, lane):
        total = jnp.zeros(lane.shape, jnp.float32)
        for j in range(lon_dev):
            total = jnp.where(lane == j, pltpu.roll(tile_of(j), j + 1, 1), total)
        return total

    row_top = lambda ref: gather_last(
        lambda j: jnp.broadcast_to(ref[j : j + 1, lats - 128 :].astype(jnp.float32), (8, 128)), lane8
    )[:1]
    row = lambda ref, j: ref[j : j + 1, :].astype(jnp.float32)
    for i, j in enumerate(ends):
        big[i].wait()
        ss[i] = terms(xs[i], row(sea_ref, j), row(wind, j), row(ice_ref, j))
        send(ss.at[i], src.at[i])
    wait_all(slim)
    raw_top[...] = gather_last(
        lambda j: xs[ends.index(j), :, lats - 128 :] if j in ends else xt[j - 1], lane
    )
    top_stage[:comps, :] = terms(raw_top[...], row_top(sea_ref), row_top(wind), row_top(ice_ref))
    send(top_stage.at[:comps], own_top)
    lat_w = top.shape[1]
    top_hi, top_lo = halves(top_stage[:comps, :])
    top_pack = packing(place[2:3, :], lat_w)
    packed = (dot(top_pack, top_hi) + dot(top_pack, top_lo)).T[:lon_dev]
    sea_top = sea_ref[:, lats - 1 : lats].astype(jnp.float32)
    top[...] = jnp.where(lax.broadcasted_iota(jnp.int32, (lon_dev, lat_w), 1) == lat_w - 1, sea_top, packed)
    for slot in range(top_hbm.shape[0]):
        send(top, top_hbm.at[slot])
    wait_all(done)


def messages_kernel(
    cap, src_hbm, places_hbm, sea_hbm, odd_hbm, even_hbm, ss, places, sea_ref, odd_msg, even_msg, in_sems, out_sems
):
    lats = ss.shape[2]
    odd = lax.rem(position()[1], 2)
    copies = [
        pltpu.make_async_copy(here, there, in_sems.at[i])
        for i, (here, there) in enumerate(((places_hbm, places), (sea_hbm, sea_ref), (src_hbm, ss)))
    ]
    start_all(copies)
    wait_all(copies[:2])
    packs = [packing(places[i : i + 1, :], cap) for i in range(2)]
    sea_w, sea_e = (sea_ref[j : j + 1, :].astype(jnp.float32) for j in (0, sea_ref.shape[0] - 1))
    copies[2].wait()
    done = []
    for i, (msg, msg_hbm) in enumerate(((odd_msg, odd_hbm), (even_msg, even_hbm))):
        end = odd if i == 0 else 1 - odd
        hi, lo = halves(ss[end])
        msg[:cap, :] = dot(packs[i], hi) + dot(packs[i], lo)
        msg[cap : cap + 8, :] = jnp.broadcast_to(jnp.where(end == 1, sea_e, sea_w), (8, lats))
        done.append(pltpu.make_async_copy(msg, msg_hbm, out_sems.at[i]))
        done[-1].start()
    wait_all(done)


def inner_kernel(
    x_hbm, coup_hbm, src_hbm, wind_hbm, growth_hbm, dissip_hbm, ice_rate_hbm, cfl_lon_hbm, cfl_lat_hbm, sea_hbm, ice_hbm,
    out, xs, src, outs, stage, cols, coupling, wind, growth, dissip, ice_rate, cfl_lon, cfl_lat, sea_ref, ice_ref,
    in_sems, out_sems,
):
    comps, lon_dev, lats = x_hbm.shape
    middle = range(1, lon_dev - 1)
    pairs = [
        (cfl_lon_hbm, cfl_lon), (cfl_lat_hbm, cfl_lat), (growth_hbm, growth), (dissip_hbm, dissip),
        (ice_rate_hbm, ice_rate), (coup_hbm, coupling), (wind_hbm, wind), (sea_hbm, sea_ref), (ice_hbm, ice_ref),
        *((x_hbm.at[:, j, :], xs.at[j - 1]) for j in middle),
        (src_hbm.at[0], src.at[0]), (src_hbm.at[1], src.at[lon_dev - 1]),
    ]
    copies = [pltpu.make_async_copy(here, there, in_sems.at[i]) for i, (here, there) in enumerate(pairs)]
    start_all(copies)
    wait_all(copies[:5])
    cols[...] = columns_of((growth[...], dissip[...], ice_rate[...], cfl_lon[...], cfl_lat[...]), stage)
    grow_c, diss_c, rate_c = (cols[:comps, i : i + 1] for i in range(3))
    wait_all(copies[5:])
    coup_hi, coup_lo = halves(coupling[...])
    row = lambda ref, j: ref[j : j + 1, :].astype(jnp.float32)
    for j in middle:
        src[j] = source_terms(
            xs[j - 1], row(sea_ref, j), row(wind, j), row(ice_ref, j), grow_c, diss_c, rate_c, coup_hi, coup_lo
        )
    sea = [row(sea_ref, j) for j in range(lon_dev)]
    step = comps // CHUNKS
    lane = lax.broadcasted_iota(jnp.int32, (step, lats), 1)
    wide = [jnp.broadcast_to(sea[j - 1] * sea[j], (step, lats)) for j in range(1, lon_dev)]
    tall = []
    for j in range(lon_dev):
        own = jnp.broadcast_to(sea[j], (step, lats))
        tall.append(jnp.where(lane == lats - 1, 0.0, own * pltpu.roll(own, lats - 1, 1)))

    def rows(at):
        params = cols[at, :]
        lon_pos = jnp.maximum(params[:, 3:4], 0.0)
        lon_neg = jnp.minimum(params[:, 3:4], 0.0)
        lat_pos = jnp.maximum(params[:, 4:5], 0.0)
        lat_neg = jnp.minimum(params[:, 4:5], 0.0)
        vals = [src[j, at, :] for j in range(lon_dev)]
        flux = [wide[j] * (lon_pos * vals[j] + lon_neg * vals[j + 1]) for j in range(lon_dev - 1)]
        for j in range(lon_dev):
            lat = tall[j] * (lat_pos * vals[j] + lat_neg * pltpu.roll(vals[j], lats - 1, 1))
            value = vals[j] - (lat - pltpu.roll(lat, 1, 1))
            if j > 0:
                value = value + flux[j - 1]
            if j < lon_dev - 1:
                value = value - flux[j]
            outs[j, at, :] = value

    done = []
    for c in range(CHUNKS):
        at = pl.ds(c * step, step)
        rows(at)
        for j in range(lon_dev):
            done.append(pltpu.make_async_copy(outs.at[j, at, :], out.at[at, j, :], out_sems.at[c, j]))
            done[-1].start()
    wait_all(done)


def finish_kernel(
    cap, n_comp, n_geo, fold, over, part, src_hbm, own_top_hbm, odd_hbm, even_hbm, seam_hbm, halo_hbm, norths_hbm, places_hbm,
    cfl_lon_hbm, cfl_lat_hbm, sea_hbm,
    out, src, acc, acc_top, own_top, msgs, seam, halo, norths, stage, cols, top_rows, places, cfl_lon, cfl_lat, sea_ref,
    in_sems, out_sems,
):
    comps, lon_dev, lats = part.shape
    ends = (0, lon_dev - 1)
    middle = range(1, lon_dev - 1)
    last = pl.ds(lats - 128, 128)
    me_comp, me_geo = position()
    odd = lax.rem(me_geo, 2)
    q = fold[0] // lon_dev
    shift = lax.rem(fold[0], lon_dev)

    def slot_of(q):
        source = lax.rem(q - (me_comp * n_geo + me_geo) + 2 * n_comp * n_geo, n_comp * n_geo)
        y, _, x = digits(lax.rem(source, n_geo))
        return y * 4 + x

    slot_0, slot_1 = slot_of(q), slot_of(q - 1)
    pairs = [
        (places_hbm, places), (cfl_lon_hbm, cfl_lon), (cfl_lat_hbm, cfl_lat), (sea_hbm, sea_ref),
        (seam_hbm.at[slot_0], seam.at[0]), (seam_hbm.at[slot_1], seam.at[1]),
        (odd_hbm, msgs.at[0]), (even_hbm, msgs.at[1]),
        (own_top_hbm, own_top), (src_hbm, src),
        *((part.at[:, j, :], acc.at[i]) for i, j in enumerate(ends)),
        *((part.at[:, j, last], acc_top.at[j - 1]) for j in middle),
    ]
    copies = [pltpu.make_async_copy(here, there, in_sems.at[i]) for i, (here, there) in enumerate(pairs)]
    start_all(copies)
    wait_all(copies[:4])
    cols[...] = columns_of((cfl_lon[...], cfl_lat[...], places[1:2, :], places[0:1, :], places[2:3, :]), stage)

    def spread(i, width):
        at = lax.broadcasted_iota(jnp.int32, (comps, width), 1).astype(jnp.float32)
        return jnp.where(at == cols[:comps, 2 + i : 3 + i], 1.0, 0.0).astype(jnp.bfloat16)

    wait_all(copies[4:8])
    total = None
    for i in range(2):
        hi, lo = halves(msgs[i, :cap, :])
        step = spread(i, cap)
        step = dot(step, hi) + dot(step, lo)
        total = step if total is None else total + step
    halo[...] = total
    lat_w = seam.shape[2]
    top_rows[...] = jnp.zeros(top_rows.shape, jnp.float32)
    for j in range(lon_dev):
        place = shift - j
        block = jnp.where(place >= 0, 0, 1)
        row = jnp.where(place >= 0, place, place + lon_dev)
        top_rows[j : j + 1, :] = seam[block, pl.ds(row, 1), :]
    top_hi, top_lo = halves(top_rows[...])
    top_spread = spread(2, lat_w)
    norths[...] = dot(top_spread, top_hi, (1, 1)) + dot(top_spread, top_lo, (1, 1))

    @pl.when(over[0] > 0)
    def _():
        pltpu.sync_copy(halo_hbm, halo)
        pltpu.sync_copy(norths_hbm, norths)

    sea_odd, sea_even = msgs[0, cap : cap + 1, :], msgs[1, cap : cap + 1, :]
    open_west = jnp.where(odd == 1, sea_even, sea_odd) * sea_ref[0:1, :].astype(jnp.float32)
    open_east = jnp.where(odd == 1, sea_odd, sea_even) * sea_ref[lon_dev - 1 : lon_dev, :].astype(jnp.float32)
    rows_of = comps // CHUNKS
    lane_top = lax.broadcasted_iota(jnp.int32, (rows_of, 128), 1)
    open_top = jnp.zeros((rows_of, 128), jnp.float32)
    for j in range(lon_dev):
        both = top_rows[j : j + 1, lat_w - 1 : lat_w] * sea_ref[j : j + 1, lats - 1 : lats].astype(jnp.float32)
        open_top = jnp.where(lane_top == j, both, open_top)
    wide_west = jnp.broadcast_to(open_west, (rows_of, lats))
    wide_east = jnp.broadcast_to(open_east, (rows_of, lats))
    wait_all(copies[8:])

    def rows(at):
        params = cols[at, :]
        lon_pos = jnp.maximum(params[:, 0:1], 0.0)
        lon_neg = jnp.minimum(params[:, 0:1], 0.0)
        lat_pos = jnp.maximum(params[:, 1:2], 0.0)
        lat_neg = jnp.minimum(params[:, 1:2], 0.0)
        edge = halo[at, :]
        flux_top = open_top * (lat_pos * own_top[at, :] + lat_neg * norths[at, :])
        top_of = lambda j: jnp.where(lane_top == 127, pltpu.roll(flux_top, 127 - j, 1), 0.0)
        west = acc[0, at, :] + wide_west * (lon_pos * edge + lon_neg * src[0, at, :])
        east = acc[1, at, :] - wide_east * (lon_pos * src[1, at, :] + lon_neg * edge)
        for i, value in enumerate((west, east)):
            acc[i, at, : lats - 128] = value[:, : lats - 128]
            acc[i, at, lats - 128 :] = value[:, lats - 128 :] - top_of(ends[i])
        for j in middle:
            acc_top[j - 1, at, :] = acc_top[j - 1, at, :] - top_of(j)

    done = []
    for c in range(CHUNKS):
        at = pl.ds(c * rows_of, rows_of)
        rows(at)
        backs = [(acc.at[i, at, :], out.at[at, j, :]) for i, j in enumerate(ends)]
        backs += [(acc_top.at[j - 1, at, :], out.at[at, j, last]) for j in middle]
        for i, (here, there) in enumerate(backs):
            done.append(pltpu.make_async_copy(here, there, out_sems.at[c, i]))
            done[-1].start()
    wait_all(done)


def digits(place):
    return place // 8, lax.rem(place // 4, 2), lax.rem(place, 4)


def reroute_kernel(n_comp, n_geo, fold, got, out, sems):
    me_comp, me_geo = position()
    me_y, me_h, me_x = digits(me_geo)
    n_y = n_geo // 8
    total = n_comp * n_geo
    lon_dev = got.shape[1]
    copies = []
    for i in range(2):
        q = lax.rem(fold[0] // lon_dev - i + total, total)
        q_y, q_h, q_x = digits(lax.rem(q, n_geo))
        to_x = lax.rem(q_x - me_x + 4, 4)
        short = q_h - me_h - (to_x > q_x).astype(jnp.int32)
        to_y = lax.rem(q_y - me_y - (short < 0).astype(jnp.int32) + 2 * n_y, n_y)
        source = lax.rem(q - (me_comp * n_geo + to_y * 8 + me_h * 4 + to_x) + total, total)
        held = source // n_geo * 2 + lax.rem(source // 4, 2)
        copies.append(pltpu.make_async_copy(got.at[held], out.at[to_y * 4 + to_x], sems.at[i]))
    start_all(copies)
    wait_all(copies)


def seam_of(n_comp, n_geo, top, fold_partner):
    n_y = n_geo // 8
    flat = lambda c, y, h, x: c * n_geo + y * 8 + h * 4 + x
    lines = [[flat(c, y, h, x) for c in range(n_comp) for h in range(2)] for y in range(n_y) for x in range(4)]
    planes = [[flat(c, y, h, x) for y in range(n_y) for x in range(4)] for c in range(n_comp) for h in range(2)]
    by_line = lax.all_to_all(top, AXES, 0, 0, tiled=True, axis_index_groups=lines)
    slots = pl.pallas_call(
        functools.partial(reroute_kernel, n_comp, n_geo),
        out_shape=jax.ShapeDtypeStruct((n_y * 4, *top.shape[1:]), jnp.float32),
        in_specs=[SMEM, ANY],
        out_specs=ANY,
        scratch_shapes=[pltpu.SemaphoreType.DMA((2,))],
        compiler_params=pltpu.CompilerParams(vmem_limit_bytes=1024 * 1024),
        name="reroute",
    )(fold_partner, by_line)
    return lax.all_to_all(slots, AXES, 0, 0, tiled=True, axis_index_groups=planes)


def whole_edges(count, lon_dev, cfl_lon, src, own_top, fold_partner):
    forward = [(d, (d + 1) % count) for d in range(count)]
    west = lax.ppermute(src[1], AXES, forward)
    east = lax.ppermute(src[0], AXES, [(b, a) for a, b in forward])
    halo = jnp.where(cfl_lon[:, None] > 0.0, west, east)
    q, shift = fold_partner[0] // lon_dev, fold_partner[0] % lon_dev
    block = lax.ppermute(own_top[:, :lon_dev].T, AXES, [(d, -d % count) for d in range(count)])
    for bit in range((count - 1).bit_length()):
        moved = lax.ppermute(block, AXES, [(d, (d + (1 << bit)) % count) for d in range(count)])
        block = jnp.where((q >> bit) % 2 == 1, moved, block)
    before = lax.ppermute(block, AXES, [((d + 1) % count, d) for d in range(count)])
    window = jnp.concatenate([before, block], axis=0)
    norths = jnp.take(window, lon_dev + shift - jnp.arange(lon_dev), axis=0).T
    return halo, jnp.pad(norths, ((0, 0), (0, 128 - lon_dev)))


def solution(mesh):
    n_comp, n_geo = mesh.shape["comp"], mesh.shape["geo"]
    count = n_comp * n_geo
    lon = P(AXES, None)
    placed = (P(None, AXES, None), lon, P(), P(), P(), P(), P(), P(), lon, lon, P())
    f32 = jnp.float32
    params = pltpu.CompilerParams(vmem_limit_bytes=LIMIT)
    odd_pairs = [(d, (d + 1) % count if d % 2 else (d - 1) % count) for d in range(count)]
    even_pairs = [(d, d - 1 if d % 2 else d + 1) for d in range(count)]

    def on_device(
        spectrum, wind_speed, growth, dissip, ice_rate, coupling, cfl_lon, cfl_lat, sea_mask, ice_mask, fold_partner
    ):
        comps, lon_dev, lats = spectrum.shape
        wide = -(-comps // 128) * 128
        lat_w = CAP
        size = CAP + 8
        row = lambda v: v.reshape(1, comps)
        shaped = lambda *dims: jax.ShapeDtypeStruct(dims, f32)
        vmem = lambda *dims: pltpu.VMEM(dims, f32)
        dmas = lambda *dims: pltpu.SemaphoreType.DMA(dims)
        mask = pltpu.VMEM((lon_dev, lats), jnp.int32)
        rates = (row(growth), row(dissip), row(ice_rate), row(cfl_lon), row(cfl_lat))
        src, own_top, top, places = pl.pallas_call(
            edges_kernel,
            out_shape=(
                shaped(2, comps, lats), shaped(comps, 128), shaped(2 * n_comp, lon_dev, lat_w), shaped(8, comps),
            ),
            in_specs=[ANY] * 10,
            out_specs=(ANY,) * 4,
            scratch_shapes=[
                vmem(2, comps, lats), vmem(lon_dev - 2, comps, 128), vmem(2, comps, lats), vmem(comps, 128),
                vmem(128, wide), vmem(wide, 128), vmem(wide, 128), vmem(comps, comps), vmem(lon_dev, lats),
                *[vmem(1, comps)] * 5, mask, mask, vmem(lon_dev, lat_w), vmem(8, comps),
                dmas(lon_dev), dmas(9), dmas(2 * n_comp + 4),
            ],
            compiler_params=params,
            name="edges",
        )(spectrum, coupling, wind_speed, *rates, sea_mask, ice_mask)
        odd_msg, even_msg = pl.pallas_call(
            functools.partial(messages_kernel, CAP),
            out_shape=(shaped(size, lats), shaped(size, lats)),
            in_specs=[ANY] * 3,
            out_specs=(ANY,) * 2,
            scratch_shapes=[
                vmem(2, comps, lats), vmem(8, comps), mask, vmem(size, lats), vmem(size, lats), dmas(3), dmas(2),
            ],
            compiler_params=params,
            cost_estimate=pl.CostEstimate(flops=500_000_000, bytes_accessed=2_000_000, transcendentals=0),
            name="messages",
        )(src, places, sea_mask)
        odd_got = lax.ppermute(odd_msg, AXES, odd_pairs)
        even_got = lax.ppermute(even_msg, AXES, even_pairs)
        seam = seam_of(n_comp, n_geo, top, fold_partner)
        part = pl.pallas_call(
            inner_kernel,
            out_shape=shaped(comps, lon_dev, lats),
            in_specs=[ANY] * 11,
            out_specs=ANY,
            scratch_shapes=[
                vmem(lon_dev - 2, comps, lats), vmem(lon_dev, comps, lats), vmem(lon_dev, comps, lats),
                vmem(128, wide), vmem(wide, 128), vmem(comps, comps), vmem(lon_dev, lats),
                *[vmem(1, comps)] * 5, mask, mask, dmas(lon_dev + 9), dmas(CHUNKS, lon_dev),
            ],
            compiler_params=params,
            cost_estimate=pl.CostEstimate(flops=2_000_000_000, bytes_accessed=8_000_000, transcendentals=500_000),
            name="inner",
        )(spectrum, coupling, src, wind_speed, *rates, sea_mask, ice_mask)
        signs = jnp.stack([cfl_lon, -cfl_lon, -cfl_lat])
        over = jnp.max(jnp.sum((signs > 0.0).astype(jnp.int32), axis=1)) >= CAP
        halo, norths = lax.cond(
            over,
            functools.partial(whole_edges, count, lon_dev),
            lambda *_: (jnp.zeros((comps, lats), f32), jnp.zeros((comps, 128), f32)),
            cfl_lon, src, own_top, fold_partner,
        )
        return pl.pallas_call(
            functools.partial(finish_kernel, CAP, n_comp, n_geo),
            out_shape=shaped(comps, lon_dev, lats),
            in_specs=[SMEM, SMEM] + [ANY] * 12,
            out_specs=ANY,
            input_output_aliases={2: 0},
            scratch_shapes=[
                vmem(2, comps, lats), vmem(2, comps, lats), vmem(lon_dev - 2, comps, 128), vmem(comps, 128),
                vmem(2, size, lats), vmem(2, lon_dev, lat_w), vmem(comps, lats), vmem(comps, 128), vmem(128, wide),
                vmem(wide, 128), vmem(128, lat_w), vmem(8, comps), vmem(1, comps), vmem(1, comps), mask,
                dmas(lon_dev + 10), dmas(CHUNKS, lon_dev),
            ],
            compiler_params=pltpu.CompilerParams(vmem_limit_bytes=ROOMY),
            name="finish",
        )(
            fold_partner, over.astype(jnp.int32).reshape(1), part, src, own_top, odd_got, even_got, seam, halo, norths,
            places, row(cfl_lon), row(cfl_lat), sea_mask,
        )

    return jax.shard_map(
        on_device, mesh=mesh, in_specs=placed, out_specs=P(None, AXES, None), check_vma=False
    )
```

```python
import functools

import jax
import jax.numpy as jnp
from jax import lax
from jax.experimental import pallas as pl
from jax.experimental.pallas import tpu as pltpu
from jax.sharding import PartitionSpec as P

AXES = ("comp", "geo")
CAP = 256
VMEM = pl.BlockSpec(memory_space=pltpu.VMEM)
SMEM = pl.BlockSpec(memory_space=pltpu.SMEM)
ANY = pl.BlockSpec(memory_space=pl.ANY)
LIMIT = 56 * 1024 * 1024
ROOMY = 24 * 1024 * 1024


CHUNKS = 3


def columns_of(rows, stage):
    stage[...] = jnp.zeros(stage.shape, jnp.float32)
    for i, value in enumerate(rows):
        stage[i : i + 1, : value.shape[1]] = value
    return stage[...].T


def position():
    return lax.axis_index("comp"), lax.axis_index("geo")


def halves(value):
    high = value.astype(jnp.bfloat16)
    return high, (value - high.astype(jnp.float32)).astype(jnp.bfloat16)


def dot(a, b, contract=(1, 0)):
    return lax.dot_general(a, b, (((contract[0],), (contract[1],)), ((), ())), preferred_element_type=jnp.float32)


def start_all(copies):
    for copy in copies:
        copy.start()


def wait_all(copies):
    for copy in copies:
        copy.wait()


def source_terms(x, sea, wind, ice, grow_c, diss_c, rate_c, coup_hi, coup_lo):
    mean = jnp.sum(x, axis=0, keepdims=True) / x.shape[0]
    x_hi, x_lo = halves(x)
    coupled = dot(coup_hi, x_hi) + dot(coup_hi, x_lo) + dot(coup_lo, x_hi)
    net = grow_c * wind - diss_c * (mean / (1.0 + mean)) - rate_c * ice
    return sea * (x * jnp.exp(net) + 0.5 * coupled)


def packing(place, rows):
    at = lax.broadcasted_iota(jnp.int32, (rows, place.shape[1]), 0).astype(jnp.float32)
    return jnp.where(at == place, 1.0, 0.0).astype(jnp.bfloat16)


def edges_kernel(
    x_hbm, coup_hbm, wind_hbm, growth_hbm, dissip_hbm, ice_rate_hbm, cfl_lon_hbm, cfl_lat_hbm, sea_hbm, ice_hbm,
    src, own_top, top_hbm, places_hbm,
    xs, xt, ss, raw_top, stage, cols, top_stage, coupling, wind, growth, dissip, ice_rate, cfl_lon, cfl_lat, sea_ref, ice_ref,
    top, places, x_sems, in_sems, out_sems,
):
    comps, lon_dev, lats = x_hbm.shape
    ends = (0, lon_dev - 1)
    last = pl.ds(lats - 128, 128)
    big = [pltpu.make_async_copy(x_hbm.at[:, j, :], xs.at[i], x_sems.at[i]) for i, j in enumerate(ends)]
    slim = [
        pltpu.make_async_copy(x_hbm.at[:, j, last], xt.at[j - 1], x_sems.at[j + 1]) for j in range(1, lon_dev - 1)
    ]
    small = [
        pltpu.make_async_copy(here, there, in_sems.at[i])
        for i, (here, there) in enumerate((
            (cfl_lon_hbm, cfl_lon), (cfl_lat_hbm, cfl_lat), (growth_hbm, growth), (dissip_hbm, dissip),
            (ice_rate_hbm, ice_rate), (coup_hbm, coupling), (wind_hbm, wind), (sea_hbm, sea_ref), (ice_hbm, ice_ref),
        ))
    ]
    start_all((*small[:5], small[5], *small[6:], *big, *slim))
    outs = iter(out_sems.at[i] for i in range(out_sems.shape[0]))
    done = []

    def send(here, there):
        copy = pltpu.make_async_copy(here, there, next(outs))
        copy.start()
        done.append(copy)

    odd = lax.rem(position()[1], 2)
    wait_all(small[:5])
    cols[...] = columns_of((growth[...], dissip[...], ice_rate[...]), stage)
    grow_c, diss_c, rate_c = (cols[:comps, i : i + 1] for i in range(3))
    speed = cfl_lon[...] * jnp.where(odd == 1, 1.0, -1.0)
    pick = lax.broadcasted_iota(jnp.int32, (16, comps), 0)
    flags = jnp.where(pick == 0, speed, jnp.where(pick == 1, -speed, -cfl_lat[...])) > 0.0
    upto = lax.broadcasted_iota(jnp.int32, (comps, comps), 0) <= lax.broadcasted_iota(jnp.int32, (comps, comps), 1)
    ones = jnp.where(upto, 1.0, 0.0).astype(jnp.bfloat16)
    rank = dot(jnp.where(flags, 1.0, 0.0).astype(jnp.bfloat16), ones)
    place = jnp.where(flags, rank - 1.0, -1.0)
    places[...] = place[:8]
    send(places, places_hbm)

    wait_all(small[5:])
    coup_hi, coup_lo = halves(coupling[...])
    terms = functools.partial(
        source_terms, grow_c=grow_c, diss_c=diss_c, rate_c=rate_c, coup_hi=coup_hi, coup_lo=coup_lo
    )
    lane = lax.broadcasted_iota(jnp.int32, (comps, 128), 1)
    lane8 = lax.broadcasted_iota(jnp.int32, (8, 128), 1)

    def gather_last(tile_of, lane):
        total = jnp.zeros(lane.shape, jnp.float32)
        for j in range(lon_dev):
            total = jnp.where(lane == j, pltpu.roll(tile_of(j), j + 1, 1), total)
        return total

    row_top = lambda ref: gather_last(
        lambda j: jnp.broadcast_to(ref[j : j + 1, lats - 128 :].astype(jnp.float32), (8, 128)), lane8
    )[:1]
    row = lambda ref, j: ref[j : j + 1, :].astype(jnp.float32)
    for i, j in enumerate(ends):
        big[i].wait()
        ss[i] = terms(xs[i], row(sea_ref, j), row(wind, j), row(ice_ref, j))
        send(ss.at[i], src.at[i])
    wait_all(slim)
    raw_top[...] = gather_last(
        lambda j: xs[ends.index(j), :, lats - 128 :] if j in ends else xt[j - 1], lane
    )
    top_stage[:comps, :] = terms(raw_top[...], row_top(sea_ref), row_top(wind), row_top(ice_ref))
    send(top_stage.at[:comps], own_top)
    lat_w = top.shape[1]
    top_hi, top_lo = halves(top_stage[:comps, :])
    top_pack = packing(place[2:3, :], lat_w)
    packed = (dot(top_pack, top_hi) + dot(top_pack, top_lo)).T[:lon_dev]
    sea_top = sea_ref[:, lats - 1 : lats].astype(jnp.float32)
    top[...] = jnp.where(lax.broadcasted_iota(jnp.int32, (lon_dev, lat_w), 1) == lat_w - 1, sea_top, packed)
    for slot in range(top_hbm.shape[0]):
        send(top, top_hbm.at[slot])
    wait_all(done)


def message_kernel(cap, even, src_hbm, places_hbm, sea_hbm, msg_hbm, ss, places, sea_ref, msg, in_sems, out_sem):
    lats = ss.shape[1]
    odd = lax.rem(position()[1], 2)
    end = 1 - odd if even else odd
    copies = [
        pltpu.make_async_copy(here, there, in_sems.at[i])
        for i, (here, there) in enumerate(((places_hbm, places), (sea_hbm, sea_ref), (src_hbm.at[end], ss)))
    ]
    start_all(copies)
    wait_all(copies[:2])
    pack = packing(places[even : even + 1, :], cap)
    sea_w, sea_e = (sea_ref[j : j + 1, :].astype(jnp.float32) for j in (0, sea_ref.shape[0] - 1))
    copies[2].wait()
    hi, lo = halves(ss[...])
    msg[:cap, :] = dot(pack, hi) + dot(pack, lo)
    msg[cap : cap + 8, :] = jnp.broadcast_to(jnp.where(end == 1, sea_e, sea_w), (8, lats))
    out = pltpu.make_async_copy(msg, msg_hbm, out_sem)
    out.start()
    out.wait()


def inner_kernel(
    x_hbm, coup_hbm, src_hbm, wind_hbm, growth_hbm, dissip_hbm, ice_rate_hbm, cfl_lon_hbm, cfl_lat_hbm, sea_hbm, ice_hbm,
    out, xs, src, outs, stage, cols, coupling, wind, growth, dissip, ice_rate, cfl_lon, cfl_lat, sea_ref, ice_ref,
    in_sems, out_sems,
):
    comps, lon_dev, lats = x_hbm.shape
    middle = range(1, lon_dev - 1)
    pairs = [
        (cfl_lon_hbm, cfl_lon), (cfl_lat_hbm, cfl_lat), (growth_hbm, growth), (dissip_hbm, dissip),
        (ice_rate_hbm, ice_rate), (coup_hbm, coupling), (wind_hbm, wind), (sea_hbm, sea_ref), (ice_hbm, ice_ref),
        *((x_hbm.at[:, j, :], xs.at[j - 1]) for j in middle),
        (src_hbm.at[0], src.at[0]), (src_hbm.at[1], src.at[lon_dev - 1]),
    ]
    copies = [pltpu.make_async_copy(here, there, in_sems.at[i]) for i, (here, there) in enumerate(pairs)]
    start_all(copies)
    wait_all(copies[:5])
    cols[...] = columns_of((growth[...], dissip[...], ice_rate[...], cfl_lon[...], cfl_lat[...]), stage)
    grow_c, diss_c, rate_c = (cols[:comps, i : i + 1] for i in range(3))
    wait_all(copies[5:])
    coup_hi, coup_lo = halves(coupling[...])
    row = lambda ref, j: ref[j : j + 1, :].astype(jnp.float32)
    for j in middle:
        src[j] = source_terms(
            xs[j - 1], row(sea_ref, j), row(wind, j), row(ice_ref, j), grow_c, diss_c, rate_c, coup_hi, coup_lo
        )
    sea = [row(sea_ref, j) for j in range(lon_dev)]
    step = comps // CHUNKS
    lane = lax.broadcasted_iota(jnp.int32, (step, lats), 1)
    wide = [jnp.broadcast_to(sea[j - 1] * sea[j], (step, lats)) for j in range(1, lon_dev)]
    tall = []
    for j in range(lon_dev):
        own = jnp.broadcast_to(sea[j], (step, lats))
        tall.append(jnp.where(lane == lats - 1, 0.0, own * pltpu.roll(own, lats - 1, 1)))

    def rows(at):
        params = cols[at, :]
        lon_pos = jnp.maximum(params[:, 3:4], 0.0)
        lon_neg = jnp.minimum(params[:, 3:4], 0.0)
        lat_pos = jnp.maximum(params[:, 4:5], 0.0)
        lat_neg = jnp.minimum(params[:, 4:5], 0.0)
        vals = [src[j, at, :] for j in range(lon_dev)]
        flux = [wide[j] * (lon_pos * vals[j] + lon_neg * vals[j + 1]) for j in range(lon_dev - 1)]
        for j in range(lon_dev):
            lat = tall[j] * (lat_pos * vals[j] + lat_neg * pltpu.roll(vals[j], lats - 1, 1))
            value = vals[j] - (lat - pltpu.roll(lat, 1, 1))
            if j > 0:
                value = value + flux[j - 1]
            if j < lon_dev - 1:
                value = value - flux[j]
            outs[j, at, :] = value

    done = []
    for c in range(CHUNKS):
        at = pl.ds(c * step, step)
        rows(at)
        for j in range(lon_dev):
            done.append(pltpu.make_async_copy(outs.at[j, at, :], out.at[at, j, :], out_sems.at[c, j]))
            done[-1].start()
    wait_all(done)


def finish_kernel(
    cap, n_comp, n_geo, fold, over, part, src_hbm, own_top_hbm, odd_hbm, even_hbm, seam_hbm, halo_hbm, norths_hbm, places_hbm,
    cfl_lon_hbm, cfl_lat_hbm, sea_hbm,
    out, src, acc, acc_top, own_top, msgs, seam, halo, norths, stage, cols, top_rows, places, cfl_lon, cfl_lat, sea_ref,
    in_sems, out_sems,
):
    comps, lon_dev, lats = part.shape
    ends = (0, lon_dev - 1)
    middle = range(1, lon_dev - 1)
    last = pl.ds(lats - 128, 128)
    me_comp, me_geo = position()
    odd = lax.rem(me_geo, 2)
    q = fold[0] // lon_dev
    shift = lax.rem(fold[0], lon_dev)

    def slot_of(q):
        source = lax.rem(q - (me_comp * n_geo + me_geo) + 2 * n_comp * n_geo, n_comp * n_geo)
        y, _, x = digits(lax.rem(source, n_geo))
        return y * 4 + x

    slot_0, slot_1 = slot_of(q), slot_of(q - 1)
    pairs = [
        (places_hbm, places), (cfl_lon_hbm, cfl_lon), (cfl_lat_hbm, cfl_lat), (sea_hbm, sea_ref),
        (seam_hbm.at[slot_0], seam.at[0]), (seam_hbm.at[slot_1], seam.at[1]),
        (odd_hbm, msgs.at[0]), (even_hbm, msgs.at[1]),
        (own_top_hbm, own_top), (src_hbm, src),
        *((part.at[:, j, :], acc.at[i]) for i, j in enumerate(ends)),
        *((part.at[:, j, last], acc_top.at[j - 1]) for j in middle),
    ]
    copies = [pltpu.make_async_copy(here, there, in_sems.at[i]) for i, (here, there) in enumerate(pairs)]
    start_all(copies)
    wait_all(copies[:4])
    cols[...] = columns_of((cfl_lon[...], cfl_lat[...], places[1:2, :], places[0:1, :], places[2:3, :]), stage)

    def spread(i, width):
        at = lax.broadcasted_iota(jnp.int32, (comps, width), 1).astype(jnp.float32)
        return jnp.where(at == cols[:comps, 2 + i : 3 + i], 1.0, 0.0).astype(jnp.bfloat16)

    wait_all(copies[4:8])
    total = None
    for i in range(2):
        hi, lo = halves(msgs[i, :cap, :])
        step = spread(i, cap)
        step = dot(step, hi) + dot(step, lo)
        total = step if total is None else total + step
    halo[...] = total
    lat_w = seam.shape[2]
    top_rows[...] = jnp.zeros(top_rows.shape, jnp.float32)
    for j in range(lon_dev):
        place = shift - j
        block = jnp.where(place >= 0, 0, 1)
        row = jnp.where(place >= 0, place, place + lon_dev)
        top_rows[j : j + 1, :] = seam[block, pl.ds(row, 1), :]
    top_hi, top_lo = halves(top_rows[...])
    top_spread = spread(2, lat_w)
    norths[...] = dot(top_spread, top_hi, (1, 1)) + dot(top_spread, top_lo, (1, 1))

    @pl.when(over[0] > 0)
    def _():
        pltpu.sync_copy(halo_hbm, halo)
        pltpu.sync_copy(norths_hbm, norths)

    sea_odd, sea_even = msgs[0, cap : cap + 1, :], msgs[1, cap : cap + 1, :]
    open_west = jnp.where(odd == 1, sea_even, sea_odd) * sea_ref[0:1, :].astype(jnp.float32)
    open_east = jnp.where(odd == 1, sea_odd, sea_even) * sea_ref[lon_dev - 1 : lon_dev, :].astype(jnp.float32)
    rows_of = comps // CHUNKS
    lane_top = lax.broadcasted_iota(jnp.int32, (rows_of, 128), 1)
    open_top = jnp.zeros((rows_of, 128), jnp.float32)
    for j in range(lon_dev):
        both = top_rows[j : j + 1, lat_w - 1 : lat_w] * sea_ref[j : j + 1, lats - 1 : lats].astype(jnp.float32)
        open_top = jnp.where(lane_top == j, both, open_top)
    wide_west = jnp.broadcast_to(open_west, (rows_of, lats))
    wide_east = jnp.broadcast_to(open_east, (rows_of, lats))
    wait_all(copies[8:])

    def rows(at):
        params = cols[at, :]
        lon_pos = jnp.maximum(params[:, 0:1], 0.0)
        lon_neg = jnp.minimum(params[:, 0:1], 0.0)
        lat_pos = jnp.maximum(params[:, 1:2], 0.0)
        lat_neg = jnp.minimum(params[:, 1:2], 0.0)
        edge = halo[at, :]
        flux_top = open_top * (lat_pos * own_top[at, :] + lat_neg * norths[at, :])
        top_of = lambda j: jnp.where(lane_top == 127, pltpu.roll(flux_top, 127 - j, 1), 0.0)
        west = acc[0, at, :] + wide_west * (lon_pos * edge + lon_neg * src[0, at, :])
        east = acc[1, at, :] - wide_east * (lon_pos * src[1, at, :] + lon_neg * edge)
        for i, value in enumerate((west, east)):
            acc[i, at, : lats - 128] = value[:, : lats - 128]
            acc[i, at, lats - 128 :] = value[:, lats - 128 :] - top_of(ends[i])
        for j in middle:
            acc_top[j - 1, at, :] = acc_top[j - 1, at, :] - top_of(j)

    done = []
    for c in range(CHUNKS):
        at = pl.ds(c * rows_of, rows_of)
        rows(at)
        backs = [(acc.at[i, at, :], out.at[at, j, :]) for i, j in enumerate(ends)]
        backs += [(acc_top.at[j - 1, at, :], out.at[at, j, last]) for j in middle]
        for i, (here, there) in enumerate(backs):
            done.append(pltpu.make_async_copy(here, there, out_sems.at[c, i]))
            done[-1].start()
    wait_all(done)


def digits(place):
    return place // 8, lax.rem(place // 4, 2), lax.rem(place, 4)


def reroute_kernel(n_comp, n_geo, fold, got, out, sems):
    me_comp, me_geo = position()
    me_y, me_h, me_x = digits(me_geo)
    n_y = n_geo // 8
    total = n_comp * n_geo
    lon_dev = got.shape[1]
    copies = []
    for i in range(2):
        q = lax.rem(fold[0] // lon_dev - i + total, total)
        q_y, q_h, q_x = digits(lax.rem(q, n_geo))
        to_x = lax.rem(q_x - me_x + 4, 4)
        short = q_h - me_h - (to_x > q_x).astype(jnp.int32)
        to_y = lax.rem(q_y - me_y - (short < 0).astype(jnp.int32) + 2 * n_y, n_y)
        source = lax.rem(q - (me_comp * n_geo + to_y * 8 + me_h * 4 + to_x) + total, total)
        held = source // n_geo * 2 + lax.rem(source // 4, 2)
        copies.append(pltpu.make_async_copy(got.at[held], out.at[to_y * 4 + to_x], sems.at[i]))
    start_all(copies)
    wait_all(copies)


def seam_of(n_comp, n_geo, top, fold_partner):
    n_y = n_geo // 8
    flat = lambda c, y, h, x: c * n_geo + y * 8 + h * 4 + x
    lines = [[flat(c, y, h, x) for c in range(n_comp) for h in range(2)] for y in range(n_y) for x in range(4)]
    planes = [[flat(c, y, h, x) for y in range(n_y) for x in range(4)] for c in range(n_comp) for h in range(2)]
    by_line = lax.all_to_all(top, AXES, 0, 0, tiled=True, axis_index_groups=lines)
    slots = pl.pallas_call(
        functools.partial(reroute_kernel, n_comp, n_geo),
        out_shape=jax.ShapeDtypeStruct((n_y * 4, *top.shape[1:]), jnp.float32),
        in_specs=[SMEM, ANY],
        out_specs=ANY,
        scratch_shapes=[pltpu.SemaphoreType.DMA((2,))],
        compiler_params=pltpu.CompilerParams(vmem_limit_bytes=1024 * 1024),
        name="reroute",
    )(fold_partner, by_line)
    return lax.all_to_all(slots, AXES, 0, 0, tiled=True, axis_index_groups=planes)


def whole_edges(count, lon_dev, cfl_lon, src, own_top, fold_partner):
    forward = [(d, (d + 1) % count) for d in range(count)]
    west = lax.ppermute(src[1], AXES, forward)
    east = lax.ppermute(src[0], AXES, [(b, a) for a, b in forward])
    halo = jnp.where(cfl_lon[:, None] > 0.0, west, east)
    q, shift = fold_partner[0] // lon_dev, fold_partner[0] % lon_dev
    block = lax.ppermute(own_top[:, :lon_dev].T, AXES, [(d, -d % count) for d in range(count)])
    for bit in range((count - 1).bit_length()):
        moved = lax.ppermute(block, AXES, [(d, (d + (1 << bit)) % count) for d in range(count)])
        block = jnp.where((q >> bit) % 2 == 1, moved, block)
    before = lax.ppermute(block, AXES, [((d + 1) % count, d) for d in range(count)])
    window = jnp.concatenate([before, block], axis=0)
    norths = jnp.take(window, lon_dev + shift - jnp.arange(lon_dev), axis=0).T
    return halo, jnp.pad(norths, ((0, 0), (0, 128 - lon_dev)))


def solution(mesh):
    n_comp, n_geo = mesh.shape["comp"], mesh.shape["geo"]
    count = n_comp * n_geo
    lon = P(AXES, None)
    placed = (P(None, AXES, None), lon, P(), P(), P(), P(), P(), P(), lon, lon, P())
    f32 = jnp.float32
    params = pltpu.CompilerParams(vmem_limit_bytes=LIMIT)
    odd_pairs = [(d, (d + 1) % count if d % 2 else (d - 1) % count) for d in range(count)]
    even_pairs = [(d, d - 1 if d % 2 else d + 1) for d in range(count)]

    def on_device(
        spectrum, wind_speed, growth, dissip, ice_rate, coupling, cfl_lon, cfl_lat, sea_mask, ice_mask, fold_partner
    ):
        comps, lon_dev, lats = spectrum.shape
        wide = -(-comps // 128) * 128
        lat_w = CAP
        size = CAP + 8
        row = lambda v: v.reshape(1, comps)
        shaped = lambda *dims: jax.ShapeDtypeStruct(dims, f32)
        vmem = lambda *dims: pltpu.VMEM(dims, f32)
        dmas = lambda *dims: pltpu.SemaphoreType.DMA(dims)
        mask = pltpu.VMEM((lon_dev, lats), jnp.int32)
        rates = (row(growth), row(dissip), row(ice_rate), row(cfl_lon), row(cfl_lat))
        src, own_top, top, places = pl.pallas_call(
            edges_kernel,
            out_shape=(
                shaped(2, comps, lats), shaped(comps, 128), shaped(2 * n_comp, lon_dev, lat_w), shaped(8, comps),
            ),
            in_specs=[ANY] * 10,
            out_specs=(ANY,) * 4,
            scratch_shapes=[
                vmem(2, comps, lats), vmem(lon_dev - 2, comps, 128), vmem(2, comps, lats), vmem(comps, 128),
                vmem(128, wide), vmem(wide, 128), vmem(wide, 128), vmem(comps, comps), vmem(lon_dev, lats),
                *[vmem(1, comps)] * 5, mask, mask, vmem(lon_dev, lat_w), vmem(8, comps),
                dmas(lon_dev), dmas(9), dmas(2 * n_comp + 4),
            ],
            compiler_params=params,
            name="edges",
        )(spectrum, coupling, wind_speed, *rates, sea_mask, ice_mask)
        odd_msg, even_msg = (
            pl.pallas_call(
                functools.partial(message_kernel, CAP, even),
                out_shape=shaped(size, lats),
                in_specs=[ANY] * 3,
                out_specs=ANY,
                scratch_shapes=[
                    vmem(comps, lats), vmem(8, comps), mask, vmem(size, lats), dmas(3), pltpu.SemaphoreType.DMA,
                ],
                compiler_params=params,
                cost_estimate=pl.CostEstimate(flops=300_000_000, bytes_accessed=1_000_000, transcendentals=0),
                name=name,
            )(src, places, sea_mask)
            for even, name in ((0, "odd_message"), (1, "even_message"))
        )
        odd_got = lax.ppermute(odd_msg, AXES, odd_pairs)
        even_got = lax.ppermute(even_msg, AXES, even_pairs)
        seam = seam_of(n_comp, n_geo, top, fold_partner)
        part = pl.pallas_call(
            inner_kernel,
            out_shape=shaped(comps, lon_dev, lats),
            in_specs=[ANY] * 11,
            out_specs=ANY,
            scratch_shapes=[
                vmem(lon_dev - 2, comps, lats), vmem(lon_dev, comps, lats), vmem(lon_dev, comps, lats),
                vmem(128, wide), vmem(wide, 128), vmem(comps, comps), vmem(lon_dev, lats),
                *[vmem(1, comps)] * 5, mask, mask, dmas(lon_dev + 9), dmas(CHUNKS, lon_dev),
            ],
            compiler_params=params,
            cost_estimate=pl.CostEstimate(flops=2_000_000_000, bytes_accessed=8_000_000, transcendentals=500_000),
            name="inner",
        )(spectrum, coupling, src, wind_speed, *rates, sea_mask, ice_mask)
        signs = jnp.stack([cfl_lon, -cfl_lon, -cfl_lat])
        over = jnp.max(jnp.sum((signs > 0.0).astype(jnp.int32), axis=1)) >= CAP
        halo, norths = lax.cond(
            over,
            functools.partial(whole_edges, count, lon_dev),
            lambda *_: (jnp.zeros((comps, lats), f32), jnp.zeros((comps, 128), f32)),
            cfl_lon, src, own_top, fold_partner,
        )
        return pl.pallas_call(
            functools.partial(finish_kernel, CAP, n_comp, n_geo),
            out_shape=shaped(comps, lon_dev, lats),
            in_specs=[SMEM, SMEM] + [ANY] * 12,
            out_specs=ANY,
            input_output_aliases={2: 0},
            scratch_shapes=[
                vmem(2, comps, lats), vmem(2, comps, lats), vmem(lon_dev - 2, comps, 128), vmem(comps, 128),
                vmem(2, size, lats), vmem(2, lon_dev, lat_w), vmem(comps, lats), vmem(comps, 128), vmem(128, wide),
                vmem(wide, 128), vmem(128, lat_w), vmem(8, comps), vmem(1, comps), vmem(1, comps), mask,
                dmas(lon_dev + 10), dmas(CHUNKS, lon_dev),
            ],
            compiler_params=pltpu.CompilerParams(vmem_limit_bytes=ROOMY),
            name="finish",
        )(
            fold_partner, over.astype(jnp.int32).reshape(1), part, src, own_top, odd_got, even_got, seam, halo, norths,
            places, row(cfl_lon), row(cfl_lat), sea_mask,
        )

    return jax.shard_map(
        on_device, mesh=mesh, in_specs=placed, out_specs=P(None, AXES, None), check_vma=False
    )
```

```python
import functools

import jax
import jax.numpy as jnp
from jax import lax
from jax.experimental import pallas as pl
from jax.experimental.pallas import tpu as pltpu
from jax.sharding import PartitionSpec as P

AXES = ("comp", "geo")
CAP = 256
VMEM = pl.BlockSpec(memory_space=pltpu.VMEM)
SMEM = pl.BlockSpec(memory_space=pltpu.SMEM)
ANY = pl.BlockSpec(memory_space=pl.ANY)
LIMIT = 56 * 1024 * 1024
ROOMY = 24 * 1024 * 1024


CHUNKS = 3


def columns_of(rows, stage):
    stage[...] = jnp.zeros(stage.shape, jnp.float32)
    for i, value in enumerate(rows):
        stage[i : i + 1, : value.shape[1]] = value
    return stage[...].T


def position():
    return lax.axis_index("comp"), lax.axis_index("geo")


def halves(value):
    high = value.astype(jnp.bfloat16)
    return high, (value - high.astype(jnp.float32)).astype(jnp.bfloat16)


def dot(a, b, contract=(1, 0)):
    return lax.dot_general(a, b, (((contract[0],), (contract[1],)), ((), ())), preferred_element_type=jnp.float32)


def start_all(copies):
    for copy in copies:
        copy.start()


def wait_all(copies):
    for copy in copies:
        copy.wait()


def source_terms(x, sea, wind, ice, grow_c, diss_c, rate_c, coup_hi, coup_lo):
    mean = jnp.sum(x, axis=0, keepdims=True) / x.shape[0]
    x_hi, x_lo = halves(x)
    coupled = dot(coup_hi, x_hi) + dot(coup_hi, x_lo) + dot(coup_lo, x_hi)
    net = grow_c * wind - diss_c * (mean / (1.0 + mean)) - rate_c * ice
    return sea * (x * jnp.exp(net) + 0.5 * coupled)


def packing(place, rows):
    at = lax.broadcasted_iota(jnp.int32, (rows, place.shape[1]), 0).astype(jnp.float32)
    return jnp.where(at == place, 1.0, 0.0).astype(jnp.bfloat16)


def edges_kernel(
    x_hbm, coup_hbm, wind_hbm, growth_hbm, dissip_hbm, ice_rate_hbm, cfl_lon_hbm, cfl_lat_hbm, sea_hbm, ice_hbm,
    src, own_top, top_hbm, places_hbm,
    xs, xt, ss, raw_top, stage, cols, top_stage, coupling, wind, growth, dissip, ice_rate, cfl_lon, cfl_lat, sea_ref, ice_ref,
    top, places, x_sems, in_sems, out_sems,
):
    comps, lon_dev, lats = x_hbm.shape
    ends = (0, lon_dev - 1)
    last = pl.ds(lats - 128, 128)
    big = [pltpu.make_async_copy(x_hbm.at[:, j, :], xs.at[i], x_sems.at[i]) for i, j in enumerate(ends)]
    slim = [
        pltpu.make_async_copy(x_hbm.at[:, j, last], xt.at[j - 1], x_sems.at[j + 1]) for j in range(1, lon_dev - 1)
    ]
    small = [
        pltpu.make_async_copy(here, there, in_sems.at[i])
        for i, (here, there) in enumerate((
            (cfl_lon_hbm, cfl_lon), (cfl_lat_hbm, cfl_lat), (growth_hbm, growth), (dissip_hbm, dissip),
            (ice_rate_hbm, ice_rate), (coup_hbm, coupling), (wind_hbm, wind), (sea_hbm, sea_ref), (ice_hbm, ice_ref),
        ))
    ]
    start_all((*small[:5], small[5], *small[6:], *big, *slim))
    outs = iter(out_sems.at[i] for i in range(out_sems.shape[0]))
    done = []

    def send(here, there):
        copy = pltpu.make_async_copy(here, there, next(outs))
        copy.start()
        done.append(copy)

    odd = lax.rem(position()[1], 2)
    wait_all(small[:5])
    cols[...] = columns_of((growth[...], dissip[...], ice_rate[...]), stage)
    grow_c, diss_c, rate_c = (cols[:comps, i : i + 1] for i in range(3))
    speed = cfl_lon[...] * jnp.where(odd == 1, 1.0, -1.0)
    pick = lax.broadcasted_iota(jnp.int32, (16, comps), 0)
    flags = jnp.where(pick == 0, speed, jnp.where(pick == 1, -speed, -cfl_lat[...])) > 0.0
    upto = lax.broadcasted_iota(jnp.int32, (comps, comps), 0) <= lax.broadcasted_iota(jnp.int32, (comps, comps), 1)
    ones = jnp.where(upto, 1.0, 0.0).astype(jnp.bfloat16)
    rank = dot(jnp.where(flags, 1.0, 0.0).astype(jnp.bfloat16), ones)
    place = jnp.where(flags, rank - 1.0, -1.0)
    places[...] = place[:8]
    send(places, places_hbm)

    wait_all(small[5:])
    coup_hi, coup_lo = halves(coupling[...])
    terms = functools.partial(
        source_terms, grow_c=grow_c, diss_c=diss_c, rate_c=rate_c, coup_hi=coup_hi, coup_lo=coup_lo
    )
    lane = lax.broadcasted_iota(jnp.int32, (comps, 128), 1)
    lane8 = lax.broadcasted_iota(jnp.int32, (8, 128), 1)

    def gather_last(tile_of, lane):
        total = jnp.zeros(lane.shape, jnp.float32)
        for j in range(lon_dev):
            total = jnp.where(lane == j, pltpu.roll(tile_of(j), j + 1, 1), total)
        return total

    row_top = lambda ref: gather_last(
        lambda j: jnp.broadcast_to(ref[j : j + 1, lats - 128 :].astype(jnp.float32), (8, 128)), lane8
    )[:1]
    row = lambda ref, j: ref[j : j + 1, :].astype(jnp.float32)
    for i, j in enumerate(ends):
        big[i].wait()
        ss[i] = terms(xs[i], row(sea_ref, j), row(wind, j), row(ice_ref, j))
        send(ss.at[i], src.at[i])
    wait_all(slim)
    raw_top[...] = gather_last(
        lambda j: xs[ends.index(j), :, lats - 128 :] if j in ends else xt[j - 1], lane
    )
    top_stage[:comps, :] = terms(raw_top[...], row_top(sea_ref), row_top(wind), row_top(ice_ref))
    send(top_stage.at[:comps], own_top)
    lat_w = top.shape[1]
    top_hi, top_lo = halves(top_stage[:comps, :])
    top_pack = packing(place[2:3, :], lat_w)
    packed = (dot(top_pack, top_hi) + dot(top_pack, top_lo)).T[:lon_dev]
    sea_top = sea_ref[:, lats - 1 : lats].astype(jnp.float32)
    top[...] = jnp.where(lax.broadcasted_iota(jnp.int32, (lon_dev, lat_w), 1) == lat_w - 1, sea_top, packed)
    for slot in range(top_hbm.shape[0]):
        send(top, top_hbm.at[slot])
    wait_all(done)


def messages_kernel(
    cap, src_hbm, places_hbm, sea_hbm, odd_hbm, even_hbm, ss, places, sea_ref, odd_msg, even_msg, in_sems, out_sems
):
    lats = ss.shape[2]
    odd = lax.rem(position()[1], 2)
    copies = [
        pltpu.make_async_copy(here, there, in_sems.at[i])
        for i, (here, there) in enumerate(((places_hbm, places), (sea_hbm, sea_ref), (src_hbm, ss)))
    ]
    start_all(copies)
    wait_all(copies[:2])
    packs = [packing(places[i : i + 1, :], cap) for i in range(2)]
    sea_w, sea_e = (sea_ref[j : j + 1, :].astype(jnp.float32) for j in (0, sea_ref.shape[0] - 1))
    copies[2].wait()
    done = []
    for i, (msg, msg_hbm) in enumerate(((odd_msg, odd_hbm), (even_msg, even_hbm))):
        end = odd if i == 0 else 1 - odd
        hi, lo = halves(ss[end])
        msg[:cap, :] = dot(packs[i], hi) + dot(packs[i], lo)
        msg[cap : cap + 8, :] = jnp.broadcast_to(jnp.where(end == 1, sea_e, sea_w), (8, lats))
        done.append(pltpu.make_async_copy(msg, msg_hbm, out_sems.at[i]))
        done[-1].start()
    wait_all(done)


def inner_kernel(
    x_hbm, coup_hbm, src_hbm, wind_hbm, growth_hbm, dissip_hbm, ice_rate_hbm, cfl_lon_hbm, cfl_lat_hbm, sea_hbm, ice_hbm,
    out, xs, src, outs, stage, cols, coupling, wind, growth, dissip, ice_rate, cfl_lon, cfl_lat, sea_ref, ice_ref,
    in_sems, out_sems,
):
    comps, lon_dev, lats = x_hbm.shape
    middle = range(1, lon_dev - 1)
    pairs = [
        (cfl_lon_hbm, cfl_lon), (cfl_lat_hbm, cfl_lat), (growth_hbm, growth), (dissip_hbm, dissip),
        (ice_rate_hbm, ice_rate), (coup_hbm, coupling), (wind_hbm, wind), (sea_hbm, sea_ref), (ice_hbm, ice_ref),
        *((x_hbm.at[:, j, :], xs.at[j - 1]) for j in middle),
        (src_hbm.at[0], src.at[0]), (src_hbm.at[1], src.at[lon_dev - 1]),
    ]
    copies = [pltpu.make_async_copy(here, there, in_sems.at[i]) for i, (here, there) in enumerate(pairs)]
    start_all(copies)
    wait_all(copies[:5])
    cols[...] = columns_of((growth[...], dissip[...], ice_rate[...], cfl_lon[...], cfl_lat[...]), stage)
    grow_c, diss_c, rate_c = (cols[:comps, i : i + 1] for i in range(3))
    wait_all(copies[5:])
    coup_hi, coup_lo = halves(coupling[...])
    row = lambda ref, j: ref[j : j + 1, :].astype(jnp.float32)
    for j in middle:
        src[j] = source_terms(
            xs[j - 1], row(sea_ref, j), row(wind, j), row(ice_ref, j), grow_c, diss_c, rate_c, coup_hi, coup_lo
        )
    sea = [row(sea_ref, j) for j in range(lon_dev)]
    step = comps // CHUNKS
    lane = lax.broadcasted_iota(jnp.int32, (step, lats), 1)
    wide = [jnp.broadcast_to(sea[j - 1] * sea[j], (step, lats)) for j in range(1, lon_dev)]
    tall = []
    for j in range(lon_dev):
        own = jnp.broadcast_to(sea[j], (step, lats))
        tall.append(jnp.where(lane == lats - 1, 0.0, own * pltpu.roll(own, lats - 1, 1)))

    def rows(at):
        params = cols[at, :]
        lon_pos = jnp.maximum(params[:, 3:4], 0.0)
        lon_neg = jnp.minimum(params[:, 3:4], 0.0)
        lat_pos = jnp.maximum(params[:, 4:5], 0.0)
        lat_neg = jnp.minimum(params[:, 4:5], 0.0)
        vals = [src[j, at, :] for j in range(lon_dev)]
        flux = [wide[j] * (lon_pos * vals[j] + lon_neg * vals[j + 1]) for j in range(lon_dev - 1)]
        for j in range(lon_dev):
            lat = tall[j] * (lat_pos * vals[j] + lat_neg * pltpu.roll(vals[j], lats - 1, 1))
            value = vals[j] - (lat - pltpu.roll(lat, 1, 1))
            if j > 0:
                value = value + flux[j - 1]
            if j < lon_dev - 1:
                value = value - flux[j]
            outs[j, at, :] = value

    done = []
    for c in range(CHUNKS):
        at = pl.ds(c * step, step)
        rows(at)
        for j in range(lon_dev):
            done.append(pltpu.make_async_copy(outs.at[j, at, :], out.at[at, j, :], out_sems.at[c, j]))
            done[-1].start()
    wait_all(done)


def finish_kernel(
    cap, n_comp, n_geo, fold, over, part, src_hbm, own_top_hbm, odd_hbm, even_hbm, seam_hbm, halo_hbm, norths_hbm, places_hbm,
    cfl_lon_hbm, cfl_lat_hbm, sea_hbm,
    out, src, acc, acc_top, own_top, msgs, seam, halo, norths, stage, cols, top_rows, places, cfl_lon, cfl_lat, sea_ref,
    in_sems, out_sems,
):
    comps, lon_dev, lats = part.shape
    ends = (0, lon_dev - 1)
    middle = range(1, lon_dev - 1)
    last = pl.ds(lats - 128, 128)
    me_comp, me_geo = position()
    odd = lax.rem(me_geo, 2)
    q = fold[0] // lon_dev
    shift = lax.rem(fold[0], lon_dev)

    def slot_of(q):
        source = lax.rem(q - (me_comp * n_geo + me_geo) + 2 * n_comp * n_geo, n_comp * n_geo)
        y, _, x = digits(lax.rem(source, n_geo))
        return y * 4 + x

    slot_0, slot_1 = slot_of(q), slot_of(q - 1)
    pairs = [
        (places_hbm, places), (cfl_lon_hbm, cfl_lon), (cfl_lat_hbm, cfl_lat), (sea_hbm, sea_ref),
        (seam_hbm.at[slot_0], seam.at[0]), (seam_hbm.at[slot_1], seam.at[1]),
        (odd_hbm, msgs.at[0]), (even_hbm, msgs.at[1]),
        (own_top_hbm, own_top), (src_hbm, src),
        *((part.at[:, j, :], acc.at[i]) for i, j in enumerate(ends)),
        *((part.at[:, j, last], acc_top.at[j - 1]) for j in middle),
    ]
    copies = [pltpu.make_async_copy(here, there, in_sems.at[i]) for i, (here, there) in enumerate(pairs)]
    start_all(copies)
    wait_all(copies[:4])
    cols[...] = columns_of((cfl_lon[...], cfl_lat[...], places[1:2, :], places[0:1, :], places[2:3, :]), stage)

    def spread(i, width):
        at = lax.broadcasted_iota(jnp.int32, (comps, width), 1).astype(jnp.float32)
        return jnp.where(at == cols[:comps, 2 + i : 3 + i], 1.0, 0.0).astype(jnp.bfloat16)

    wait_all(copies[4:8])
    total = None
    for i in range(2):
        hi, lo = halves(msgs[i, :cap, :])
        step = spread(i, cap)
        step = dot(step, hi) + dot(step, lo)
        total = step if total is None else total + step
    halo[...] = total
    lat_w = seam.shape[2]
    top_rows[...] = jnp.zeros(top_rows.shape, jnp.float32)
    for j in range(lon_dev):
        place = shift - j
        block = jnp.where(place >= 0, 0, 1)
        row = jnp.where(place >= 0, place, place + lon_dev)
        top_rows[j : j + 1, :] = seam[block, pl.ds(row, 1), :]
    top_hi, top_lo = halves(top_rows[...])
    top_spread = spread(2, lat_w)
    norths[...] = dot(top_spread, top_hi, (1, 1)) + dot(top_spread, top_lo, (1, 1))

    @pl.when(over[0] > 0)
    def _():
        pltpu.sync_copy(halo_hbm, halo)
        pltpu.sync_copy(norths_hbm, norths)

    sea_odd, sea_even = msgs[0, cap : cap + 1, :], msgs[1, cap : cap + 1, :]
    open_west = jnp.where(odd == 1, sea_even, sea_odd) * sea_ref[0:1, :].astype(jnp.float32)
    open_east = jnp.where(odd == 1, sea_odd, sea_even) * sea_ref[lon_dev - 1 : lon_dev, :].astype(jnp.float32)
    rows_of = comps // CHUNKS
    lane_top = lax.broadcasted_iota(jnp.int32, (rows_of, 128), 1)
    open_top = jnp.zeros((rows_of, 128), jnp.float32)
    for j in range(lon_dev):
        both = top_rows[j : j + 1, lat_w - 1 : lat_w] * sea_ref[j : j + 1, lats - 1 : lats].astype(jnp.float32)
        open_top = jnp.where(lane_top == j, both, open_top)
    wide_west = jnp.broadcast_to(open_west, (rows_of, lats))
    wide_east = jnp.broadcast_to(open_east, (rows_of, lats))
    wait_all(copies[8:])

    def rows(at):
        params = cols[at, :]
        lon_pos = jnp.maximum(params[:, 0:1], 0.0)
        lon_neg = jnp.minimum(params[:, 0:1], 0.0)
        lat_pos = jnp.maximum(params[:, 1:2], 0.0)
        lat_neg = jnp.minimum(params[:, 1:2], 0.0)
        edge = halo[at, :]
        flux_top = open_top * (lat_pos * own_top[at, :] + lat_neg * norths[at, :])
        top_of = lambda j: jnp.where(lane_top == 127, pltpu.roll(flux_top, 127 - j, 1), 0.0)
        west = acc[0, at, :] + wide_west * (lon_pos * edge + lon_neg * src[0, at, :])
        east = acc[1, at, :] - wide_east * (lon_pos * src[1, at, :] + lon_neg * edge)
        for i, value in enumerate((west, east)):
            acc[i, at, : lats - 128] = value[:, : lats - 128]
            acc[i, at, lats - 128 :] = value[:, lats - 128 :] - top_of(ends[i])
        for j in middle:
            acc_top[j - 1, at, :] = acc_top[j - 1, at, :] - top_of(j)

    done = []
    for c in range(CHUNKS):
        at = pl.ds(c * rows_of, rows_of)
        rows(at)
        backs = [(acc.at[i, at, :], out.at[at, j, :]) for i, j in enumerate(ends)]
        backs += [(acc_top.at[j - 1, at, :], out.at[at, j, last]) for j in middle]
        for i, (here, there) in enumerate(backs):
            done.append(pltpu.make_async_copy(here, there, out_sems.at[c, i]))
            done[-1].start()
    wait_all(done)


def digits(place):
    return place // 8, lax.rem(place // 4, 2), lax.rem(place, 4)


def reroute_kernel(n_comp, n_geo, fold, got, out, sems):
    me_comp, me_geo = position()
    me_y, me_h, me_x = digits(me_geo)
    n_y = n_geo // 8
    total = n_comp * n_geo
    lon_dev = got.shape[1]
    copies = []
    for i in range(2):
        q = lax.rem(fold[0] // lon_dev - i + total, total)
        q_y, q_h, q_x = digits(lax.rem(q, n_geo))
        to_x = lax.rem(q_x - me_x + 4, 4)
        short = q_h - me_h - (to_x > q_x).astype(jnp.int32)
        to_y = lax.rem(q_y - me_y - (short < 0).astype(jnp.int32) + 2 * n_y, n_y)
        source = lax.rem(q - (me_comp * n_geo + to_y * 8 + me_h * 4 + to_x) + total, total)
        held = source // n_geo * 2 + lax.rem(source // 4, 2)
        copies.append(pltpu.make_async_copy(got.at[held], out.at[to_y * 4 + to_x], sems.at[i]))
    start_all(copies)
    wait_all(copies)


def seam_of(n_comp, n_geo, top, fold_partner):
    n_y = n_geo // 8
    flat = lambda c, y, h, x: c * n_geo + y * 8 + h * 4 + x
    lines = [[flat(c, y, h, x) for c in range(n_comp) for h in range(2)] for y in range(n_y) for x in range(4)]
    planes = [[flat(c, y, h, x) for y in range(n_y) for x in range(4)] for c in range(n_comp) for h in range(2)]
    by_line = lax.all_to_all(top, AXES, 0, 0, tiled=True, axis_index_groups=lines)
    slots = pl.pallas_call(
        functools.partial(reroute_kernel, n_comp, n_geo),
        out_shape=jax.ShapeDtypeStruct((n_y * 4, *top.shape[1:]), jnp.float32),
        in_specs=[SMEM, ANY],
        out_specs=ANY,
        scratch_shapes=[pltpu.SemaphoreType.DMA((2,))],
        compiler_params=pltpu.CompilerParams(vmem_limit_bytes=1024 * 1024),
        name="reroute",
    )(fold_partner, by_line)
    return lax.all_to_all(slots, AXES, 0, 0, tiled=True, axis_index_groups=planes)


def whole_edges(count, lon_dev, cfl_lon, src, own_top, fold_partner):
    forward = [(d, (d + 1) % count) for d in range(count)]
    west = lax.ppermute(src[1], AXES, forward)
    east = lax.ppermute(src[0], AXES, [(b, a) for a, b in forward])
    halo = jnp.where(cfl_lon[:, None] > 0.0, west, east)
    q, shift = fold_partner[0] // lon_dev, fold_partner[0] % lon_dev
    block = lax.ppermute(own_top[:, :lon_dev].T, AXES, [(d, -d % count) for d in range(count)])
    for bit in range((count - 1).bit_length()):
        moved = lax.ppermute(block, AXES, [(d, (d + (1 << bit)) % count) for d in range(count)])
        block = jnp.where((q >> bit) % 2 == 1, moved, block)
    before = lax.ppermute(block, AXES, [((d + 1) % count, d) for d in range(count)])
    window = jnp.concatenate([before, block], axis=0)
    norths = jnp.take(window, lon_dev + shift - jnp.arange(lon_dev), axis=0).T
    return halo, jnp.pad(norths, ((0, 0), (0, 128 - lon_dev)))


def solution(mesh):
    n_comp, n_geo = mesh.shape["comp"], mesh.shape["geo"]
    count = n_comp * n_geo
    lon = P(AXES, None)
    placed = (P(None, AXES, None), lon, P(), P(), P(), P(), P(), P(), lon, lon, P())
    f32 = jnp.float32
    params = pltpu.CompilerParams(vmem_limit_bytes=LIMIT)
    odd_pairs = [(d, (d + 1) % count if d % 2 else (d - 1) % count) for d in range(count)]
    even_pairs = [(d, d - 1 if d % 2 else d + 1) for d in range(count)]

    def on_device(
        spectrum, wind_speed, growth, dissip, ice_rate, coupling, cfl_lon, cfl_lat, sea_mask, ice_mask, fold_partner
    ):
        comps, lon_dev, lats = spectrum.shape
        wide = -(-comps // 128) * 128
        lat_w = CAP
        size = CAP + 8
        row = lambda v: v.reshape(1, comps)
        shaped = lambda *dims: jax.ShapeDtypeStruct(dims, f32)
        vmem = lambda *dims: pltpu.VMEM(dims, f32)
        dmas = lambda *dims: pltpu.SemaphoreType.DMA(dims)
        mask = pltpu.VMEM((lon_dev, lats), jnp.int32)
        rates = (row(growth), row(dissip), row(ice_rate), row(cfl_lon), row(cfl_lat))
        src, own_top, top, places = pl.pallas_call(
            edges_kernel,
            out_shape=(
                shaped(2, comps, lats), shaped(comps, 128), shaped(2 * n_comp, lon_dev, lat_w), shaped(8, comps),
            ),
            in_specs=[ANY] * 10,
            out_specs=(ANY,) * 4,
            scratch_shapes=[
                vmem(2, comps, lats), vmem(lon_dev - 2, comps, 128), vmem(2, comps, lats), vmem(comps, 128),
                vmem(128, wide), vmem(wide, 128), vmem(wide, 128), vmem(comps, comps), vmem(lon_dev, lats),
                *[vmem(1, comps)] * 5, mask, mask, vmem(lon_dev, lat_w), vmem(8, comps),
                dmas(lon_dev), dmas(9), dmas(2 * n_comp + 4),
            ],
            compiler_params=params,
            name="edges",
        )(spectrum, coupling, wind_speed, *rates, sea_mask, ice_mask)
        odd_msg, even_msg = pl.pallas_call(
            functools.partial(messages_kernel, CAP),
            out_shape=(shaped(size, lats), shaped(size, lats)),
            in_specs=[ANY] * 3,
            out_specs=(ANY,) * 2,
            scratch_shapes=[
                vmem(2, comps, lats), vmem(8, comps), mask, vmem(size, lats), vmem(size, lats), dmas(3), dmas(2),
            ],
            compiler_params=params,
            cost_estimate=pl.CostEstimate(flops=500_000_000, bytes_accessed=2_000_000, transcendentals=0),
            name="messages",
        )(src, places, sea_mask)
        odd_got = lax.ppermute(odd_msg, AXES, odd_pairs)
        even_got = lax.ppermute(even_msg, AXES, even_pairs)
        seam = seam_of(n_comp, n_geo, top, fold_partner)
        part = pl.pallas_call(
            inner_kernel,
            out_shape=shaped(comps, lon_dev, lats),
            in_specs=[ANY] * 11,
            out_specs=ANY,
            scratch_shapes=[
                vmem(lon_dev - 2, comps, lats), vmem(lon_dev, comps, lats), vmem(lon_dev, comps, lats),
                vmem(128, wide), vmem(wide, 128), vmem(comps, comps), vmem(lon_dev, lats),
                *[vmem(1, comps)] * 5, mask, mask, dmas(lon_dev + 9), dmas(CHUNKS, lon_dev),
            ],
            compiler_params=params,
            cost_estimate=pl.CostEstimate(flops=2_000_000_000, bytes_accessed=8_000_000, transcendentals=500_000),
            name="inner",
        )(spectrum, coupling, src, wind_speed, *rates, sea_mask, ice_mask)
        over = jnp.max(places) >= CAP - 1
        halo, norths = lax.cond(
            over,
            functools.partial(whole_edges, count, lon_dev),
            lambda *_: (jnp.zeros((comps, lats), f32), jnp.zeros((comps, 128), f32)),
            cfl_lon, src, own_top, fold_partner,
        )
        return pl.pallas_call(
            functools.partial(finish_kernel, CAP, n_comp, n_geo),
            out_shape=shaped(comps, lon_dev, lats),
            in_specs=[SMEM, SMEM] + [ANY] * 12,
            out_specs=ANY,
            input_output_aliases={2: 0},
            scratch_shapes=[
                vmem(2, comps, lats), vmem(2, comps, lats), vmem(lon_dev - 2, comps, 128), vmem(comps, 128),
                vmem(2, size, lats), vmem(2, lon_dev, lat_w), vmem(comps, lats), vmem(comps, 128), vmem(128, wide),
                vmem(wide, 128), vmem(128, lat_w), vmem(8, comps), vmem(1, comps), vmem(1, comps), mask,
                dmas(lon_dev + 10), dmas(CHUNKS, lon_dev),
            ],
            compiler_params=pltpu.CompilerParams(vmem_limit_bytes=ROOMY),
            name="finish",
        )(
            fold_partner, over.astype(jnp.int32).reshape(1), part, src, own_top, odd_got, even_got, seam, halo, norths,
            places, row(cfl_lon), row(cfl_lat), sea_mask,
        )

    return jax.shard_map(
        on_device, mesh=mesh, in_specs=placed, out_specs=P(None, AXES, None), check_vma=False
    )
```
